32 devices in a mesh: dp: 16 (over z, y, core), tensor: 2 (over x).
Axes of the slice: x: 2, y: 2, z: 4, core: 2. Of those that a mesh axis runs over, the one named last changes fastest.
Arguments:
- patches: float32 [15104, 768], P('dp'), may hold values from -6 to 6
- segment_ids: int32 [16, 944], P('dp'), may hold values from 0 to 18, never falling along the last dimension, each value on 1 to 50 neighbouring positions
- proprio: float32 [304, 9], P('dp'), may hold values from -6 to 6
- ln1_gain: float32 [768], replicated, may hold values from 0.5 to 1.5
- ln1_bias: float32 [768], replicated, may hold values from -2 to 2
- qkv_weight: float32 [768, 3, 768], P(None, None, 'tensor'), may hold values from -0.21875 to 0.21875
- qv_bias: float32 [2, 768], P(None, 'tensor'), may hold values from -2 to 2
- out_weight: float32 [768, 768], P('tensor'), may hold values from -1.5 to 1.5
- out_bias: float32 [768], replicated, may hold values from -2 to 2
- ln2_gain: float32 [768], replicated, may hold values from 0.5 to 1.5
- ln2_bias: float32 [768], replicated, may hold values from -2 to 2
- fc1_weight: float32 [768, 3072], P(None, 'tensor'), may hold values from -0.21875 to 0.21875
- fc1_bias: float32 [3072], P('tensor'), may hold values from -2 to 2
- fc2_weight: float32 [3072, 768], P('tensor'), may hold values from -0.109375 to 0.109375
- fc2_bias: float32 [768], replicated, may hold values from -2 to 2
- pol_image: float32 [768, 256], replicated, may hold values from -0.21875 to 0.21875
- pol_proprio: float32 [9, 256], replicated, may hold values from -2 to 2
- pol_hidden: float32 [256, 128], replicated, may hold values from -0.375 to 0.375
- pol_third: float32 [128, 64], replicated, may hold values from -0.5 to 0.5
- pol_action: float32 [64, 8], replicated, may hold values from -0.75 to 0.75
- out_cotangent: float32 [15104, 768], P('dp'), may hold values from -6 to 6
- action_cotangent: float32 [304, 8], P('dp'), may hold values from -6 to 6
Outputs:
- encoded: float32 [15104, 768], P('dp')
- actions: float32 [304, 8], P('dp')
- patches_grad: float32 [15104, 768], P('dp')
- ln1_gain_grad: float32 [768], replicated
- ln1_bias_grad: float32 [768], replicated
- qkv_weight_grad: float32 [768, 3, 768], P('dp', None, 'tensor')
- qv_bias_grad: float32 [2, 768], P(None, 'tensor')
- out_weight_grad: float32 [768, 768], P('tensor', 'dp')
- out_bias_grad: float32 [768], replicated
- ln2_gain_grad: float32 [768], replicated
- ln2_bias_grad: float32 [768], replicated
- fc1_weight_grad: float32 [768, 3072], P('dp', 'tensor')
- fc1_bias_grad: float32 [3072], P('tensor')
- fc2_weight_grad: float32 [3072, 768], P('tensor', 'dp')
- fc2_bias_grad: float32 [768], replicated
- pol_image_grad: float32 [768, 256], replicated
- pol_proprio_grad: float32 [9, 256], replicated
- pol_hidden_grad: float32 [256, 128], replicated
- pol_third_grad: float32 [128, 64], replicated
- pol_action_grad: float32 [64, 8], replicated
The draws below stay inside these ranges and needn't reach their ends.
Inputs may be any that keep to these rules, and one draw needn't show every extreme that they name: `segment_ids`: in each packed row the image numbers never fall, every number from 0 to 18 appears, each image has 1 to 50 tokens and some image of the row has exactly 50.
All inputs are finite; a program needn't handle non-finite values.
Results may differ from the reference program's by a relative error of at most 0.0003.
Values sent between devices are 32-bit elements; how exact they have to be, the bound alone decides.
No kernel may reach another device: no remote copies, remote signals or barrier semaphores. Data moves between devices by JAX's collectives and lax.ppermute only.
A program may use at most 192 MiB of HBM per device.

```python
import math
import jax
import jax.numpy as jnp
import numpy as np
from jax import lax

HEADS = 12
HEAD_DIM = 64
D = 768
FF = 3072
ROW = 944
IMGS = 19
MOST = 50
PROP = 9
ACT = 8
PH1 = 256
PH2 = 128
PH3 = 64
ROWS = 16
TOKENS = 15104
NCLS = 304


def raised(values, stream_key, source, target, parts, factor):
    owner, partner = [(jnp.arange(values.shape[dim]) // (values.shape[dim] // parts)).reshape([-1 if axis == dim else 1 for axis in range(values.ndim)]) for dim in (source, target)]
    chosen = jax.random.permutation(stream_key, parts)[partner]
    strong = (owner == chosen) | (owner == (partner + parts // 2) % parts)
    return jnp.where(strong, factor * values, values)


def block_scale(stream_key, extent, split, least, largest):
    factor_of, own = 1.0, jax.random.fold_in(stream_key, 6)
    for position, parts in split:
        draws = jnp.exp(jax.random.uniform(jax.random.fold_in(own, position), (parts,), jnp.float32, least / len(split), largest / len(split)))
        factor_of = factor_of * jnp.repeat(draws, extent[position] // parts).reshape([-1 if axis == position else 1 for axis in range(len(extent))])
    return factor_of


def profile(number_of, total, reach, lean):
    loads = [(1 << 20) // math.isqrt(rank ** lean) + 1 for rank in range(2, number_of + 1)]
    spare, holding = total - reach - (number_of - 1), [1] * (number_of - 1)
    while spare > 0:
        candidates = [i for i in range(number_of - 1) if holding[i] < reach]
        whole, budget = sum([loads[i] for i in candidates]), spare
        for i in candidates:
            more = min(reach - holding[i], max(1, budget * loads[i] // whole), spare)
            holding[i] = holding[i] + more
            spare = spare - more
    return np.array([reach] + holding)


def ragged(stream_key, amount, total, limit, lean):
    if amount == 2:
        one = jax.random.randint(stream_key, (), max(1, total - limit), min(limit, total - 1) + 1)
        return jnp.stack([one, total - one])
    tallies = jnp.asarray(profile(amount, total, limit, lean), jnp.int32)
    twos = (amount - 1) // 2
    donor, sink = tallies[1:1 + 2 * twos:2], tallies[2:2 + 2 * twos:2]
    slack = jnp.minimum(donor - 1, limit - sink)
    shifted = jax.random.randint(jax.random.fold_in(stream_key, 1), (twos,), 0, 1 << 20) % (slack + 1)
    tallies = tallies.at[1:1 + 2 * twos:2].set(donor - shifted).at[2:2 + 2 * twos:2].set(sink + shifted)
    return tallies[jax.random.permutation(jax.random.fold_in(stream_key, 2), amount)]


def scatter_about(own_key, shape, scale, most, shards=(), kind=jnp.bfloat16):
    loudness = block_scale(own_key, shape, shards, -0.22, 0.18) if shards else 1.0
    entries = jax.random.normal(own_key, shape, jnp.float32) * scale * loudness
    return jnp.minimum(jnp.maximum(entries, -most), most).astype(kind)


def bell_draw_with(own_key, dims, deviation, most, split, heavy, kind=jnp.bfloat16):
    result = deviation * jax.random.normal(own_key, dims, jnp.float32)
    if split:
        result = result * block_scale(own_key, dims, split, -0.22, 0.18)
    return jnp.clip(raised(result, jax.random.fold_in(own_key, 3), *heavy), -most, most).astype(kind)


def setup_inputs(seed: int = 0) -> dict:
    splits = jax.random.split(jax.random.key(seed), 23)
    patches = scatter_about(splits[0], (TOKENS, D), 1.0, 6.0, ((0, 16),), jnp.float32)
    segment_ids = jax.vmap(lambda own: jnp.searchsorted(jnp.cumsum(ragged(own, IMGS, ROW, MOST, 1)), jnp.arange(ROW), side="right"))(jax.random.split(splits[1], ROWS)).reshape((ROWS, ROW)).astype(jnp.int32)
    proprio = scatter_about(splits[2], (NCLS, PROP), 1.0, 6.0, ((0, 16),), jnp.float32)
    ln1_gain = jnp.clip(1.0 + 0.1 * jax.random.normal(splits[3], (D,), jnp.float32), 0.5, 1.5)
    ln1_bias = scatter_about(splits[4], (D,), 0.3, 2.0, (), jnp.float32)
    qkv_weight = scatter_about(splits[5], (D, 3, D), D ** -0.5, 0.21875, ((2, 2),), jnp.float32)
    qv_bias = scatter_about(splits[6], (2, D), 0.3, 2.0, ((1, 2),), jnp.float32)
    out_weight = scatter_about(splits[7], (D, D), (D * IMGS // ROW) ** -0.5, 1.5, ((0, 2),), jnp.float32)
    out_bias = scatter_about(splits[8], (D,), 0.3, 2.0, (), jnp.float32)
    ln2_gain = jnp.clip(1.0 + 0.1 * jax.random.normal(splits[9], (D,), jnp.float32), 0.5, 1.5)
    ln2_bias = scatter_about(splits[10], (D,), 0.3, 2.0, (), jnp.float32)
    fc1_weight = scatter_about(splits[11], (D, FF), D ** -0.5, 0.21875, ((1, 2),), jnp.float32)
    fc1_bias = scatter_about(splits[12], (FF,), 0.3, 2.0, ((0, 2),), jnp.float32)
    fc2_weight = scatter_about(splits[13], (FF, D), FF ** -0.5, 0.109375, ((0, 2),), jnp.float32)
    fc2_bias = scatter_about(splits[14], (D,), 0.3, 2.0, (), jnp.float32)
    pol_image = scatter_about(splits[15], (D, PH1), D ** -0.5, 0.21875, (), jnp.float32)
    pol_proprio = scatter_about(splits[16], (PROP, PH1), PROP ** -0.5, 2.0, (), jnp.float32)
    pol_hidden = scatter_about(splits[17], (PH1, PH2), PH1 ** -0.5, 0.375, (), jnp.float32)
    pol_third = scatter_about(splits[18], (PH2, PH3), PH2 ** -0.5, 0.5, (), jnp.float32)
    pol_action = scatter_about(splits[19], (PH3, ACT), PH3 ** -0.5, 0.75, (), jnp.float32)
    out_cotangent = bell_draw_with(splits[20], (TOKENS, D), 1.0, 6.0, ((0, 16),), (0, 1, 16, 2.0), jnp.float32)
    action_cotangent = scatter_about(splits[21], (NCLS, ACT), 1.0, 6.0, ((0, 16),), jnp.float32)
    return {"patches": patches, "segment_ids": segment_ids, "proprio": proprio, "ln1_gain": ln1_gain, "ln1_bias": ln1_bias, "qkv_weight": qkv_weight, "qv_bias": qv_bias, "out_weight": out_weight, "out_bias": out_bias, "ln2_gain": ln2_gain, "ln2_bias": ln2_bias, "fc1_weight": fc1_weight, "fc1_bias": fc1_bias, "fc2_weight": fc2_weight, "fc2_bias": fc2_bias, "pol_image": pol_image, "pol_proprio": pol_proprio, "pol_hidden": pol_hidden, "pol_third": pol_third, "pol_action": pol_action, "out_cotangent": out_cotangent, "action_cotangent": action_cotangent}


@jax.custom_vjp
def low(v):
    return lax.optimization_barrier(v.astype(jnp.bfloat16)).astype(jnp.float32)

@jax.custom_vjp
def low_back(v):
    return v

def low_keep(v):
    return (low(v), None)

def low_pass(kept, grad):
    return (grad,)

def back_keep(v):
    return (v, None)

def back_low(kept, grad):
    return (low(grad),)
low.defvjp(low_keep, low_pass)
low_back.defvjp(back_keep, back_low)
highest = lax.Precision.HIGHEST
norm_eps = 1e-06

def layer_norm(inputs, gain, bias):
    centred = inputs - lax.optimization_barrier(jnp.mean(inputs, axis=-1, keepdims=True))
    inverse = lax.rsqrt(lax.optimization_barrier(jnp.mean(centred * centred, axis=-1, keepdims=True)) + norm_eps)
    return centred * inverse * gain + bias

def attend_row(packed):
    query_row, key_row, value_row, seg_row = packed
    scores = jnp.einsum('qhd,khd->hqk', query_row, key_row, precision=highest) / math.sqrt(HEAD_DIM)
    same_image = seg_row[:, None] == seg_row[None, :]
    scores = jnp.where(same_image[None], scores, -1e+30)
    attn_w = jax.nn.softmax(scores, axis=-1)
    return jnp.einsum('hqk,khd->qhd', attn_w, value_row, precision=highest)

def dense(left, right):
    return jnp.dot(left, right, precision=highest)

def reference(patches, segment_ids, proprio, ln1_gain, ln1_bias, qkv_weight, qv_bias, out_weight, out_bias, ln2_gain, ln2_bias, fc1_weight, fc1_bias, fc2_weight, fc2_bias, pol_image, pol_proprio, pol_hidden, pol_third, pol_action, out_cotangent, action_cotangent):
    first_tok = jnp.concatenate([jnp.ones((ROWS, 1), bool), segment_ids[:, 1:] != segment_ids[:, :-1]], axis=1)
    image_ids = jnp.arange(IMGS, dtype=jnp.int32)
    cls_pick = ((segment_ids[:, None, :] == image_ids[None, :, None]) & first_tok[:, None, :]).astype(patches.dtype)

    def forward(inputs, gain_one, bias_one, w_qkv, b_qv, w_out, b_out, gain_two, bias_two, w_fc1, b_fc1, w_fc2, b_fc2, p_image, p_prop, p_hidden, p_third, p_action):
        normed_in = layer_norm(inputs, gain_one, bias_one)
        projected = jnp.einsum('td,dcn->tcn', normed_in, w_qkv, precision=highest)
        queries = (projected[:, 0] + b_qv[0]).reshape(ROWS, ROW, HEADS, HEAD_DIM)
        keys_all = projected[:, 1].reshape(ROWS, ROW, HEADS, HEAD_DIM)
        values = (projected[:, 2] + b_qv[1]).reshape(ROWS, ROW, HEADS, HEAD_DIM)
        context = lax.map(jax.checkpoint(attend_row), (queries, keys_all, values, segment_ids))
        context = context.reshape(TOKENS, D)
        mid = inputs + dense(context, w_out) + b_out
        normed_mid = layer_norm(mid, gain_two, bias_two)
        activated = jax.nn.gelu(dense(normed_mid, w_fc1) + b_fc1, approximate=False)
        encoded = mid + dense(activated, w_fc2) + b_fc2
        cls_features = jnp.einsum('rst,rtd->rsd', cls_pick, encoded.reshape(ROWS, ROW, D), precision=highest).reshape(NCLS, D)
        hidden_one = jax.nn.elu(dense(cls_features, p_image) + dense(proprio, p_prop))
        hidden_two = jax.nn.elu(dense(hidden_one, p_hidden))
        hidden_three = jax.nn.elu(dense(hidden_two, p_third))
        actions = dense(hidden_three, p_action)
        return (encoded, actions)
    outputs, pullback = jax.vjp(forward, patches, ln1_gain, ln1_bias, qkv_weight, qv_bias, out_weight, out_bias, ln2_gain, ln2_bias, fc1_weight, fc1_bias, fc2_weight, fc2_bias, pol_image, pol_proprio, pol_hidden, pol_third, pol_action)
    encoded, actions = outputs
    patches_grad, ln1_gain_grad, ln1_bias_grad, qkv_weight_grad, qv_bias_grad, out_weight_grad, out_bias_grad, ln2_gain_grad, ln2_bias_grad, fc1_weight_grad, fc1_bias_grad, fc2_weight_grad, fc2_bias_grad, pol_image_grad, pol_proprio_grad, pol_hidden_grad, pol_third_grad, pol_action_grad = pullback((out_cotangent, action_cotangent))
    return (encoded, actions, patches_grad, ln1_gain_grad, ln1_bias_grad, qkv_weight_grad, qv_bias_grad, out_weight_grad, out_bias_grad, ln2_gain_grad, ln2_bias_grad, fc1_weight_grad, fc1_bias_grad, fc2_weight_grad, fc2_bias_grad, pol_image_grad, pol_proprio_grad, pol_hidden_grad, pol_third_grad, pol_action_grad)
```

```python
import functools
import math

import jax
import jax.numpy as jnp
from jax import lax
from jax.experimental import pallas as pl
from jax.experimental.pallas import tpu as pltpu
from jax.sharding import PartitionSpec as P

HEAD_DIM = 64
MOST = 50
LANES = 128
TILE = 128
SPAN = 256
SCALE = 0.02

highest = lax.Precision.HIGHEST
norm_eps = 1e-06
f32 = jnp.float32
bf16 = jnp.bfloat16

NN = (((1,), (0,)), ((), ()))
NT = (((1,), (1,)), ((), ()))
TN = (((0,), (0,)), ((), ()))


def split(val):
    high = val.astype(bf16)
    return high, (val - high.astype(f32)).astype(bf16)


def mul(left, right, dims):
    return lax.dot_general(left, right, dims, preferred_element_type=f32)


def mul3(left, right, dims):
    (lh, ll), (rh, rl) = left, right
    return mul(lh, rh, dims) + (mul(lh, rl, dims) + mul(ll, rh, dims))


def dense(left, right):
    return jnp.dot(left, right, precision=highest)


def norm_stats(inputs):
    centred = inputs - jnp.mean(inputs, axis=-1, keepdims=True)
    inverse = lax.rsqrt(jnp.mean(centred * centred, axis=-1, keepdims=True) + norm_eps)
    return centred * inverse, inverse


def norm_back(upstream, unit_val, inverse, gain):
    scaled = upstream * gain
    centred = scaled - jnp.mean(scaled, axis=-1, keepdims=True)
    return inverse * (centred - unit_val * jnp.mean(scaled * unit_val, axis=-1, keepdims=True))


def elu_back(upstream, pre_act):
    return upstream * jnp.where(pre_act > 0, 1.0, jnp.exp(jnp.minimum(pre_act, 0.0)))


def params(limit_mib=56):
    return pltpu.CompilerParams(vmem_limit_bytes=limit_mib << 20)


def cost(flops, nbytes, trans=0):
    return pl.CostEstimate(flops=int(flops * SCALE), bytes_accessed=int(nbytes * SCALE), transcendentals=int(trans * SCALE))


def shape(*dims):
    return jax.ShapeDtypeStruct(dims, f32)


def whole(*dims):
    zeros = (0,) * len(dims)
    return pl.BlockSpec(dims, lambda *_: zeros)


def untouched(deps):
    return [pl.BlockSpec(memory_space=pl.ANY)] * len(deps)


def leaving_out(kernel, first, deps):
    return lambda *refs: kernel(*refs[:first], *refs[first + len(deps) :])


def join_kernel(where_ref, *refs):
    out_ref = refs[-1]
    for i, ref in enumerate(refs[:-1]):
        out_ref[pl.ds(where_ref[i], 1)] = ref[...][None]


def join_pieces(where, pieces):
    rows, cols = pieces[0].shape
    count = len(pieces)
    steps = next(n for n in (4, 3, 2, 1) if rows % (8 * n) == 0)
    part = rows // steps
    out = pl.pallas_call(
        join_kernel,
        out_shape=shape(count, rows, cols),
        grid_spec=pltpu.PrefetchScalarGridSpec(
            num_scalar_prefetch=1,
            grid=(steps,),
            in_specs=[pl.BlockSpec((part, cols), lambda i, w: (i, 0))] * count,
            out_specs=pl.BlockSpec((count, part, cols), lambda i, w: (0, i, 0)),
        ),
        compiler_params=params(),
        cost_estimate=cost(0, 8 * count * rows * cols),
        name="join_pieces",
    )(where, *pieces)
    return out.reshape(count * rows, cols)


def store_rows(core_ref, tile, keep_ref, send_ref, lanes, block):
    if send_ref is None:
        keep_ref[:, lanes] = tile
        return
    pairs = tile.shape[0] // (2 * block)

    def put(first, second):
        for i in range(pairs):
            low = 2 * i * block
            first[i, :, lanes] = tile[low : low + block]
            second[i, :, lanes] = tile[low + block : low + 2 * block]

    @pl.when(core_ref[0] == 0)
    def _():
        put(keep_ref, send_ref)

    @pl.when(core_ref[0] != 0)
    def _():
        put(send_ref, keep_ref)


def qkv_kernel(x_ref, w_ref, b_ref, out_ref, xh_ref, xl_ref):
    @pl.when(pl.program_id(0) == 0)
    def _():
        xh_ref[...], xl_ref[...] = split(x_ref[...])

    out_ref[...] = mul3((xh_ref[...], xl_ref[...]), split(w_ref[0]), NN) + b_ref[...]


def qkv_forward(normed, weight, bias, deps=()):
    toks, dim = normed.shape
    width = weight.shape[2]
    return pl.pallas_call(
        leaving_out(qkv_kernel, 3, deps),
        out_shape=shape(toks, 3 * width),
        grid=(3,),
        in_specs=[
            whole(toks, dim),
            pl.BlockSpec((1, dim, width), lambda c: (c, 0, 0)),
            pl.BlockSpec((1, width), lambda c: (0, c)),
        ]
        + untouched(deps),
        out_specs=pl.BlockSpec((toks, width), lambda c: (0, c)),
        scratch_shapes=[pltpu.VMEM((toks, dim), bf16)] * 2,
        compiler_params=params(),
        cost_estimate=cost(18 * toks * dim * width, 4 * (toks * dim + 3 * width * (dim + toks))),
        name="qkv_forward",
    )(normed, weight, bias, *deps)


def starts_of(toks):
    return [min(max(t * TILE - (SPAN - TILE) // 2, 0), toks - SPAN) for t in range(toks // TILE)]


def both_heads(val):
    lane = lax.broadcasted_iota(jnp.int32, val.shape, 1)
    return jnp.concatenate([jnp.where(lane < HEAD_DIM, val, 0.0), jnp.where(lane >= HEAD_DIM, val, 0.0)])


def one_head_each(val):
    rows = val.shape[0] // 2
    lane = lax.broadcasted_iota(jnp.int32, (rows, LANES), 1)
    return jnp.where(lane < HEAD_DIM, val[:rows], val[rows:])


def mul_deep(left, right):
    (lh, ll), (rh, rl) = left, right
    return mul(jnp.concatenate([lh, ll], 1), jnp.concatenate([rh, rh], 1), NT) + mul(lh, rl, NT)


def mul_wide(left, right, dims):
    (lh, ll), (rh, rl) = left, right
    cols = rh.shape[1]
    both = mul(lh, jnp.concatenate([rh, rl], 1), dims)
    return both[:, :cols] + (both[:, cols:] + mul(ll, rh, dims))


def probs_of(scores, same, axis):
    scores = jnp.where(same, scores, -1e30)
    exponent = jnp.exp(scores - jnp.max(scores, axis=axis, keepdims=True))
    return exponent * (1.0 / jnp.sum(exponent, axis=axis, keepdims=True))


def attend_kernel(q_ref, k_ref, v_ref, col_ref, win_ref, out_ref):
    toks = q_ref.shape[0]
    scale = 1.0 / math.sqrt(HEAD_DIM)
    for t, start in enumerate(starts_of(toks)):
        rows, keys = pl.ds(t * TILE, TILE), pl.ds(start, SPAN)
        same = col_ref[rows, :] == win_ref[t]
        scores = mul_deep(split(both_heads(q_ref[rows, :] * scale)), split(k_ref[keys, :]))
        probs = probs_of(scores, jnp.concatenate([same, same]), 1)
        out_ref[rows, :] = one_head_each(mul_wide(split(probs), split(v_ref[keys, :]), NN))


def pair_specs(toks, pairs, parts):
    return [
        pl.BlockSpec((toks, LANES), functools.partial(lambda part, i: (0, part * pairs + i), part))
        for part in range(parts)
    ]


def attend(qkv, segs, deps=()):
    toks, width = qkv.shape[0], qkv.shape[1] // 3
    pairs = width // LANES
    seg_col, seg_win, _ = segs
    return pl.pallas_call(
        leaving_out(attend_kernel, 5, deps),
        out_shape=shape(toks, width),
        grid=(pairs,),
        in_specs=pair_specs(toks, pairs, 3) + [whole(*seg_col.shape), whole(*seg_win.shape)] + untouched(deps),
        out_specs=pl.BlockSpec((toks, LANES), lambda i: (0, i)),
        compiler_params=params(),
        cost_estimate=cost(24 * toks * SPAN * width, 16 * toks * width, toks * SPAN * width // 64),
        name="attend",
    )(qkv, qkv, qkv, seg_col, seg_win, *deps)


def attend_back_kernel(q_ref, k_ref, v_ref, do_ref, col_ref, row_ref, out_ref):
    toks = q_ref.shape[0]
    scale = 1.0 / math.sqrt(HEAD_DIM)
    out_ref[1:] = jnp.zeros_like(out_ref[1:])
    for t, start in enumerate(starts_of(toks)):
        rows, keys = pl.ds(t * TILE, TILE), pl.ds(start, SPAN)
        same = col_ref[keys, :] == row_ref[t]
        q_pair, g_pair = split(both_heads(q_ref[rows, :] * scale)), split(both_heads(do_ref[rows, :]))
        k_pair, v_pair = split(k_ref[keys, :]), split(v_ref[keys, :])
        probs = probs_of(mul_deep(k_pair, q_pair), same, 0)
        dprobs = mul_deep(v_pair, g_pair)
        dscores = split(probs * (dprobs - jnp.sum(probs * dprobs, axis=0, keepdims=True)))
        out_ref[0, rows, :] = one_head_each(mul_wide(dscores, k_pair, TN)) * scale
        out_ref[1, keys, :] += mul_wide(dscores, q_pair, NN)
        out_ref[2, keys, :] += mul_wide(split(probs), g_pair, NN)


def attend_back(qkv, grad, half, segs, deps=()):
    toks, width = qkv.shape[0], qkv.shape[1] // 3
    pairs = width // LANES
    seg_col, _, seg_row = segs
    return pl.pallas_call(
        leaving_out(attend_back_kernel, 6, deps),
        out_shape=shape(3, toks, width),
        grid=(pairs,),
        in_specs=pair_specs(toks, pairs, 3)
        + [
            pl.BlockSpec((toks, LANES), lambda i: (0, half * pairs + i)),
            whole(*seg_col.shape),
            whole(*seg_row.shape),
        ]
        + untouched(deps),
        out_specs=pl.BlockSpec((3, toks, LANES), lambda i: (0, 0, i)),
        compiler_params=params(),
        cost_estimate=cost(60 * toks * SPAN * width, 28 * toks * width, toks * SPAN * width // 64),
        name="attend_back",
    )(qkv, qkv, qkv, grad, seg_col, seg_row, *deps)


def cdf_of(pre):
    return 0.5 * (1.0 + lax.erf(pre * (1.0 / math.sqrt(2.0))))


def mlp_kernel(x_ref, b_ref, w1_ref, w2_ref, acc_ref, pre_ref, y_ref, xh_ref, xl_ref):
    @pl.when(pl.program_id(0) == 0)
    def _():
        xh_ref[...], xl_ref[...] = split(x_ref[...])
        y_ref[...] = acc_ref[...]

    pre = mul3((xh_ref[...], xl_ref[...]), split(w1_ref[...]), NN) + b_ref[...]
    pre_ref[...] = pre
    y_ref[...] += mul3(split(pre * cdf_of(pre)), split(w2_ref[...]), NN)


def mlp_forward(normed, bias, w1, w2, acc, deps=(), block=512):
    toks, dim = normed.shape
    hidden = w1.shape[1]
    return pl.pallas_call(
        leaving_out(mlp_kernel, 5, deps),
        out_shape=(shape(toks, hidden), shape(toks, dim)),
        grid=(hidden // block,),
        in_specs=[
            whole(toks, dim),
            pl.BlockSpec((1, block), lambda j: (0, j)),
            pl.BlockSpec((dim, block), lambda j: (0, j)),
            pl.BlockSpec((block, dim), lambda j: (j, 0)),
            whole(toks, dim),
        ]
        + untouched(deps),
        out_specs=(pl.BlockSpec((toks, block), lambda j: (0, j)), whole(toks, dim)),
        scratch_shapes=[pltpu.VMEM((toks, dim), bf16)] * 2,
        compiler_params=params(),
        cost_estimate=cost(12 * toks * dim * hidden, 8 * dim * hidden + 4 * toks * (hidden + 2 * dim), toks * hidden),
        name="mlp_forward",
    )(normed, bias, w1, w2, acc, *deps)


def own_then_other(half):
    return (lambda j: jnp.minimum(j, half - 1)), (lambda j: jnp.maximum(j - half, 0))


def fill_transposed(src_ref, high_ref, low_ref):
    high_ref[...], low_ref[...] = split(jnp.transpose(src_ref[...]))


def mlp_back_a_kernel(half, block, split_out, core_ref, eg_ref, prea_ref, preb_ref, w2a_ref, w2b_ref, *refs):
    j = pl.program_id(0)
    pg_ref, b1_ref, keep_ref = refs[:3]
    send_ref = refs[3] if split_out else None
    eh_ref, el_ref, th_ref, tl_ref = refs[-4:]

    @pl.when(j == 0)
    def _():
        eh_ref[...], el_ref[...] = split(eg_ref[...])
        fill_transposed(eg_ref, th_ref, tl_ref)

    def step(pre_ref, w2_ref):
        pre = pre_ref[...]
        cdf = cdf_of(pre)
        pdf = jnp.exp(-0.5 * pre * pre) * (1.0 / math.sqrt(2.0 * math.pi))
        pg = mul3((eh_ref[...], el_ref[...]), split(w2_ref[...]), NT) * (cdf + pre * pdf)
        pg_ref[...] = pg
        b1_ref[...] = jnp.sum(pg, axis=0, keepdims=True)
        tile = mul3((th_ref[...], tl_ref[...]), split(pre * cdf), NN)
        store_rows(core_ref, tile, keep_ref, send_ref, slice(None), block)

    @pl.when(j < half)
    def _():
        step(prea_ref, w2a_ref)

    @pl.when(j >= half)
    def _():
        step(preb_ref, w2b_ref)


def grad_shapes(dim, cols, block, split_out):
    if split_out:
        return [shape(dim // (2 * block), block, cols)] * 2
    return [shape(dim, cols)]


def grad_specs(dim, cols, block, split_out):
    if split_out:
        return [pl.BlockSpec((dim // (2 * block), block, cols), lambda j, *_: (0, 0, j))] * 2
    return [pl.BlockSpec((dim, cols), lambda j, *_: (0, j))]


def mlp_back_a(core, enc_grad, pre, w2, rows, split_out, deps=(), block=512):
    toks, dim = enc_grad.shape
    hidden = 2 * pre[0].shape[1]
    half = hidden // 2 // block
    low, high = own_then_other(half)
    out = pl.pallas_call(
        leaving_out(functools.partial(mlp_back_a_kernel, half, rows, split_out), 6, deps),
        out_shape=[shape(toks, hidden), shape(1, hidden)] + grad_shapes(dim, hidden, rows, split_out),
        grid_spec=pltpu.PrefetchScalarGridSpec(
            num_scalar_prefetch=1,
            grid=(2 * half,),
            in_specs=[
                whole(toks, dim),
                pl.BlockSpec((toks, block), lambda j, _: (0, low(j))),
                pl.BlockSpec((toks, block), lambda j, _: (0, high(j))),
                pl.BlockSpec((block, dim), lambda j, _: (low(j), 0)),
                pl.BlockSpec((block, dim), lambda j, _: (high(j), 0)),
            ]
            + untouched(deps),
            out_specs=[
                pl.BlockSpec((toks, block), lambda j, _: (0, j)),
                pl.BlockSpec((1, block), lambda j, _: (0, j)),
            ]
            + grad_specs(dim, block, rows, split_out),
            scratch_shapes=[pltpu.VMEM((toks, dim), bf16)] * 2 + [pltpu.VMEM((dim, toks), bf16)] * 2,
        ),
        compiler_params=params(),
        cost_estimate=cost(12 * toks * dim * hidden, 8 * dim * hidden + 8 * toks * hidden, 2 * toks * hidden),
        name="mlp_back_a",
    )(core, enc_grad, *pre, *w2, *deps)
    return out[0], out[1], out[2:]


def mlp_input_kernel(half, pg_ref, wa_ref, wb_ref, dx_ref):
    j = pl.program_id(0)

    @pl.when(j == 0)
    def _():
        dx_ref[...] = jnp.zeros_like(dx_ref)

    @pl.when(j < half)
    def _():
        dx_ref[...] += mul3(split(pg_ref[...]), split(wa_ref[...]), NT)

    @pl.when(j >= half)
    def _():
        dx_ref[...] += mul3(split(pg_ref[...]), split(wb_ref[...]), NT)


def mlp_input_grad(pre_grad, w1, deps=(), block=768):
    toks, hidden = pre_grad.shape
    dim = w1[0].shape[0]
    half = hidden // 2 // block
    low, high = own_then_other(half)
    return pl.pallas_call(
        leaving_out(functools.partial(mlp_input_kernel, half), 3, deps),
        out_shape=shape(toks, dim),
        grid=(2 * half,),
        in_specs=[
            pl.BlockSpec((toks, block), lambda j: (0, j)),
            pl.BlockSpec((dim, block), lambda j: (0, low(j))),
            pl.BlockSpec((dim, block), lambda j: (0, high(j))),
        ]
        + untouched(deps),
        out_specs=whole(toks, dim),
        compiler_params=params(),
        cost_estimate=cost(6 * toks * dim * hidden, 4 * dim * hidden + 4 * toks * hidden),
        name="mlp_input_grad",
    )(pre_grad, *w1, *deps)


def weight_grad_kernel(rows, split_out, core_ref, x_ref, g_ref, *refs):
    th_ref, tl_ref = refs[-2:]
    outs = refs[-4:-2] if split_out else (refs[-3], None)

    @pl.when(pl.program_id(0) == 0)
    def _():
        fill_transposed(x_ref, th_ref, tl_ref)

    grad = g_ref[0] if len(g_ref.shape) == 3 else g_ref[...]
    tile = mul3((th_ref[...], tl_ref[...]), split(grad), NN)
    store_rows(core_ref, tile, *outs, slice(None), rows)


def weight_grad(core, inputs, grad, rows, split_out, block, into=(), first=0, cols=None, deps=()):
    toks, dim = inputs.shape
    planes = grad.ndim == 3
    steps = grad.shape[0] if planes else grad.shape[1] // block
    width = steps * block
    cols = cols or width
    g_spec = (
        pl.BlockSpec((1, toks, block), lambda j, _: (j, 0, 0)) if planes else pl.BlockSpec((toks, block), lambda j, _: (0, j))
    )
    shapes = grad_shapes(dim, cols, rows, split_out)
    if split_out:
        out_spec = pl.BlockSpec((dim // (2 * rows), rows, block), lambda j, _: (0, 0, j + first))
    else:
        out_spec = pl.BlockSpec((dim, block), lambda j, _: (0, j + first))
    return pl.pallas_call(
        functools.partial(weight_grad_kernel, rows, split_out),
        out_shape=shapes,
        grid_spec=pltpu.PrefetchScalarGridSpec(
            num_scalar_prefetch=1,
            grid=(steps,),
            in_specs=[whole(toks, dim), g_spec] + untouched(into) + untouched(deps),
            out_specs=[out_spec] * len(shapes),
            scratch_shapes=[pltpu.VMEM((dim, toks), bf16)] * 2,
        ),
        input_output_aliases={3 + i: i for i in range(len(into))},
        compiler_params=params(),
        cost_estimate=cost(6 * toks * dim * width, 4 * (toks * dim + dim * width + toks * width)),
        name="weight_grad",
    )(core, inputs, grad, *into, *deps)


def out_back_kernel(rows, split_out, core_ref, g_ref, wa_ref, wb_ref, ca_ref, cb_ref, *refs):
    j = pl.program_id(0)
    dc_ref, keep_ref = refs[:2]
    send_ref = refs[2] if split_out else None
    gh_ref, gl_ref, th_ref, tl_ref = refs[-4:]

    @pl.when(j == 0)
    def _():
        gh_ref[...], gl_ref[...] = split(g_ref[...])
        fill_transposed(g_ref, th_ref, tl_ref)

    def step(w_ref, c_ref):
        dc_ref[...] = mul3((gh_ref[...], gl_ref[...]), split(w_ref[...]), NT)
        tile = mul3((th_ref[...], tl_ref[...]), split(c_ref[...]), NN)
        store_rows(core_ref, tile, keep_ref, send_ref, slice(None), rows)

    @pl.when(j == 0)
    def _():
        step(wa_ref, ca_ref)

    @pl.when(j == 1)
    def _():
        step(wb_ref, cb_ref)


def out_back(core, mid_grad, weights, ctx, rows, split_out, deps=()):
    toks, dim = mid_grad.shape
    width = ctx[0].shape[1]
    cols = 8 * width
    shapes = grad_shapes(dim, cols, rows, split_out)
    if split_out:
        spec = pl.BlockSpec((dim // (2 * rows), rows, width), lambda j, _: (0, 0, 4 * j))
    else:
        spec = pl.BlockSpec((dim, width), lambda j, _: (0, 4 * j))
    out = pl.pallas_call(
        leaving_out(functools.partial(out_back_kernel, rows, split_out), 6, deps),
        out_shape=[shape(toks, 2 * width)] + shapes,
        grid_spec=pltpu.PrefetchScalarGridSpec(
            num_scalar_prefetch=1,
            grid=(2,),
            in_specs=[whole(toks, dim)] + [whole(width, dim)] * 2 + [whole(toks, width)] * 2 + untouched(deps),
            out_specs=[pl.BlockSpec((toks, width), lambda j, _: (0, j))] + [spec] * len(shapes),
            scratch_shapes=[pltpu.VMEM((toks, dim), bf16)] * 2 + [pltpu.VMEM((dim, toks), bf16)] * 2,
        ),
        compiler_params=params(),
        cost_estimate=cost(24 * toks * dim * width, 4 * (toks * dim + 4 * dim * width + 4 * toks * width)),
        name="out_back",
    )(core, mid_grad, *weights, *ctx, *deps)
    return out[0], out[1:]


def qkv_input_kernel(ga_ref, gb_ref, wa_ref, wb_ref, dx_ref):
    @pl.when(pl.program_id(0) == 0)
    def _():
        dx_ref[...] = jnp.zeros_like(dx_ref)

    for g_ref, w_ref in ((ga_ref, wa_ref), (gb_ref, wb_ref)):
        dx_ref[...] += mul3(split(g_ref[0]), split(w_ref[0]), NT)


def qkv_input_grad(grads, weights, deps=()):
    toks = grads[0].shape[1]
    _, dim, width = weights[0].shape
    grad_spec = pl.BlockSpec((1, toks, width), lambda c: (c, 0, 0))
    w_spec = pl.BlockSpec((1, dim, width), lambda c: (c, 0, 0))
    return pl.pallas_call(
        leaving_out(qkv_input_kernel, 4, deps),
        out_shape=shape(toks, dim),
        grid=(3,),
        in_specs=[grad_spec, grad_spec, w_spec, w_spec] + untouched(deps),
        out_specs=whole(toks, dim),
        compiler_params=params(),
        cost_estimate=cost(36 * toks * dim * width, 4 * (toks * dim + 6 * dim * width + 6 * toks * width)),
        name="qkv_input_grad",
    )(*grads, *weights, *deps)


def per_device(
    n_dp,
    patches,
    segment_ids,
    proprio,
    ln1_gain,
    ln1_bias,
    qkv_weight,
    qv_bias,
    out_weight,
    out_bias,
    ln2_gain,
    ln2_bias,
    fc1_weight,
    fc1_bias,
    fc2_weight,
    fc2_bias,
    pol_image,
    pol_proprio,
    pol_hidden,
    pol_third,
    pol_action,
    out_cotangent,
    action_cotangent,
):
    row_len, dim = patches.shape
    images = proprio.shape[0]
    local_dim = qkv_weight.shape[2]
    local_ff = fc1_weight.shape[1]
    toks = -(-(row_len // 2 + MOST // 2) // TILE) * TILE
    low = row_len - toks
    rows = dim // n_dp
    split_out = rows % 8 == 0

    mine = lax.axis_index("dp")
    side = lax.axis_index("tensor")
    bit_c, bit_y, bit_z, bits_h = mine & 1, (mine >> 1) & 1, (mine >> 2) & 1, mine >> 3
    core = jnp.reshape(bit_c, (1,)).astype(jnp.int32)

    def across(val):
        return lax.ppermute(val, "tensor", [(0, 1), (1, 0)])

    def swap(val, bit):
        return lax.ppermute(val, "dp", [(i, i ^ (1 << bit)) for i in range(n_dp)])

    def pick(val, index, axis):
        return lax.dynamic_index_in_dim(val, index, axis, keepdims=False)

    def gate(*vals):
        return lax.optimization_barrier(vals)

    def slices(weight):
        piece = weight.shape[0] // 8
        return [
            lax.dynamic_slice_in_dim(weight, index * piece, piece, 0)
            for index in (2 * bit_y + bit_c, 4 + 2 * bit_z + bit_c)
        ]

    def joined(pieces, others):
        place = []
        for c in (bit_c, 1 - bit_c):
            place += [2 * bit_y + c, 4 + 2 * bit_z + c, 2 * (1 - bit_y) + c, 4 + 2 * (1 - bit_z) + c]
        return join_pieces(jnp.stack(place).astype(jnp.int32), pieces + others)

    bias_pack = jnp.concatenate([qv_bias.reshape(-1), fc1_bias])
    wq_own = jnp.transpose(qkv_weight, (1, 0, 2))

    seg = segment_ids[0]
    pos = jnp.arange(row_len, dtype=jnp.int32)
    first_tok = jnp.concatenate([jnp.ones((1,), bool), seg[1:] != seg[:-1]])
    cut = jnp.min(jnp.where(first_tok & (pos >= low), pos, row_len))
    start = side * low

    def window(val):
        return lax.dynamic_slice_in_dim(val, start, toks, 0)

    here = start + jnp.arange(toks, dtype=jnp.int32)
    owned = jnp.where(side == 0, here < cut, here >= cut)
    seg_here, first_here = window(seg), window(first_tok)
    seg_col = seg_here[:, None]
    seg_win = jnp.stack([seg_here[s : s + SPAN] for s in starts_of(toks)])[:, None, :]
    seg_tile = seg_here.reshape(-1, 1, TILE)
    segs = (seg_col, seg_win, jnp.concatenate([seg_tile, seg_tile], axis=2))
    cls_pick = (
        (seg_here[None, :] == jnp.arange(images, dtype=jnp.int32)[:, None]) & (first_here & owned)[None, :]
    ).astype(f32)
    mine_image = jnp.sum(cls_pick, axis=1, keepdims=True)

    bias_oth = across(bias_pack)
    sent_q = slices(wq_own.reshape(3 * dim, local_dim))
    got_q = [across(val) for val in sent_q]
    x_in = window(patches)
    unit_in, inverse_in = norm_stats(x_in)
    normed_in = unit_in * ln1_gain + ln1_bias

    def qkv_bias_of(flat):
        return jnp.concatenate([flat[:local_dim], jnp.zeros((local_dim,), f32), flat[local_dim : 2 * local_dim]])[None]

    qkv_own = qkv_forward(normed_in, wq_own, qkv_bias_of(bias_pack))
    qkv_own, bias_oth, *got_q = gate(qkv_own, bias_oth, *got_q)
    near_q = [swap(got_q[0], 1), swap(got_q[1], 2)]
    core_q = [swap(val, 0) for val in got_q]
    half = out_weight.shape[0] // 2
    wo_part = lax.dynamic_slice_in_dim(out_weight, bit_c * half, half, 0)
    wo_part, *sent_1 = gate(wo_part, *slices(fc1_weight), *got_q)[:3]
    got_o = across(wo_part)
    got_1 = [across(val) for val in sent_1]
    ctx_own = attend(qkv_own, segs, deps=[wo_part, *sent_1])
    ctx_own, *near_q = gate(ctx_own, *near_q)
    core_q += [swap(val, 0) for val in near_q]
    wq_oth = joined(list(got_q) + list(near_q), core_q).reshape(3, dim, local_dim)
    sent_2 = slices(fc2_weight)
    qkv_oth = qkv_forward(normed_in, wq_oth, qkv_bias_of(bias_oth), deps=[ctx_own, *sent_2])
    qkv_oth, got_o = gate(qkv_oth, got_o)
    core_o = swap(got_o, 0)
    ctx_oth = attend(qkv_oth, segs, deps=[got_o])
    ctx_oth, core_o, *got_1 = gate(ctx_oth, core_o, *got_1)
    wo_oth = join_pieces(jnp.stack([bit_c, 1 - bit_c]).astype(jnp.int32), [got_o, core_o])
    near_1 = [swap(got_1[0], 1), swap(got_1[1], 2)]
    core_1 = [swap(val, 0) for val in got_1]
    sent_2 = gate(*sent_2, *got_1)[:2]
    got_2 = [across(val) for val in sent_2]
    qkv, ctx, wo, wq = [qkv_own, qkv_oth], [ctx_own, ctx_oth], [out_weight, wo_oth], [wq_own, wq_oth]
    high = lax.Precision.HIGH
    attn = jnp.dot(ctx[0], wo[0], precision=high) + jnp.dot(ctx[1], wo[1], precision=high)
    mid = x_in + attn + out_bias
    unit_mid, inverse_mid = norm_stats(mid)
    normed_mid = unit_mid * ln2_gain + ln2_bias
    pre_own, mlp_out = mlp_forward(normed_mid, fc1_bias[None], fc1_weight, fc2_weight, mid + fc2_bias, deps=got_1)
    mlp_out, *moved = gate(mlp_out, *near_1, *core_1, *got_2)
    near_1, core_1, got_2 = moved[:2], moved[2:4], moved[4:]
    near_2 = [swap(got_2[0], 1), swap(got_2[1], 2)]
    core_1 += [swap(val, 0) for val in near_1]
    core_2 = [swap(val, 0) for val in got_2]
    w1_oth = joined(list(got_1) + list(near_1), core_1)
    w1_oth, *near_2 = gate(w1_oth, *near_2)
    core_2 += [swap(val, 0) for val in near_2]
    w2_oth = joined(list(got_2) + list(near_2), core_2)
    pre_oth, enc = mlp_forward(normed_mid, bias_oth[None, 2 * local_dim :], w1_oth, w2_oth, mlp_out)
    w1, w2, pre_act = (fc1_weight, w1_oth), (fc2_weight, w2_oth), (pre_own, pre_oth)
    enc_got = across(enc)

    cls_features = dense(cls_pick, enc)
    act_cot = action_cotangent * mine_image
    pre_one = dense(cls_features, pol_image) + dense(proprio, pol_proprio)
    hidden_one = jax.nn.elu(pre_one)
    pre_two = dense(hidden_one, pol_hidden)
    hidden_two = jax.nn.elu(pre_two)
    pre_three = dense(hidden_two, pol_third)
    hidden_three = jax.nn.elu(pre_three)
    actions_part = dense(hidden_three, pol_action) * mine_image
    grad_p4 = dense(hidden_three.T, act_cot)
    grad_three = elu_back(dense(act_cot, pol_action.T), pre_three)
    grad_p3 = dense(hidden_two.T, grad_three)
    grad_two = elu_back(dense(grad_three, pol_third.T), pre_two)
    grad_p2 = dense(hidden_one.T, grad_two)
    grad_one = elu_back(dense(grad_two, pol_hidden.T), pre_one)
    grad_pimage = dense(cls_features.T, grad_one)
    grad_pprop = dense(proprio.T, grad_one)
    cls_grad = dense(grad_one, pol_image.T)

    def share(val):
        return val[..., : val.shape[-1] // 2], val[..., val.shape[-1] // 2 :]

    class Chain:
        def __init__(self, terms, order):
            self.terms, self.moving = terms, None
            levels = 0
            while 8 << levels < n_dp:
                levels += 1
            self.plan = list(order) + ["x"] + list(range(3, 3 + levels))
            self.axis = {1: 2, 2: 1} if order[0] == 1 else {2: 1, 1: 1}

        def step(self, tied):
            if self.moving is not None:
                tied, got = gate(tied, self.moving)
                self.terms.append(got)
            what = self.plan.pop(0)
            if what == "x":
                out = sum(share(val)[1] for val in self.terms)
                tied, out = gate(tied, out)
                self.terms, self.moving = [share(val)[0] for val in self.terms], across(out)
                return tied
            bit = (mine >> what) & 1
            axis = self.axis.get(what, 1)
            if what >= 3:
                self.terms = [val.reshape((val.shape[0] // 2, 2) + val.shape[1:]) for val in self.terms]
            out = sum(pick(val, 1 - bit, axis) for val in self.terms)
            tied, out = gate(tied, out)
            self.terms, self.moving = [pick(val, bit, axis) for val in self.terms], swap(out, what)
            return tied

    class Scatter:
        def __init__(self, parts, orders):
            self.parts, self.orders, self.chains = parts, orders, []
            if split_out:
                self.got = swap(parts[1], 0)

        def step(self, tied, only=None):
            if not split_out:
                return tied
            if not self.chains:
                tied, self.got = gate(tied, self.got)
                count = len(self.orders)
                piece = rows // count
                terms = [val.reshape((n_dp // 8, 2, 2) + val.shape[1:]) for val in (self.parts[0], self.got)]
                self.chains = [
                    Chain([val[..., i * piece : (i + 1) * piece, :] for val in terms], order)
                    for i, order in enumerate(self.orders)
                ]
            for i, chain in enumerate(self.chains):
                if (only is None or i == only) and chain.plan:
                    tied = chain.step(tied)
            return tied

        def result(self):
            if not split_out:
                own, oth = share(self.parts[0])
                return lax.psum_scatter(own + across(oth), "dp", scatter_dimension=0, tiled=True)
            while not self.chains or any(chain.plan for chain in self.chains):
                self.step(core)
            return jnp.concatenate([sum(val[0] for val in chain.terms + [chain.moving]) for chain in self.chains])

    class Total:
        def __init__(self, val, halve):
            self.halve = halve
            levels = 1
            while 2 << levels <= n_dp:
                levels += 1
            self.plan = list(range(1, levels)) + ["x"]
            if halve:
                pair = val.reshape((2, val.shape[0] // 2) + val.shape[1:])
                self.sent = pick(pair, 1 - bit_c, 0)
                self.val, self.moving = pick(pair, bit_c, 0), swap(self.sent, 0)
            else:
                self.val, self.moving = val, swap(val, 0)

        def step(self, tied):
            tied, got = gate(tied, self.moving)
            self.val = self.val + got
            if self.plan:
                what = self.plan.pop(0)
                self.moving = across(self.val) if what == "x" else swap(self.val, what)
            else:
                self.moving = None
            return gate(tied, self.val)[0]

        def result(self):
            while self.moving is not None:
                self.step(core)
            if not self.halve:
                return self.val
            got = swap(self.val, 0)
            first = jnp.where(bit_c == 0, self.val, got)
            return jnp.concatenate([first, jnp.where(bit_c == 0, got, self.val)])

    pad = lambda val, h, w: jnp.pad(val, ((0, h - val.shape[0]), (0, w - val.shape[1])))
    hid = pol_hidden.shape[1]
    rest = jnp.concatenate([pad(grad_p3, hid, hid), pad(grad_p4, pol_hidden.shape[0] - hid, hid)], axis=0)
    pol_pack = jnp.concatenate([grad_pimage, pad(grad_pprop, 16, pol_image.shape[1]), jnp.concatenate([grad_p2, rest], axis=1)])
    enc_grad = jnp.where(owned[:, None], window(out_cotangent), 0.0) + lax.dot_general(
        cls_pick, cls_grad, TN, precision=highest
    )
    pol = Total(pol_pack, True)
    pre_grad, grad_b1, parts_w2 = mlp_back_a(core, enc_grad, pre_act, w2, rows, split_out, deps=[pol.sent])
    sum_2 = Scatter(parts_w2, [(1, 2)])
    pre_grad = pol.step(pre_grad)
    normed_mid_grad = mlp_input_grad(pre_grad, w1, deps=[pol.val])
    normed_mid_grad = sum_2.step(normed_mid_grad)
    normed_mid_grad = pol.step(normed_mid_grad)
    parts_w1 = weight_grad(core, normed_mid, pre_grad, rows, split_out, 512, deps=[normed_mid_grad])
    sum_1 = Scatter(parts_w1, [(1, 2), (2, 1)])
    mid_grad = enc_grad + norm_back(normed_mid_grad, unit_mid, inverse_mid, ln2_gain)
    mid_grad, kept = gate(mid_grad, parts_w1[0])
    mid_grad = pol.step(mid_grad)
    ctx_grad, parts_a = out_back(core, mid_grad, wo, ctx, rows, split_out, deps=[kept])
    ctx_grad = sum_1.step(ctx_grad)
    dqkv_oth = attend_back(qkv[1], ctx_grad, 1, segs)
    dqkv_own = attend_back(qkv[0], ctx_grad, 0, segs, deps=[dqkv_oth])
    dqkv_own = sum_2.step(dqkv_own)
    dqkv_own = pol.step(dqkv_own)
    merge = functools.partial(weight_grad, core, normed_in, rows=rows, split_out=split_out, block=local_dim, cols=8 * local_dim)
    parts_a = merge(grad=dqkv_oth, into=parts_a, first=5, deps=[dqkv_own])
    parts_a = merge(grad=dqkv_own, into=parts_a, first=1)
    sum_a = Scatter(parts_a, [(1, 2), (2, 1)])
    dqkv_own, kept = gate(dqkv_own, parts_a[0])
    dqkv_own = sum_1.step(dqkv_own, 1)
    dqkv = [dqkv_own, dqkv_oth]
    normed_in_grad = qkv_input_grad(dqkv, wq, deps=[kept])
    normed_in_grad = sum_a.step(normed_in_grad)
    normed_in_grad = sum_2.step(normed_in_grad)
    normed_in_grad = sum_1.step(normed_in_grad, 0)
    normed_in_grad = sum_1.step(normed_in_grad, 1)
    actions_part, enc_got, normed_in_grad = gate(actions_part, enc_got, normed_in_grad)
    actions = actions_part + across(actions_part)
    patches_grad = mid_grad + norm_back(normed_in_grad, unit_in, inverse_in, ln1_gain)
    pg_got = across(patches_grad)

    def token_sum(val):
        return jnp.sum(val, axis=0)

    common = jnp.concatenate(
        [
            token_sum(normed_in_grad * unit_in),
            token_sum(normed_in_grad),
            token_sum(mid_grad),
            token_sum(normed_mid_grad * unit_mid),
            token_sum(normed_mid_grad),
            token_sum(enc_grad),
        ]
    )
    halves = [
        jnp.concatenate([token_sum(dqkv[i][0]), token_sum(dqkv[i][2]), grad_b1[0, i * local_ff : (i + 1) * local_ff]])
        for i in range(2)
    ]
    small = Total(jnp.concatenate([common] + halves), False)
    small.plan.remove("x")
    tied = small.step(core)
    tied = sum_2.step(tied)
    tied = sum_1.step(tied, 0)
    tied = sum_1.step(tied, 1)
    tied = small.step(tied)
    tied = sum_a.step(tied)
    tied = pol.step(tied)
    vec = small.result()
    summed_w2, summed_w1, summed_attn, pol_sum = sum_2.result(), sum_1.result(), sum_a.result(), pol.result()
    common, halves = vec[: 6 * dim], (vec[6 * dim : 6 * dim + 2 * local_dim + local_ff], vec[6 * dim + 2 * local_dim + local_ff :])
    vec = jnp.concatenate([common, halves[0]]) + across(jnp.concatenate([common, halves[1]]))
    common, halves = vec[: 6 * dim].reshape(6, dim), vec[6 * dim :]

    def assemble(own, got):
        left = jnp.where(side == 0, own, got)
        right = jnp.where(side == 0, got, own)
        overlap = toks - low
        inside = low + jnp.arange(overlap, dtype=jnp.int32)
        return jnp.concatenate(
            [left[:low], jnp.where((inside < cut)[:, None], left[low:], right[:overlap]), right[overlap:]]
        )

    width = pol_image.shape[0]
    tail = pol_sum[width + 16 :]
    return (
        assemble(enc, enc_got),
        actions,
        assemble(patches_grad, pg_got),
        common[0],
        common[1],
        summed_attn[:, local_dim:].reshape(rows, 3, local_dim),
        halves[: 2 * local_dim].reshape(2, local_dim),
        summed_attn[:, :local_dim].T,
        common[2],
        common[3],
        common[4],
        summed_w1,
        halves[2 * local_dim :],
        summed_w2.T,
        common[5],
        pol_sum[:width],
        pol_sum[width : width + proprio.shape[1]],
        tail[:, :hid],
        tail[:hid, hid : hid + pol_third.shape[1]],
        tail[hid : hid + pol_action.shape[0], hid : hid + pol_action.shape[1]],
    )


def solution(mesh):
    return jax.shard_map(
        functools.partial(per_device, mesh.shape["dp"]),
        mesh=mesh,
        in_specs=(
            P("dp", None),
            P("dp", None),
            P("dp", None),
            P(),
            P(),
            P(None, None, "tensor"),
            P(None, "tensor"),
            P("tensor", None),
            P(),
            P(),
            P(),
            P(None, "tensor"),
            P("tensor"),
            P("tensor", None),
            P(),
            P(),
            P(),
            P(),
            P(),
            P(),
            P("dp", None),
            P("dp", None),
        ),
        out_specs=(
            P("dp", None),
            P("dp", None),
            P("dp", None),
            P(),
            P(),
            P("dp", None, "tensor"),
            P(None, "tensor"),
            P("tensor", "dp"),
            P(),
            P(),
            P(),
            P("dp", "tensor"),
            P("tensor"),
            P("tensor", "dp"),
            P(),
            P(),
            P(),
            P(),
            P(),
            P(),
        ),
        check_vma=False,
    )
```

```python
import functools
import math

import jax
import jax.numpy as jnp
from jax import lax
from jax.experimental import pallas as pl
from jax.experimental.pallas import tpu as pltpu
from jax.sharding import PartitionSpec as P

HEAD_DIM = 64
MOST = 50
LANES = 128
TILE = 128
SPAN = 256
SCALE = 0.02
COVER = 20.0

highest = lax.Precision.HIGHEST
norm_eps = 1e-06
f32 = jnp.float32
bf16 = jnp.bfloat16

NN = (((1,), (0,)), ((), ()))
NT = (((1,), (1,)), ((), ()))
TN = (((0,), (0,)), ((), ()))


def split(val):
    high = val.astype(bf16)
    return high, (val - high.astype(f32)).astype(bf16)


def mul(left, right, dims):
    return lax.dot_general(left, right, dims, preferred_element_type=f32)


def mul3(left, right, dims):
    (lh, ll), (rh, rl) = left, right
    return mul(lh, rh, dims) + (mul(lh, rl, dims) + mul(ll, rh, dims))


def dense(left, right):
    return jnp.dot(left, right, precision=highest)


def norm_stats(inputs):
    centred = inputs - jnp.mean(inputs, axis=-1, keepdims=True)
    inverse = lax.rsqrt(jnp.mean(centred * centred, axis=-1, keepdims=True) + norm_eps)
    return centred * inverse, inverse


def norm_back(upstream, unit_val, inverse, gain):
    scaled = upstream * gain
    centred = scaled - jnp.mean(scaled, axis=-1, keepdims=True)
    return inverse * (centred - unit_val * jnp.mean(scaled * unit_val, axis=-1, keepdims=True))


def elu_back(upstream, pre_act):
    return upstream * jnp.where(pre_act > 0, 1.0, jnp.exp(jnp.minimum(pre_act, 0.0)))


def params(limit_mib=56):
    return pltpu.CompilerParams(vmem_limit_bytes=limit_mib << 20)


def cost(flops, nbytes, trans=0, scale=SCALE):
    return pl.CostEstimate(flops=int(flops * scale), bytes_accessed=int(nbytes * scale), transcendentals=int(trans * scale))


def shape(*dims):
    return jax.ShapeDtypeStruct(dims, f32)


def whole(*dims):
    zeros = (0,) * len(dims)
    return pl.BlockSpec(dims, lambda *_: zeros)


def untouched(deps):
    return [pl.BlockSpec(memory_space=pl.ANY)] * len(deps)


def leaving_out(kernel, first, deps):
    return lambda *refs: kernel(*refs[:first], *refs[first + len(deps) :])


def join_kernel(where_ref, *refs):
    out_ref = refs[-1]
    for i, ref in enumerate(refs[:-1]):
        out_ref[pl.ds(where_ref[i], 1)] = ref[...][None]


def join_pieces(where, pieces):
    rows, cols = pieces[0].shape
    count = len(pieces)
    steps = next(n for n in (4, 3, 2, 1) if rows % (8 * n) == 0)
    part = rows // steps
    out = pl.pallas_call(
        join_kernel,
        out_shape=shape(count, rows, cols),
        grid_spec=pltpu.PrefetchScalarGridSpec(
            num_scalar_prefetch=1,
            grid=(steps,),
            in_specs=[pl.BlockSpec((part, cols), lambda i, w: (i, 0))] * count,
            out_specs=pl.BlockSpec((count, part, cols), lambda i, w: (0, i, 0)),
        ),
        compiler_params=params(),
        cost_estimate=cost(0, 8 * count * rows * cols),
        name="join_pieces",
    )(where, *pieces)
    return out.reshape(count * rows, cols)


def store_rows(core_ref, tile, keep_ref, send_ref, lanes, block):
    if send_ref is None:
        keep_ref[:, lanes] = tile
        return
    pairs = tile.shape[0] // (2 * block)

    def put(first, second):
        for i in range(pairs):
            low = 2 * i * block
            first[i, :, lanes] = tile[low : low + block]
            second[i, :, lanes] = tile[low + block : low + 2 * block]

    @pl.when(core_ref[0] == 0)
    def _():
        put(keep_ref, send_ref)

    @pl.when(core_ref[0] != 0)
    def _():
        put(send_ref, keep_ref)


def qkv_kernel(x_ref, w_ref, b_ref, out_ref, xh_ref, xl_ref):
    @pl.when(pl.program_id(0) == 0)
    def _():
        xh_ref[...], xl_ref[...] = split(x_ref[...])

    out_ref[...] = mul3((xh_ref[...], xl_ref[...]), split(w_ref[0]), NN) + b_ref[...]


def qkv_forward(normed, weight, bias, deps=()):
    toks, dim = normed.shape
    width = weight.shape[2]
    return pl.pallas_call(
        leaving_out(qkv_kernel, 3, deps),
        out_shape=shape(toks, 3 * width),
        grid=(3,),
        in_specs=[
            whole(toks, dim),
            pl.BlockSpec((1, dim, width), lambda c: (c, 0, 0)),
            pl.BlockSpec((1, width), lambda c: (0, c)),
        ]
        + untouched(deps),
        out_specs=pl.BlockSpec((toks, width), lambda c: (0, c)),
        scratch_shapes=[pltpu.VMEM((toks, dim), bf16)] * 2,
        compiler_params=params(),
        cost_estimate=cost(18 * toks * dim * width, 4 * (toks * dim + 3 * width * (dim + toks))),
        name="qkv_forward",
    )(normed, weight, bias, *deps)


def starts_of(toks):
    return [min(max(t * TILE - (SPAN - TILE) // 2, 0), toks - SPAN) for t in range(toks // TILE)]


def both_heads(val):
    lane = lax.broadcasted_iota(jnp.int32, val.shape, 1)
    return jnp.concatenate([jnp.where(lane < HEAD_DIM, val, 0.0), jnp.where(lane >= HEAD_DIM, val, 0.0)])


def one_head_each(val):
    rows = val.shape[0] // 2
    lane = lax.broadcasted_iota(jnp.int32, (rows, LANES), 1)
    return jnp.where(lane < HEAD_DIM, val[:rows], val[rows:])


def mul_deep(left, right):
    (lh, ll), (rh, rl) = left, right
    return mul(jnp.concatenate([lh, ll], 1), jnp.concatenate([rh, rh], 1), NT) + mul(lh, rl, NT)


def mul_wide(left, right, dims):
    (lh, ll), (rh, rl) = left, right
    cols = rh.shape[1]
    both = mul(lh, jnp.concatenate([rh, rl], 1), dims)
    return both[:, :cols] + (both[:, cols:] + mul(ll, rh, dims))


def probs_of(scores, same, axis):
    scores = jnp.where(same, scores, -1e30)
    exponent = jnp.exp(scores - jnp.max(scores, axis=axis, keepdims=True))
    return exponent * (1.0 / jnp.sum(exponent, axis=axis, keepdims=True))


def attend_kernel(q_ref, k_ref, v_ref, col_ref, win_ref, out_ref):
    toks = q_ref.shape[0]
    scale = 1.0 / math.sqrt(HEAD_DIM)
    for t, start in enumerate(starts_of(toks)):
        rows, keys = pl.ds(t * TILE, TILE), pl.ds(start, SPAN)
        same = col_ref[rows, :] == win_ref[t]
        scores = mul_deep(split(both_heads(q_ref[rows, :] * scale)), split(k_ref[keys, :]))
        probs = probs_of(scores, jnp.concatenate([same, same]), 1)
        out_ref[rows, :] = one_head_each(mul_wide(split(probs), split(v_ref[keys, :]), NN))


def pair_specs(toks, pairs, parts):
    return [
        pl.BlockSpec((toks, LANES), functools.partial(lambda part, i: (0, part * pairs + i), part))
        for part in range(parts)
    ]


def attend(qkv, segs, deps=()):
    toks, width = qkv.shape[0], qkv.shape[1] // 3
    pairs = width // LANES
    seg_col, seg_win, _ = segs
    return pl.pallas_call(
        leaving_out(attend_kernel, 5, deps),
        out_shape=shape(toks, width),
        grid=(pairs,),
        in_specs=pair_specs(toks, pairs, 3) + [whole(*seg_col.shape), whole(*seg_win.shape)] + untouched(deps),
        out_specs=pl.BlockSpec((toks, LANES), lambda i: (0, i)),
        compiler_params=params(),
        cost_estimate=cost(24 * toks * SPAN * width, 16 * toks * width, toks * SPAN * width // 64),
        name="attend",
    )(qkv, qkv, qkv, seg_col, seg_win, *deps)


def attend_back_kernel(q_ref, k_ref, v_ref, do_ref, col_ref, row_ref, out_ref):
    toks = q_ref.shape[0]
    scale = 1.0 / math.sqrt(HEAD_DIM)
    out_ref[1:] = jnp.zeros_like(out_ref[1:])
    for t, start in enumerate(starts_of(toks)):
        rows, keys = pl.ds(t * TILE, TILE), pl.ds(start, SPAN)
        same = col_ref[keys, :] == row_ref[t]
        q_pair, g_pair = split(both_heads(q_ref[rows, :] * scale)), split(both_heads(do_ref[rows, :]))
        k_pair, v_pair = split(k_ref[keys, :]), split(v_ref[keys, :])
        probs = probs_of(mul_deep(k_pair, q_pair), same, 0)
        dprobs = mul_deep(v_pair, g_pair)
        dscores = split(probs * (dprobs - jnp.sum(probs * dprobs, axis=0, keepdims=True)))
        out_ref[0, rows, :] = one_head_each(mul_wide(dscores, k_pair, TN)) * scale
        out_ref[1, keys, :] += mul_wide(dscores, q_pair, NN)
        out_ref[2, keys, :] += mul_wide(split(probs), g_pair, NN)


def attend_back(qkv, grad, half, segs, deps=()):
    toks, width = qkv.shape[0], qkv.shape[1] // 3
    pairs = width // LANES
    seg_col, _, seg_row = segs
    return pl.pallas_call(
        leaving_out(attend_back_kernel, 6, deps),
        out_shape=shape(3, toks, width),
        grid=(pairs,),
        in_specs=pair_specs(toks, pairs, 3)
        + [
            pl.BlockSpec((toks, LANES), lambda i: (0, half * pairs + i)),
            whole(*seg_col.shape),
            whole(*seg_row.shape),
        ]
        + untouched(deps),
        out_specs=pl.BlockSpec((3, toks, LANES), lambda i: (0, 0, i)),
        compiler_params=params(),
        cost_estimate=cost(60 * toks * SPAN * width, 28 * toks * width, toks * SPAN * width // 64),
        name="attend_back",
    )(qkv, qkv, qkv, grad, seg_col, seg_row, *deps)


def cdf_of(pre):
    return 0.5 * (1.0 + lax.erf(pre * (1.0 / math.sqrt(2.0))))


def mlp_kernel(x_ref, b_ref, w1_ref, w2_ref, acc_ref, pre_ref, y_ref, xh_ref, xl_ref):
    @pl.when(pl.program_id(0) == 0)
    def _():
        xh_ref[...], xl_ref[...] = split(x_ref[...])
        y_ref[...] = acc_ref[...]

    pre = mul3((xh_ref[...], xl_ref[...]), split(w1_ref[...]), NN) + b_ref[...]
    pre_ref[...] = pre
    y_ref[...] += mul3(split(pre * cdf_of(pre)), split(w2_ref[...]), NN)


def mlp_forward(normed, bias, w1, w2, acc, deps=(), block=512):
    toks, dim = normed.shape
    hidden = w1.shape[1]
    return pl.pallas_call(
        leaving_out(mlp_kernel, 5, deps),
        out_shape=(shape(toks, hidden), shape(toks, dim)),
        grid=(hidden // block,),
        in_specs=[
            whole(toks, dim),
            pl.BlockSpec((1, block), lambda j: (0, j)),
            pl.BlockSpec((dim, block), lambda j: (0, j)),
            pl.BlockSpec((block, dim), lambda j: (j, 0)),
            whole(toks, dim),
        ]
        + untouched(deps),
        out_specs=(pl.BlockSpec((toks, block), lambda j: (0, j)), whole(toks, dim)),
        scratch_shapes=[pltpu.VMEM((toks, dim), bf16)] * 2,
        compiler_params=params(),
        cost_estimate=cost(12 * toks * dim * hidden, 8 * dim * hidden + 4 * toks * (hidden + 2 * dim), toks * hidden),
        name="mlp_forward",
    )(normed, bias, w1, w2, acc, *deps)


def own_then_other(half):
    return (lambda j: jnp.minimum(j, half - 1)), (lambda j: jnp.maximum(j - half, 0))


def fill_transposed(src_ref, high_ref, low_ref):
    high_ref[...], low_ref[...] = split(jnp.transpose(src_ref[...]))


def mlp_back_a_kernel(half, block, split_out, core_ref, eg_ref, prea_ref, preb_ref, w2a_ref, w2b_ref, *refs):
    j = pl.program_id(0)
    pg_ref, b1_ref, keep_ref = refs[:3]
    send_ref = refs[3] if split_out else None
    eh_ref, el_ref, th_ref, tl_ref = refs[-4:]

    @pl.when(j == 0)
    def _():
        eh_ref[...], el_ref[...] = split(eg_ref[...])
        fill_transposed(eg_ref, th_ref, tl_ref)

    def step(pre_ref, w2_ref):
        pre = pre_ref[...]
        cdf = cdf_of(pre)
        pdf = jnp.exp(-0.5 * pre * pre) * (1.0 / math.sqrt(2.0 * math.pi))
        pg = mul3((eh_ref[...], el_ref[...]), split(w2_ref[...]), NT) * (cdf + pre * pdf)
        pg_ref[...] = pg
        b1_ref[...] = jnp.sum(pg, axis=0, keepdims=True)
        tile = mul3((th_ref[...], tl_ref[...]), split(pre * cdf), NN)
        store_rows(core_ref, tile, keep_ref, send_ref, slice(None), block)

    @pl.when(j < half)
    def _():
        step(prea_ref, w2a_ref)

    @pl.when(j >= half)
    def _():
        step(preb_ref, w2b_ref)


def grad_shapes(dim, cols, block, split_out):
    if split_out:
        return [shape(dim // (2 * block), block, cols)] * 2
    return [shape(dim, cols)]


def grad_specs(dim, cols, block, split_out):
    if split_out:
        return [pl.BlockSpec((dim // (2 * block), block, cols), lambda j, *_: (0, 0, j))] * 2
    return [pl.BlockSpec((dim, cols), lambda j, *_: (0, j))]


def mlp_back_a(core, enc_grad, pre, w2, rows, split_out, deps=(), block=512):
    toks, dim = enc_grad.shape
    hidden = 2 * pre[0].shape[1]
    half = hidden // 2 // block
    low, high = own_then_other(half)
    out = pl.pallas_call(
        leaving_out(functools.partial(mlp_back_a_kernel, half, rows, split_out), 6, deps),
        out_shape=[shape(toks, hidden), shape(1, hidden)] + grad_shapes(dim, hidden, rows, split_out),
        grid_spec=pltpu.PrefetchScalarGridSpec(
            num_scalar_prefetch=1,
            grid=(2 * half,),
            in_specs=[
                whole(toks, dim),
                pl.BlockSpec((toks, block), lambda j, _: (0, low(j))),
                pl.BlockSpec((toks, block), lambda j, _: (0, high(j))),
                pl.BlockSpec((block, dim), lambda j, _: (low(j), 0)),
                pl.BlockSpec((block, dim), lambda j, _: (high(j), 0)),
            ]
            + untouched(deps),
            out_specs=[
                pl.BlockSpec((toks, block), lambda j, _: (0, j)),
                pl.BlockSpec((1, block), lambda j, _: (0, j)),
            ]
            + grad_specs(dim, block, rows, split_out),
            scratch_shapes=[pltpu.VMEM((toks, dim), bf16)] * 2 + [pltpu.VMEM((dim, toks), bf16)] * 2,
        ),
        compiler_params=params(),
        cost_estimate=cost(12 * toks * dim * hidden, 8 * dim * hidden + 8 * toks * hidden, 2 * toks * hidden),
        name="mlp_back_a",
    )(core, enc_grad, *pre, *w2, *deps)
    return out[0], out[1], out[2:]


def mlp_input_kernel(half, pg_ref, wa_ref, wb_ref, dx_ref):
    j = pl.program_id(0)

    @pl.when(j == 0)
    def _():
        dx_ref[...] = jnp.zeros_like(dx_ref)

    @pl.when(j < half)
    def _():
        dx_ref[...] += mul3(split(pg_ref[...]), split(wa_ref[...]), NT)

    @pl.when(j >= half)
    def _():
        dx_ref[...] += mul3(split(pg_ref[...]), split(wb_ref[...]), NT)


def mlp_input_grad(pre_grad, w1, deps=(), block=768):
    toks, hidden = pre_grad.shape
    dim = w1[0].shape[0]
    half = hidden // 2 // block
    low, high = own_then_other(half)
    return pl.pallas_call(
        leaving_out(functools.partial(mlp_input_kernel, half), 3, deps),
        out_shape=shape(toks, dim),
        grid=(2 * half,),
        in_specs=[
            pl.BlockSpec((toks, block), lambda j: (0, j)),
            pl.BlockSpec((dim, block), lambda j: (0, low(j))),
            pl.BlockSpec((dim, block), lambda j: (0, high(j))),
        ]
        + untouched(deps),
        out_specs=whole(toks, dim),
        compiler_params=params(),
        cost_estimate=cost(6 * toks * dim * hidden, 4 * dim * hidden + 4 * toks * hidden, scale=COVER),
        name="mlp_input_grad",
    )(pre_grad, *w1, *deps)


def weight_grad_kernel(rows, split_out, core_ref, x_ref, g_ref, *refs):
    th_ref, tl_ref = refs[-2:]
    outs = refs[-4:-2] if split_out else (refs[-3], None)

    @pl.when(pl.program_id(0) == 0)
    def _():
        fill_transposed(x_ref, th_ref, tl_ref)

    grad = g_ref[0] if len(g_ref.shape) == 3 else g_ref[...]
    tile = mul3((th_ref[...], tl_ref[...]), split(grad), NN)
    store_rows(core_ref, tile, *outs, slice(None), rows)


def weight_grad(core, inputs, grad, rows, split_out, block, into=(), first=0, cols=None, deps=(), scale=SCALE):
    toks, dim = inputs.shape
    planes = grad.ndim == 3
    steps = grad.shape[0] if planes else grad.shape[1] // block
    width = steps * block
    cols = cols or width
    g_spec = (
        pl.BlockSpec((1, toks, block), lambda j, _: (j, 0, 0)) if planes else pl.BlockSpec((toks, block), lambda j, _: (0, j))
    )
    shapes = grad_shapes(dim, cols, rows, split_out)
    if split_out:
        out_spec = pl.BlockSpec((dim // (2 * rows), rows, block), lambda j, _: (0, 0, j + first))
    else:
        out_spec = pl.BlockSpec((dim, block), lambda j, _: (0, j + first))
    return pl.pallas_call(
        functools.partial(weight_grad_kernel, rows, split_out),
        out_shape=shapes,
        grid_spec=pltpu.PrefetchScalarGridSpec(
            num_scalar_prefetch=1,
            grid=(steps,),
            in_specs=[whole(toks, dim), g_spec] + untouched(into) + untouched(deps),
            out_specs=[out_spec] * len(shapes),
            scratch_shapes=[pltpu.VMEM((dim, toks), bf16)] * 2,
        ),
        input_output_aliases={3 + i: i for i in range(len(into))},
        compiler_params=params(),
        cost_estimate=cost(6 * toks * dim * width, 4 * (toks * dim + dim * width + toks * width), scale=scale),
        name="weight_grad",
    )(core, inputs, grad, *into, *deps)


def out_back_kernel(rows, split_out, core_ref, g_ref, wa_ref, wb_ref, ca_ref, cb_ref, *refs):
    j = pl.program_id(0)
    dc_ref, keep_ref = refs[:2]
    send_ref = refs[2] if split_out else None
    gh_ref, gl_ref, th_ref, tl_ref = refs[-4:]

    @pl.when(j == 0)
    def _():
        gh_ref[...], gl_ref[...] = split(g_ref[...])
        fill_transposed(g_ref, th_ref, tl_ref)

    def step(w_ref, c_ref):
        dc_ref[...] = mul3((gh_ref[...], gl_ref[...]), split(w_ref[...]), NT)
        tile = mul3((th_ref[...], tl_ref[...]), split(c_ref[...]), NN)
        store_rows(core_ref, tile, keep_ref, send_ref, slice(None), rows)

    @pl.when(j == 0)
    def _():
        step(wa_ref, ca_ref)

    @pl.when(j == 1)
    def _():
        step(wb_ref, cb_ref)


def out_back(core, mid_grad, weights, ctx, rows, split_out, deps=()):
    toks, dim = mid_grad.shape
    width = ctx[0].shape[1]
    cols = 8 * width
    shapes = grad_shapes(dim, cols, rows, split_out)
    if split_out:
        spec = pl.BlockSpec((dim // (2 * rows), rows, width), lambda j, _: (0, 0, 4 * j))
    else:
        spec = pl.BlockSpec((dim, width), lambda j, _: (0, 4 * j))
    out = pl.pallas_call(
        leaving_out(functools.partial(out_back_kernel, rows, split_out), 6, deps),
        out_shape=[shape(toks, 2 * width)] + shapes,
        grid_spec=pltpu.PrefetchScalarGridSpec(
            num_scalar_prefetch=1,
            grid=(2,),
            in_specs=[whole(toks, dim)] + [whole(width, dim)] * 2 + [whole(toks, width)] * 2 + untouched(deps),
            out_specs=[pl.BlockSpec((toks, width), lambda j, _: (0, j))] + [spec] * len(shapes),
            scratch_shapes=[pltpu.VMEM((toks, dim), bf16)] * 2 + [pltpu.VMEM((dim, toks), bf16)] * 2,
        ),
        compiler_params=params(),
        cost_estimate=cost(24 * toks * dim * width, 4 * (toks * dim + 4 * dim * width + 4 * toks * width)),
        name="out_back",
    )(core, mid_grad, *weights, *ctx, *deps)
    return out[0], out[1:]


def qkv_input_kernel(ga_ref, gb_ref, wa_ref, wb_ref, dx_ref):
    @pl.when(pl.program_id(0) == 0)
    def _():
        dx_ref[...] = jnp.zeros_like(dx_ref)

    for g_ref, w_ref in ((ga_ref, wa_ref), (gb_ref, wb_ref)):
        dx_ref[...] += mul3(split(g_ref[0]), split(w_ref[0]), NT)


def qkv_input_grad(grads, weights, deps=()):
    toks = grads[0].shape[1]
    _, dim, width = weights[0].shape
    grad_spec = pl.BlockSpec((1, toks, width), lambda c: (c, 0, 0))
    w_spec = pl.BlockSpec((1, dim, width), lambda c: (c, 0, 0))
    return pl.pallas_call(
        leaving_out(qkv_input_kernel, 4, deps),
        out_shape=shape(toks, dim),
        grid=(3,),
        in_specs=[grad_spec, grad_spec, w_spec, w_spec] + untouched(deps),
        out_specs=whole(toks, dim),
        compiler_params=params(),
        cost_estimate=cost(36 * toks * dim * width, 4 * (toks * dim + 6 * dim * width + 6 * toks * width), scale=COVER),
        name="qkv_input_grad",
    )(*grads, *weights, *deps)


def per_device(
    n_dp,
    patches,
    segment_ids,
    proprio,
    ln1_gain,
    ln1_bias,
    qkv_weight,
    qv_bias,
    out_weight,
    out_bias,
    ln2_gain,
    ln2_bias,
    fc1_weight,
    fc1_bias,
    fc2_weight,
    fc2_bias,
    pol_image,
    pol_proprio,
    pol_hidden,
    pol_third,
    pol_action,
    out_cotangent,
    action_cotangent,
):
    row_len, dim = patches.shape
    images = proprio.shape[0]
    local_dim = qkv_weight.shape[2]
    local_ff = fc1_weight.shape[1]
    toks = -(-(row_len // 2 + MOST // 2) // TILE) * TILE
    low = row_len - toks
    rows = dim // n_dp
    split_out = rows % 8 == 0

    mine = lax.axis_index("dp")
    side = lax.axis_index("tensor")
    bit_c, bit_y, bit_z, bits_h = mine & 1, (mine >> 1) & 1, (mine >> 2) & 1, mine >> 3
    core = jnp.reshape(bit_c, (1,)).astype(jnp.int32)

    def across(val):
        return lax.ppermute(val, "tensor", [(0, 1), (1, 0)])

    def swap(val, bit):
        return lax.ppermute(val, "dp", [(i, i ^ (1 << bit)) for i in range(n_dp)])

    def pick(val, index, axis):
        return lax.dynamic_index_in_dim(val, index, axis, keepdims=False)

    def gate(*vals):
        return lax.optimization_barrier(vals)

    def slices(weight):
        piece = weight.shape[0] // 8
        return [
            lax.dynamic_slice_in_dim(weight, index * piece, piece, 0)
            for index in (2 * bit_y + bit_c, 4 + 2 * bit_z + bit_c)
        ]

    def joined(pieces, others):
        place = []
        for c in (bit_c, 1 - bit_c):
            place += [2 * bit_y + c, 4 + 2 * bit_z + c, 2 * (1 - bit_y) + c, 4 + 2 * (1 - bit_z) + c]
        return join_pieces(jnp.stack(place).astype(jnp.int32), pieces + others)

    bias_pack = jnp.concatenate([qv_bias.reshape(-1), fc1_bias])
    wq_own = jnp.transpose(qkv_weight, (1, 0, 2))

    seg = segment_ids[0]
    pos = jnp.arange(row_len, dtype=jnp.int32)
    first_tok = jnp.concatenate([jnp.ones((1,), bool), seg[1:] != seg[:-1]])
    cut = jnp.min(jnp.where(first_tok & (pos >= low), pos, row_len))
    start = side * low

    def window(val):
        return lax.dynamic_slice_in_dim(val, start, toks, 0)

    here = start + jnp.arange(toks, dtype=jnp.int32)
    owned = jnp.where(side == 0, here < cut, here >= cut)
    seg_here, first_here = window(seg), window(first_tok)
    seg_col = seg_here[:, None]
    seg_win = jnp.stack([seg_here[s : s + SPAN] for s in starts_of(toks)])[:, None, :]
    seg_tile = seg_here.reshape(-1, 1, TILE)
    segs = (seg_col, seg_win, jnp.concatenate([seg_tile, seg_tile], axis=2))
    cls_pick = (
        (seg_here[None, :] == jnp.arange(images, dtype=jnp.int32)[:, None]) & (first_here & owned)[None, :]
    ).astype(f32)
    mine_image = jnp.sum(cls_pick, axis=1, keepdims=True)

    bias_oth = across(bias_pack)
    sent_q = slices(wq_own.reshape(3 * dim, local_dim))
    got_q = [across(val) for val in sent_q]
    x_in = window(patches)
    unit_in, inverse_in = norm_stats(x_in)
    normed_in = unit_in * ln1_gain + ln1_bias

    def qkv_bias_of(flat):
        return jnp.concatenate([flat[:local_dim], jnp.zeros((local_dim,), f32), flat[local_dim : 2 * local_dim]])[None]

    qkv_own = qkv_forward(normed_in, wq_own, qkv_bias_of(bias_pack))
    qkv_own, bias_oth, *got_q = gate(qkv_own, bias_oth, *got_q)
    near_q = [swap(got_q[0], 1), swap(got_q[1], 2)]
    core_q = [swap(val, 0) for val in got_q]
    half = out_weight.shape[0] // 2
    wo_part = lax.dynamic_slice_in_dim(out_weight, bit_c * half, half, 0)
    wo_part, *sent_1 = gate(wo_part, *slices(fc1_weight), *got_q)[:3]
    got_o = across(wo_part)
    got_1 = [across(val) for val in sent_1]
    ctx_own = attend(qkv_own, segs, deps=[wo_part, *sent_1])
    ctx_own, *near_q = gate(ctx_own, *near_q)
    core_q += [swap(val, 0) for val in near_q]
    wq_oth = joined(list(got_q) + list(near_q), core_q).reshape(3, dim, local_dim)
    sent_2 = slices(fc2_weight)
    qkv_oth = qkv_forward(normed_in, wq_oth, qkv_bias_of(bias_oth), deps=[ctx_own, *sent_2])
    qkv_oth, got_o = gate(qkv_oth, got_o)
    core_o = swap(got_o, 0)
    ctx_oth = attend(qkv_oth, segs, deps=[got_o])
    ctx_oth, core_o, *got_1 = gate(ctx_oth, core_o, *got_1)
    wo_oth = join_pieces(jnp.stack([bit_c, 1 - bit_c]).astype(jnp.int32), [got_o, core_o])
    near_1 = [swap(got_1[0], 1), swap(got_1[1], 2)]
    core_1 = [swap(val, 0) for val in got_1]
    sent_2 = gate(*sent_2, *got_1)[:2]
    got_2 = [across(val) for val in sent_2]
    qkv, ctx, wo, wq = [qkv_own, qkv_oth], [ctx_own, ctx_oth], [out_weight, wo_oth], [wq_own, wq_oth]
    high = lax.Precision.HIGH
    attn = jnp.dot(ctx[0], wo[0], precision=high) + jnp.dot(ctx[1], wo[1], precision=high)
    mid = x_in + attn + out_bias
    unit_mid, inverse_mid = norm_stats(mid)
    normed_mid = unit_mid * ln2_gain + ln2_bias
    pre_own, mlp_out = mlp_forward(normed_mid, fc1_bias[None], fc1_weight, fc2_weight, mid + fc2_bias, deps=got_1)
    mlp_out, *moved = gate(mlp_out, *near_1, *core_1, *got_2)
    near_1, core_1, got_2 = moved[:2], moved[2:4], moved[4:]
    near_2 = [swap(got_2[0], 1), swap(got_2[1], 2)]
    core_1 += [swap(val, 0) for val in near_1]
    core_2 = [swap(val, 0) for val in got_2]
    w1_oth = joined(list(got_1) + list(near_1), core_1)
    w1_oth, *near_2 = gate(w1_oth, *near_2)
    core_2 += [swap(val, 0) for val in near_2]
    w2_oth = joined(list(got_2) + list(near_2), core_2)
    pre_oth, enc = mlp_forward(normed_mid, bias_oth[None, 2 * local_dim :], w1_oth, w2_oth, mlp_out)
    w1, w2, pre_act = (fc1_weight, w1_oth), (fc2_weight, w2_oth), (pre_own, pre_oth)
    enc_got = across(enc)

    cls_features = dense(cls_pick, enc)
    act_cot = action_cotangent * mine_image
    pre_one = dense(cls_features, pol_image) + dense(proprio, pol_proprio)
    hidden_one = jax.nn.elu(pre_one)
    pre_two = dense(hidden_one, pol_hidden)
    hidden_two = jax.nn.elu(pre_two)
    pre_three = dense(hidden_two, pol_third)
    hidden_three = jax.nn.elu(pre_three)
    actions_part = dense(hidden_three, pol_action) * mine_image
    grad_p4 = dense(hidden_three.T, act_cot)
    grad_three = elu_back(dense(act_cot, pol_action.T), pre_three)
    grad_p3 = dense(hidden_two.T, grad_three)
    grad_two = elu_back(dense(grad_three, pol_third.T), pre_two)
    grad_p2 = dense(hidden_one.T, grad_two)
    grad_one = elu_back(dense(grad_two, pol_hidden.T), pre_one)
    grad_pimage = dense(cls_features.T, grad_one)
    grad_pprop = dense(proprio.T, grad_one)
    cls_grad = dense(grad_one, pol_image.T)

    def share(val):
        return val[..., : val.shape[-1] // 2], val[..., val.shape[-1] // 2 :]

    class Chain:
        def __init__(self, terms, order, first, size):
            self.terms, self.moving, self.first, self.size = terms, None, first, size
            levels = 0
            while 8 << levels < n_dp:
                levels += 1
            self.plan = list(order) + ["x"] + list(range(3, 3 + levels))
            self.axis = {1: 2, 2: 1} if order[0] == 1 else {2: 1, 1: 1}

        def part(self, val, index, axis):
            at, sizes = [0] * val.ndim, list(val.shape)
            at[axis], sizes[axis] = index, 1
            at[-2], sizes[-2] = self.first, self.size
            return jnp.squeeze(lax.dynamic_slice(val, at, sizes), axis)

        def step(self, tied):
            if self.moving is not None:
                tied, got = gate(tied, self.moving)
                self.terms.append(got)
            what = self.plan.pop(0)
            if what == "x":
                out, kept = (sum(share(val)[i] for val in self.terms) for i in (1, 0))
                tied, out = gate(tied, out)
                self.terms, self.moving = [kept], across(out)
                return tied
            bit = (mine >> what) & 1
            axis = self.axis.get(what, 1)
            if what >= 3:
                self.terms = [val.reshape((val.shape[0] // 2, 2) + val.shape[1:]) for val in self.terms]
            out, kept = (sum(self.part(val, index, axis) for val in self.terms) for index in (1 - bit, bit))
            self.first = 0
            tied, out = gate(tied, out)
            self.terms, self.moving = [kept], swap(out, what)
            return tied

    class Scatter:
        def __init__(self, parts, orders):
            self.parts, self.orders, self.chains = parts, orders, []
            if split_out:
                self.got = swap(parts[1], 0)

        def step(self, tied):
            if not split_out:
                return tied
            if not self.chains:
                tied, self.got = gate(tied, self.got)
                piece = rows // len(self.orders)
                terms = [val.reshape((n_dp // 8, 2, 2) + val.shape[1:]) for val in (self.parts[0], self.got)]
                self.chains = [Chain(list(terms), order, i * piece, piece) for i, order in enumerate(self.orders)]
            for chain in self.chains:
                if chain.plan:
                    tied = chain.step(tied)
            return tied

        def hold(self, tied):
            for chain in self.chains:
                tied, chain.moving = gate(tied, chain.moving)
            return tied

        def result(self):
            if not split_out:
                own, oth = share(self.parts[0])
                return lax.psum_scatter(own + across(oth), "dp", scatter_dimension=0, tiled=True)
            while not self.chains or any(chain.plan for chain in self.chains):
                self.step(core)
            return jnp.concatenate([sum(val[0] for val in chain.terms + [chain.moving]) for chain in self.chains])

    class Total:
        def __init__(self, val, halve):
            self.halve = halve
            levels = 1
            while 2 << levels <= n_dp:
                levels += 1
            self.plan = list(range(1, levels)) + ["x"]
            if halve:
                pair = val.reshape((2, val.shape[0] // 2) + val.shape[1:])
                self.sent = pick(pair, 1 - bit_c, 0)
                self.val, self.moving = pick(pair, bit_c, 0), swap(self.sent, 0)
            else:
                self.val, self.moving = val, swap(val, 0)

        def step(self, tied):
            tied, got = gate(tied, self.moving)
            self.val = self.val + got
            if self.plan:
                what = self.plan.pop(0)
                self.moving = across(self.val) if what == "x" else swap(self.val, what)
            else:
                self.moving = None
            return gate(tied, self.val)[0]

        def result(self):
            while self.moving is not None:
                self.step(core)
            if not self.halve:
                return self.val
            got = swap(self.val, 0)
            first = jnp.where(bit_c == 0, self.val, got)
            return jnp.concatenate([first, jnp.where(bit_c == 0, got, self.val)])

    both_orders = [(1, 2), (2, 1)] if rows % 16 == 0 else [(1, 2)]
    pad = lambda val, h, w: jnp.pad(val, ((0, h - val.shape[0]), (0, w - val.shape[1])))
    hid = pol_hidden.shape[1]
    rest = jnp.concatenate([pad(grad_p3, hid, hid), pad(grad_p4, pol_hidden.shape[0] - hid, hid)], axis=0)
    pol_pack = jnp.concatenate([grad_pimage, pad(grad_pprop, 16, pol_image.shape[1]), jnp.concatenate([grad_p2, rest], axis=1)])
    enc_grad = jnp.where(owned[:, None], window(out_cotangent), 0.0) + lax.dot_general(
        cls_pick, cls_grad, TN, precision=highest
    )
    pol = Total(pol_pack, True)
    enc_grad = pol.step(enc_grad)
    pre_grad, grad_b1, parts_w2 = mlp_back_a(core, enc_grad, pre_act, w2, rows, split_out, deps=[pol.val])
    sum_2 = Scatter(parts_w2, both_orders)
    pre_grad, enc_got = gate(pre_grad, enc_got)
    pre_grad = pol.step(pre_grad)
    parts_w1 = weight_grad(core, normed_mid, pre_grad, rows, split_out, 512, deps=[pol.val], scale=COVER)
    sum_1 = Scatter(parts_w1, both_orders)
    pre_grad, kept = gate(pre_grad, parts_w1[0])
    pre_grad = sum_2.step(pre_grad)
    normed_mid_grad = mlp_input_grad(pre_grad, w1, deps=[kept])
    normed_mid_grad = sum_1.step(normed_mid_grad)
    mid_grad = enc_grad + norm_back(normed_mid_grad, unit_mid, inverse_mid, ln2_gain)
    ctx_grad, parts_a = out_back(core, mid_grad, wo, ctx, rows, split_out)
    ctx_grad = sum_2.step(ctx_grad)
    dqkv_oth = attend_back(qkv[1], ctx_grad, 1, segs)
    dqkv_oth = sum_1.step(dqkv_oth)
    dqkv_own = attend_back(qkv[0], ctx_grad, 0, segs, deps=[dqkv_oth])
    dqkv_own = sum_2.step(dqkv_own)
    merge = functools.partial(weight_grad, core, normed_in, rows=rows, split_out=split_out, block=local_dim, cols=8 * local_dim)
    parts_a = merge(grad=dqkv_oth, into=parts_a, first=5, deps=[dqkv_own])
    dqkv_own, *parts_a = gate(dqkv_own, *parts_a)
    dqkv_own = pol.step(dqkv_own)
    parts_a = merge(grad=dqkv_own, into=parts_a, first=1)
    sum_a = Scatter(parts_a, both_orders)
    dqkv_own, kept = gate(dqkv_own, parts_a[0])
    dqkv_own = sum_2.step(dqkv_own)
    dqkv = [dqkv_own, dqkv_oth]
    normed_in_grad = qkv_input_grad(dqkv, wq, deps=[kept])
    normed_in_grad = sum_a.step(normed_in_grad)
    normed_in_grad = sum_1.step(normed_in_grad)
    actions_part, normed_in_grad = gate(actions_part, normed_in_grad)
    actions = actions_part + across(actions_part)
    patches_grad = mid_grad + norm_back(normed_in_grad, unit_in, inverse_in, ln1_gain)
    pg_got = across(patches_grad)

    def token_sum(val):
        return jnp.sum(val, axis=0)

    common = jnp.concatenate(
        [
            token_sum(normed_in_grad * unit_in),
            token_sum(normed_in_grad),
            token_sum(mid_grad),
            token_sum(normed_mid_grad * unit_mid),
            token_sum(normed_mid_grad),
            token_sum(enc_grad),
        ]
    )
    halves = [
        jnp.concatenate([token_sum(dqkv[i][0]), token_sum(dqkv[i][2]), grad_b1[0, i * local_ff : (i + 1) * local_ff]])
        for i in range(2)
    ]
    vec_got = across(jnp.concatenate([common, halves[1]]))
    tied = pol.step(patches_grad)
    tied = sum_2.hold(tied)
    tied = sum_a.step(tied)
    tied, vec_got = gate(tied, vec_got)
    small = Total(jnp.concatenate([common, halves[0]]) + vec_got, False)
    small.plan.remove("x")
    tied = small.step(tied)
    tied = sum_1.step(tied)
    tied, pg_got = gate(tied, pg_got)
    tied = sum_a.step(tied)
    tied = small.step(tied)
    tied = sum_1.hold(tied)
    tied = pol.step(tied)
    tied = sum_a.step(tied)
    patches_grad = small.step(tied)
    vec = small.result()
    summed_w2, summed_w1, summed_attn, pol_sum = sum_2.result(), sum_1.result(), sum_a.result(), pol.result()
    common, halves = vec[: 6 * dim].reshape(6, dim), vec[6 * dim :]

    def assemble(own, got):
        left = jnp.where(side == 0, own, got)
        right = jnp.where(side == 0, got, own)
        overlap = toks - low
        inside = low + jnp.arange(overlap, dtype=jnp.int32)
        return jnp.concatenate(
            [left[:low], jnp.where((inside < cut)[:, None], left[low:], right[:overlap]), right[overlap:]]
        )

    width = pol_image.shape[0]
    tail = pol_sum[width + 16 :]
    return (
        assemble(enc, enc_got),
        actions,
        assemble(patches_grad, pg_got),
        common[0],
        common[1],
        summed_attn[:, local_dim:].reshape(rows, 3, local_dim),
        halves[: 2 * local_dim].reshape(2, local_dim),
        summed_attn[:, :local_dim].T,
        common[2],
        common[3],
        common[4],
        summed_w1,
        halves[2 * local_dim :],
        summed_w2.T,
        common[5],
        pol_sum[:width],
        pol_sum[width : width + proprio.shape[1]],
        tail[:, :hid],
        tail[:hid, hid : hid + pol_third.shape[1]],
        tail[hid : hid + pol_action.shape[0], hid : hid + pol_action.shape[1]],
    )


def solution(mesh):
    return jax.shard_map(
        functools.partial(per_device, mesh.shape["dp"]),
        mesh=mesh,
        in_specs=(
            P("dp", None),
            P("dp", None),
            P("dp", None),
            P(),
            P(),
            P(None, None, "tensor"),
            P(None, "tensor"),
            P("tensor", None),
            P(),
            P(),
            P(),
            P(None, "tensor"),
            P("tensor"),
            P("tensor", None),
            P(),
            P(),
            P(),
            P(),
            P(),
            P(),
            P("dp", None),
            P("dp", None),
        ),
        out_specs=(
            P("dp", None),
            P("dp", None),
            P("dp", None),
            P(),
            P(),
            P("dp", None, "tensor"),
            P(None, "tensor"),
            P("tensor", "dp"),
            P(),
            P(),
            P(),
            P("dp", "tensor"),
            P("tensor"),
            P("tensor", "dp"),
            P(),
            P(),
            P(),
            P(),
            P(),
            P(),
        ),
        check_vma=False,
    )
```

```python
import functools
import math

import jax
import jax.numpy as jnp
from jax import lax
from jax.experimental import pallas as pl
from jax.experimental.pallas import tpu as pltpu
from jax.sharding import PartitionSpec as P

HEAD_DIM = 64
MOST = 50
LANES = 128
TILE = 128
SPAN = 256
SCALE = 0.02
COVER = 20.0

highest = lax.Precision.HIGHEST
norm_eps = 1e-06
f32 = jnp.float32
bf16 = jnp.bfloat16

NN = (((1,), (0,)), ((), ()))
NT = (((1,), (1,)), ((), ()))
TN = (((0,), (0,)), ((), ()))


def split(val):
    high = val.astype(bf16)
    return high, (val - high.astype(f32)).astype(bf16)


def mul(left, right, dims):
    return lax.dot_general(left, right, dims, preferred_element_type=f32)


def mul3(left, right, dims):
    (lh, ll), (rh, rl) = left, right
    return mul(lh, rh, dims) + (mul(lh, rl, dims) + mul(ll, rh, dims))


def dense(left, right):
    return jnp.dot(left, right, precision=highest)


def norm_stats(inputs):
    centred = inputs - jnp.mean(inputs, axis=-1, keepdims=True)
    inverse = lax.rsqrt(jnp.mean(centred * centred, axis=-1, keepdims=True) + norm_eps)
    return centred * inverse, inverse


def norm_back(upstream, unit_val, inverse, gain):
    scaled = upstream * gain
    centred = scaled - jnp.mean(scaled, axis=-1, keepdims=True)
    return inverse * (centred - unit_val * jnp.mean(scaled * unit_val, axis=-1, keepdims=True))


def elu_back(upstream, pre_act):
    return upstream * jnp.where(pre_act > 0, 1.0, jnp.exp(jnp.minimum(pre_act, 0.0)))


def params(limit_mib=56):
    return pltpu.CompilerParams(vmem_limit_bytes=limit_mib << 20)


def cost(flops, nbytes, trans=0, scale=SCALE):
    return pl.CostEstimate(flops=int(flops * scale), bytes_accessed=int(nbytes * scale), transcendentals=int(trans * scale))


def shape(*dims):
    return jax.ShapeDtypeStruct(dims, f32)


def whole(*dims):
    zeros = (0,) * len(dims)
    return pl.BlockSpec(dims, lambda *_: zeros)


def untouched(deps):
    return [pl.BlockSpec(memory_space=pl.ANY)] * len(deps)


def leaving_out(kernel, first, deps):
    return lambda *refs: kernel(*refs[:first], *refs[first + len(deps) :])


def join_kernel(where_ref, *refs):
    out_ref = refs[-1]
    for i, ref in enumerate(refs[:-1]):
        out_ref[pl.ds(where_ref[i], 1)] = ref[...][None]


def join_pieces(where, pieces):
    rows, cols = pieces[0].shape
    count = len(pieces)
    steps = next(n for n in (4, 3, 2, 1) if rows % (8 * n) == 0)
    part = rows // steps
    out = pl.pallas_call(
        join_kernel,
        out_shape=shape(count, rows, cols),
        grid_spec=pltpu.PrefetchScalarGridSpec(
            num_scalar_prefetch=1,
            grid=(steps,),
            in_specs=[pl.BlockSpec((part, cols), lambda i, w: (i, 0))] * count,
            out_specs=pl.BlockSpec((count, part, cols), lambda i, w: (0, i, 0)),
        ),
        compiler_params=params(),
        cost_estimate=cost(0, 8 * count * rows * cols),
        name="join_pieces",
    )(where, *pieces)
    return out.reshape(count * rows, cols)


def store_rows(core_ref, tile, keep_ref, send_ref, lanes, block):
    if send_ref is None:
        keep_ref[:, lanes] = tile
        return
    pairs = tile.shape[0] // (2 * block)

    def put(first, second):
        for i in range(pairs):
            low = 2 * i * block
            first[i, :, lanes] = tile[low : low + block]
            second[i, :, lanes] = tile[low + block : low + 2 * block]

    @pl.when(core_ref[0] == 0)
    def _():
        put(keep_ref, send_ref)

    @pl.when(core_ref[0] != 0)
    def _():
        put(send_ref, keep_ref)


def qkv_kernel(x_ref, w_ref, b_ref, out_ref, xh_ref, xl_ref):
    @pl.when(pl.program_id(0) == 0)
    def _():
        xh_ref[...], xl_ref[...] = split(x_ref[...])

    out_ref[...] = mul3((xh_ref[...], xl_ref[...]), split(w_ref[0]), NN) + b_ref[...]


def qkv_forward(normed, weight, bias, deps=()):
    toks, dim = normed.shape
    width = weight.shape[2]
    return pl.pallas_call(
        leaving_out(qkv_kernel, 3, deps),
        out_shape=shape(toks, 3 * width),
        grid=(3,),
        in_specs=[
            whole(toks, dim),
            pl.BlockSpec((1, dim, width), lambda c: (c, 0, 0)),
            pl.BlockSpec((1, width), lambda c: (0, c)),
        ]
        + untouched(deps),
        out_specs=pl.BlockSpec((toks, width), lambda c: (0, c)),
        scratch_shapes=[pltpu.VMEM((toks, dim), bf16)] * 2,
        compiler_params=params(),
        cost_estimate=cost(18 * toks * dim * width, 4 * (toks * dim + 3 * width * (dim + toks))),
        name="qkv_forward",
    )(normed, weight, bias, *deps)


def starts_of(toks):
    return [min(max(t * TILE - (SPAN - TILE) // 2, 0), toks - SPAN) for t in range(toks // TILE)]


def both_heads(val):
    lane = lax.broadcasted_iota(jnp.int32, val.shape, 1)
    return jnp.concatenate([jnp.where(lane < HEAD_DIM, val, 0.0), jnp.where(lane >= HEAD_DIM, val, 0.0)])


def one_head_each(val):
    rows = val.shape[0] // 2
    lane = lax.broadcasted_iota(jnp.int32, (rows, LANES), 1)
    return jnp.where(lane < HEAD_DIM, val[:rows], val[rows:])


def mul_deep(left, right):
    (lh, ll), (rh, rl) = left, right
    return mul(jnp.concatenate([lh, ll], 1), jnp.concatenate([rh, rh], 1), NT) + mul(lh, rl, NT)


def mul_wide(left, right, dims):
    (lh, ll), (rh, rl) = left, right
    cols = rh.shape[1]
    both = mul(lh, jnp.concatenate([rh, rl], 1), dims)
    return both[:, :cols] + (both[:, cols:] + mul(ll, rh, dims))


def probs_of(scores, same, axis):
    scores = jnp.where(same, scores, -1e30)
    exponent = jnp.exp(scores - jnp.max(scores, axis=axis, keepdims=True))
    return exponent * (1.0 / jnp.sum(exponent, axis=axis, keepdims=True))


def attend_kernel(q_ref, k_ref, v_ref, col_ref, win_ref, out_ref):
    toks = q_ref.shape[0]
    scale = 1.0 / math.sqrt(HEAD_DIM)
    for t, start in enumerate(starts_of(toks)):
        rows, keys = pl.ds(t * TILE, TILE), pl.ds(start, SPAN)
        same = col_ref[rows, :] == win_ref[t]
        scores = mul_deep(split(both_heads(q_ref[rows, :] * scale)), split(k_ref[keys, :]))
        probs = probs_of(scores, jnp.concatenate([same, same]), 1)
        out_ref[rows, :] = one_head_each(mul_wide(split(probs), split(v_ref[keys, :]), NN))


def pair_specs(toks, pairs, parts):
    return [
        pl.BlockSpec((toks, LANES), functools.partial(lambda part, i: (0, part * pairs + i), part))
        for part in range(parts)
    ]


def attend(qkv, segs, deps=()):
    toks, width = qkv.shape[0], qkv.shape[1] // 3
    pairs = width // LANES
    seg_col, seg_win, _ = segs
    return pl.pallas_call(
        leaving_out(attend_kernel, 5, deps),
        out_shape=shape(toks, width),
        grid=(pairs,),
        in_specs=pair_specs(toks, pairs, 3) + [whole(*seg_col.shape), whole(*seg_win.shape)] + untouched(deps),
        out_specs=pl.BlockSpec((toks, LANES), lambda i: (0, i)),
        compiler_params=params(),
        cost_estimate=cost(24 * toks * SPAN * width, 16 * toks * width, toks * SPAN * width // 64),
        name="attend",
    )(qkv, qkv, qkv, seg_col, seg_win, *deps)


def attend_back_kernel(q_ref, k_ref, v_ref, do_ref, col_ref, row_ref, out_ref):
    toks = q_ref.shape[0]
    scale = 1.0 / math.sqrt(HEAD_DIM)
    out_ref[1:] = jnp.zeros_like(out_ref[1:])
    for t, start in enumerate(starts_of(toks)):
        rows, keys = pl.ds(t * TILE, TILE), pl.ds(start, SPAN)
        same = col_ref[keys, :] == row_ref[t]
        q_pair, g_pair = split(both_heads(q_ref[rows, :] * scale)), split(both_heads(do_ref[rows, :]))
        k_pair, v_pair = split(k_ref[keys, :]), split(v_ref[keys, :])
        probs = probs_of(mul_deep(k_pair, q_pair), same, 0)
        dprobs = mul_deep(v_pair, g_pair)
        dscores = split(probs * (dprobs - jnp.sum(probs * dprobs, axis=0, keepdims=True)))
        out_ref[0, rows, :] = one_head_each(mul_wide(dscores, k_pair, TN)) * scale
        out_ref[1, keys, :] += mul_wide(dscores, q_pair, NN)
        out_ref[2, keys, :] += mul_wide(split(probs), g_pair, NN)


def attend_back(qkv, grad, half, segs, deps=()):
    toks, width = qkv.shape[0], qkv.shape[1] // 3
    pairs = width // LANES
    seg_col, _, seg_row = segs
    return pl.pallas_call(
        leaving_out(attend_back_kernel, 6, deps),
        out_shape=shape(3, toks, width),
        grid=(pairs,),
        in_specs=pair_specs(toks, pairs, 3)
        + [
            pl.BlockSpec((toks, LANES), lambda i: (0, half * pairs + i)),
            whole(*seg_col.shape),
            whole(*seg_row.shape),
        ]
        + untouched(deps),
        out_specs=pl.BlockSpec((3, toks, LANES), lambda i: (0, 0, i)),
        compiler_params=params(),
        cost_estimate=cost(60 * toks * SPAN * width, 28 * toks * width, toks * SPAN * width // 64),
        name="attend_back",
    )(qkv, qkv, qkv, grad, seg_col, seg_row, *deps)


def cdf_of(pre):
    return 0.5 * (1.0 + lax.erf(pre * (1.0 / math.sqrt(2.0))))


def mlp_kernel(x_ref, b_ref, w1_ref, w2_ref, acc_ref, pre_ref, y_ref, xh_ref, xl_ref):
    @pl.when(pl.program_id(0) == 0)
    def _():
        xh_ref[...], xl_ref[...] = split(x_ref[...])
        y_ref[...] = acc_ref[...]

    pre = mul3((xh_ref[...], xl_ref[...]), split(w1_ref[...]), NN) + b_ref[...]
    pre_ref[...] = pre
    y_ref[...] += mul3(split(pre * cdf_of(pre)), split(w2_ref[...]), NN)


def mlp_forward(normed, bias, w1, w2, acc, deps=(), block=512):
    toks, dim = normed.shape
    hidden = w1.shape[1]
    return pl.pallas_call(
        leaving_out(mlp_kernel, 5, deps),
        out_shape=(shape(toks, hidden), shape(toks, dim)),
        grid=(hidden // block,),
        in_specs=[
            whole(toks, dim),
            pl.BlockSpec((1, block), lambda j: (0, j)),
            pl.BlockSpec((dim, block), lambda j: (0, j)),
            pl.BlockSpec((block, dim), lambda j: (j, 0)),
            whole(toks, dim),
        ]
        + untouched(deps),
        out_specs=(pl.BlockSpec((toks, block), lambda j: (0, j)), whole(toks, dim)),
        scratch_shapes=[pltpu.VMEM((toks, dim), bf16)] * 2,
        compiler_params=params(),
        cost_estimate=cost(12 * toks * dim * hidden, 8 * dim * hidden + 4 * toks * (hidden + 2 * dim), toks * hidden),
        name="mlp_forward",
    )(normed, bias, w1, w2, acc, *deps)


def own_then_other(half):
    return (lambda j: jnp.minimum(j, half - 1)), (lambda j: jnp.maximum(j - half, 0))


def fill_transposed(src_ref, high_ref, low_ref):
    high_ref[...], low_ref[...] = split(jnp.transpose(src_ref[...]))


def mlp_back_a_kernel(half, block, split_out, core_ref, eg_ref, prea_ref, preb_ref, w2a_ref, w2b_ref, *refs):
    j = pl.program_id(0)
    pg_ref, b1_ref, keep_ref = refs[:3]
    send_ref = refs[3] if split_out else None
    eh_ref, el_ref, th_ref, tl_ref = refs[-4:]

    @pl.when(j == 0)
    def _():
        eh_ref[...], el_ref[...] = split(eg_ref[...])
        fill_transposed(eg_ref, th_ref, tl_ref)

    def step(pre_ref, w2_ref):
        pre = pre_ref[...]
        cdf = cdf_of(pre)
        pdf = jnp.exp(-0.5 * pre * pre) * (1.0 / math.sqrt(2.0 * math.pi))
        pg = mul3((eh_ref[...], el_ref[...]), split(w2_ref[...]), NT) * (cdf + pre * pdf)
        pg_ref[...] = pg
        b1_ref[...] = jnp.sum(pg, axis=0, keepdims=True)
        tile = mul3((th_ref[...], tl_ref[...]), split(pre * cdf), NN)
        store_rows(core_ref, tile, keep_ref, send_ref, slice(None), block)

    @pl.when(j < half)
    def _():
        step(prea_ref, w2a_ref)

    @pl.when(j >= half)
    def _():
        step(preb_ref, w2b_ref)


def grad_shapes(dim, cols, block, split_out):
    if split_out:
        return [shape(dim // (2 * block), block, cols)] * 2
    return [shape(dim, cols)]


def grad_specs(dim, cols, block, split_out):
    if split_out:
        return [pl.BlockSpec((dim // (2 * block), block, cols), lambda j, *_: (0, 0, j))] * 2
    return [pl.BlockSpec((dim, cols), lambda j, *_: (0, j))]


def mlp_back_a(core, enc_grad, pre, w2, rows, split_out, deps=(), block=512):
    toks, dim = enc_grad.shape
    hidden = 2 * pre[0].shape[1]
    half = hidden // 2 // block
    low, high = own_then_other(half)
    out = pl.pallas_call(
        leaving_out(functools.partial(mlp_back_a_kernel, half, rows, split_out), 6, deps),
        out_shape=[shape(toks, hidden), shape(1, hidden)] + grad_shapes(dim, hidden, rows, split_out),
        grid_spec=pltpu.PrefetchScalarGridSpec(
            num_scalar_prefetch=1,
            grid=(2 * half,),
            in_specs=[
                whole(toks, dim),
                pl.BlockSpec((toks, block), lambda j, _: (0, low(j))),
                pl.BlockSpec((toks, block), lambda j, _: (0, high(j))),
                pl.BlockSpec((block, dim), lambda j, _: (low(j), 0)),
                pl.BlockSpec((block, dim), lambda j, _: (high(j), 0)),
            ]
            + untouched(deps),
            out_specs=[
                pl.BlockSpec((toks, block), lambda j, _: (0, j)),
                pl.BlockSpec((1, block), lambda j, _: (0, j)),
            ]
            + grad_specs(dim, block, rows, split_out),
            scratch_shapes=[pltpu.VMEM((toks, dim), bf16)] * 2 + [pltpu.VMEM((dim, toks), bf16)] * 2,
        ),
        compiler_params=params(),
        cost_estimate=cost(12 * toks * dim * hidden, 8 * dim * hidden + 8 * toks * hidden, 2 * toks * hidden),
        name="mlp_back_a",
    )(core, enc_grad, *pre, *w2, *deps)
    return out[0], out[1], out[2:]


def mlp_input_kernel(half, pg_ref, wa_ref, wb_ref, dx_ref):
    j = pl.program_id(0)

    @pl.when(j == 0)
    def _():
        dx_ref[...] = jnp.zeros_like(dx_ref)

    @pl.when(j < half)
    def _():
        dx_ref[...] += mul3(split(pg_ref[...]), split(wa_ref[...]), NT)

    @pl.when(j >= half)
    def _():
        dx_ref[...] += mul3(split(pg_ref[...]), split(wb_ref[...]), NT)


def mlp_input_grad(pre_grad, w1, deps=(), block=768):
    toks, hidden = pre_grad.shape
    dim = w1[0].shape[0]
    half = hidden // 2 // block
    low, high = own_then_other(half)
    return pl.pallas_call(
        leaving_out(functools.partial(mlp_input_kernel, half), 3, deps),
        out_shape=shape(toks, dim),
        grid=(2 * half,),
        in_specs=[
            pl.BlockSpec((toks, block), lambda j: (0, j)),
            pl.BlockSpec((dim, block), lambda j: (0, low(j))),
            pl.BlockSpec((dim, block), lambda j: (0, high(j))),
        ]
        + untouched(deps),
        out_specs=whole(toks, dim),
        compiler_params=params(),
        cost_estimate=cost(6 * toks * dim * hidden, 4 * dim * hidden + 4 * toks * hidden, scale=COVER),
        name="mlp_input_grad",
    )(pre_grad, *w1, *deps)


def weight_grad_kernel(rows, split_out, core_ref, x_ref, g_ref, *refs):
    th_ref, tl_ref = refs[-2:]
    outs = refs[-4:-2] if split_out else (refs[-3], None)

    @pl.when(pl.program_id(0) == 0)
    def _():
        fill_transposed(x_ref, th_ref, tl_ref)

    grad = g_ref[0] if len(g_ref.shape) == 3 else g_ref[...]
    tile = mul3((th_ref[...], tl_ref[...]), split(grad), NN)
    store_rows(core_ref, tile, *outs, slice(None), rows)


def weight_grad(core, inputs, grad, rows, split_out, block, into=(), first=0, cols=None, deps=(), scale=SCALE):
    toks, dim = inputs.shape
    planes = grad.ndim == 3
    steps = grad.shape[0] if planes else grad.shape[1] // block
    width = steps * block
    cols = cols or width
    g_spec = (
        pl.BlockSpec((1, toks, block), lambda j, _: (j, 0, 0)) if planes else pl.BlockSpec((toks, block), lambda j, _: (0, j))
    )
    shapes = grad_shapes(dim, cols, rows, split_out)
    if split_out:
        out_spec = pl.BlockSpec((dim // (2 * rows), rows, block), lambda j, _: (0, 0, j + first))
    else:
        out_spec = pl.BlockSpec((dim, block), lambda j, _: (0, j + first))
    return pl.pallas_call(
        functools.partial(weight_grad_kernel, rows, split_out),
        out_shape=shapes,
        grid_spec=pltpu.PrefetchScalarGridSpec(
            num_scalar_prefetch=1,
            grid=(steps,),
            in_specs=[whole(toks, dim), g_spec] + untouched(into) + untouched(deps),
            out_specs=[out_spec] * len(shapes),
            scratch_shapes=[pltpu.VMEM((dim, toks), bf16)] * 2,
        ),
        input_output_aliases={3 + i: i for i in range(len(into))},
        compiler_params=params(),
        cost_estimate=cost(6 * toks * dim * width, 4 * (toks * dim + dim * width + toks * width), scale=scale),
        name="weight_grad",
    )(core, inputs, grad, *into, *deps)


def out_back_kernel(rows, split_out, core_ref, g_ref, wa_ref, wb_ref, ca_ref, cb_ref, *refs):
    j = pl.program_id(0)
    dc_ref, keep_ref = refs[:2]
    send_ref = refs[2] if split_out else None
    gh_ref, gl_ref, th_ref, tl_ref = refs[-4:]

    @pl.when(j == 0)
    def _():
        gh_ref[...], gl_ref[...] = split(g_ref[...])
        fill_transposed(g_ref, th_ref, tl_ref)

    def step(w_ref, c_ref):
        dc_ref[...] = mul3((gh_ref[...], gl_ref[...]), split(w_ref[...]), NT)
        tile = mul3((th_ref[...], tl_ref[...]), split(c_ref[...]), NN)
        store_rows(core_ref, tile, keep_ref, send_ref, slice(None), rows)

    @pl.when(j == 0)
    def _():
        step(wa_ref, ca_ref)

    @pl.when(j == 1)
    def _():
        step(wb_ref, cb_ref)


def out_back(core, mid_grad, weights, ctx, rows, split_out, deps=()):
    toks, dim = mid_grad.shape
    width = ctx[0].shape[1]
    cols = 8 * width
    shapes = grad_shapes(dim, cols, rows, split_out)
    if split_out:
        spec = pl.BlockSpec((dim // (2 * rows), rows, width), lambda j, _: (0, 0, 4 * j))
    else:
        spec = pl.BlockSpec((dim, width), lambda j, _: (0, 4 * j))
    out = pl.pallas_call(
        leaving_out(functools.partial(out_back_kernel, rows, split_out), 6, deps),
        out_shape=[shape(toks, 2 * width)] + shapes,
        grid_spec=pltpu.PrefetchScalarGridSpec(
            num_scalar_prefetch=1,
            grid=(2,),
            in_specs=[whole(toks, dim)] + [whole(width, dim)] * 2 + [whole(toks, width)] * 2 + untouched(deps),
            out_specs=[pl.BlockSpec((toks, width), lambda j, _: (0, j))] + [spec] * len(shapes),
            scratch_shapes=[pltpu.VMEM((toks, dim), bf16)] * 2 + [pltpu.VMEM((dim, toks), bf16)] * 2,
        ),
        compiler_params=params(),
        cost_estimate=cost(24 * toks * dim * width, 4 * (toks * dim + 4 * dim * width + 4 * toks * width)),
        name="out_back",
    )(core, mid_grad, *weights, *ctx, *deps)
    return out[0], out[1:]


def qkv_input_kernel(ga_ref, gb_ref, wa_ref, wb_ref, dx_ref):
    @pl.when(pl.program_id(0) == 0)
    def _():
        dx_ref[...] = jnp.zeros_like(dx_ref)

    for g_ref, w_ref in ((ga_ref, wa_ref), (gb_ref, wb_ref)):
        dx_ref[...] += mul3(split(g_ref[0]), split(w_ref[0]), NT)


def qkv_input_grad(grads, weights, deps=()):
    toks = grads[0].shape[1]
    _, dim, width = weights[0].shape
    grad_spec = pl.BlockSpec((1, toks, width), lambda c: (c, 0, 0))
    w_spec = pl.BlockSpec((1, dim, width), lambda c: (c, 0, 0))
    return pl.pallas_call(
        leaving_out(qkv_input_kernel, 4, deps),
        out_shape=shape(toks, dim),
        grid=(3,),
        in_specs=[grad_spec, grad_spec, w_spec, w_spec] + untouched(deps),
        out_specs=whole(toks, dim),
        compiler_params=params(),
        cost_estimate=cost(36 * toks * dim * width, 4 * (toks * dim + 6 * dim * width + 6 * toks * width), scale=COVER),
        name="qkv_input_grad",
    )(*grads, *weights, *deps)


def norm_back_kernel(up_ref, unit_ref, inverse_ref, gain_ref, base_ref, out_ref, sums_ref):
    @pl.when(pl.program_id(0) == 0)
    def _():
        sums_ref[...] = jnp.zeros_like(sums_ref)

    upstream, unit_val, base = up_ref[...], unit_ref[...], base_ref[...]
    out_ref[...] = base + norm_back(upstream, unit_val, inverse_ref[...], gain_ref[...])
    for i, val in enumerate((upstream * unit_val, upstream, base)):
        sums_ref[i : i + 1, :] += jnp.sum(val, axis=0, keepdims=True)


def norm_back_sums(upstream, unit_val, inverse, gain, base, steps=4):
    toks, dim = upstream.shape
    block = pl.BlockSpec((toks // steps, dim), lambda i: (i, 0))
    out, sums = pl.pallas_call(
        norm_back_kernel,
        out_shape=(shape(toks, dim), shape(8, dim)),
        grid=(steps,),
        in_specs=[block, block, pl.BlockSpec((toks // steps, 1), lambda i: (i, 0)), whole(1, dim), block],
        out_specs=(block, whole(8, dim)),
        compiler_params=params(),
        cost_estimate=cost(20 * toks * dim, 16 * toks * dim),
        name="norm_back",
    )(upstream, unit_val, inverse, gain[None], base)
    return out, sums[:3].reshape(-1)


def per_device(
    n_dp,
    patches,
    segment_ids,
    proprio,
    ln1_gain,
    ln1_bias,
    qkv_weight,
    qv_bias,
    out_weight,
    out_bias,
    ln2_gain,
    ln2_bias,
    fc1_weight,
    fc1_bias,
    fc2_weight,
    fc2_bias,
    pol_image,
    pol_proprio,
    pol_hidden,
    pol_third,
    pol_action,
    out_cotangent,
    action_cotangent,
):
    row_len, dim = patches.shape
    images = proprio.shape[0]
    local_dim = qkv_weight.shape[2]
    local_ff = fc1_weight.shape[1]
    toks = -(-(row_len // 2 + MOST // 2) // TILE) * TILE
    low = row_len - toks
    rows = dim // n_dp
    split_out = rows % 8 == 0

    mine = lax.axis_index("dp")
    side = lax.axis_index("tensor")
    bit_c, bit_y, bit_z, bits_h = mine & 1, (mine >> 1) & 1, (mine >> 2) & 1, mine >> 3
    core = jnp.reshape(bit_c, (1,)).astype(jnp.int32)

    def across(val):
        return lax.ppermute(val, "tensor", [(0, 1), (1, 0)])

    def swap(val, bit):
        return lax.ppermute(val, "dp", [(i, i ^ (1 << bit)) for i in range(n_dp)])

    def pick(val, index, axis):
        return lax.dynamic_index_in_dim(val, index, axis, keepdims=False)

    def gate(*vals):
        return lax.optimization_barrier(vals)

    def slices(weight):
        piece = weight.shape[0] // 8
        return [
            lax.dynamic_slice_in_dim(weight, index * piece, piece, 0)
            for index in (2 * bit_y + bit_c, 4 + 2 * bit_z + bit_c)
        ]

    def joined(pieces, others):
        place = []
        for c in (bit_c, 1 - bit_c):
            place += [2 * bit_y + c, 4 + 2 * bit_z + c, 2 * (1 - bit_y) + c, 4 + 2 * (1 - bit_z) + c]
        return join_pieces(jnp.stack(place).astype(jnp.int32), pieces + others)

    bias_pack = jnp.concatenate([qv_bias.reshape(-1), fc1_bias])
    wq_own = jnp.transpose(qkv_weight, (1, 0, 2))

    seg = segment_ids[0]
    pos = jnp.arange(row_len, dtype=jnp.int32)
    first_tok = jnp.concatenate([jnp.ones((1,), bool), seg[1:] != seg[:-1]])
    cut = jnp.min(jnp.where(first_tok & (pos >= low), pos, row_len))
    start = side * low

    def window(val):
        return lax.dynamic_slice_in_dim(val, start, toks, 0)

    here = start + jnp.arange(toks, dtype=jnp.int32)
    owned = jnp.where(side == 0, here < cut, here >= cut)
    seg_here, first_here = window(seg), window(first_tok)
    seg_col = seg_here[:, None]
    seg_win = jnp.stack([seg_here[s : s + SPAN] for s in starts_of(toks)])[:, None, :]
    seg_tile = seg_here.reshape(-1, 1, TILE)
    segs = (seg_col, seg_win, jnp.concatenate([seg_tile, seg_tile], axis=2))
    cls_pick = (
        (seg_here[None, :] == jnp.arange(images, dtype=jnp.int32)[:, None]) & (first_here & owned)[None, :]
    ).astype(f32)
    mine_image = jnp.sum(cls_pick, axis=1, keepdims=True)

    bias_oth = across(bias_pack)
    sent_q = slices(wq_own.reshape(3 * dim, local_dim))
    got_q = [across(val) for val in sent_q]
    x_in = window(patches)
    unit_in, inverse_in = norm_stats(x_in)
    normed_in = unit_in * ln1_gain + ln1_bias

    def qkv_bias_of(flat):
        return jnp.concatenate([flat[:local_dim], jnp.zeros((local_dim,), f32), flat[local_dim : 2 * local_dim]])[None]

    qkv_own = qkv_forward(normed_in, wq_own, qkv_bias_of(bias_pack))
    qkv_own, bias_oth, *got_q = gate(qkv_own, bias_oth, *got_q)
    near_q = [swap(got_q[0], 1), swap(got_q[1], 2)]
    core_q = [swap(val, 0) for val in got_q]
    half = out_weight.shape[0] // 2
    wo_part = lax.dynamic_slice_in_dim(out_weight, bit_c * half, half, 0)
    wo_part, *sent_1 = gate(wo_part, *slices(fc1_weight), *got_q)[:3]
    got_o = across(wo_part)
    got_1 = [across(val) for val in sent_1]
    ctx_own = attend(qkv_own, segs, deps=[wo_part, *sent_1])
    ctx_own, *near_q = gate(ctx_own, *near_q)
    core_q += [swap(val, 0) for val in near_q]
    wq_oth = joined(list(got_q) + list(near_q), core_q).reshape(3, dim, local_dim)
    sent_2 = slices(fc2_weight)
    qkv_oth = qkv_forward(normed_in, wq_oth, qkv_bias_of(bias_oth), deps=[ctx_own, *sent_2])
    qkv_oth, got_o = gate(qkv_oth, got_o)
    core_o = swap(got_o, 0)
    ctx_oth = attend(qkv_oth, segs, deps=[got_o])
    ctx_oth, core_o, *got_1 = gate(ctx_oth, core_o, *got_1)
    wo_oth = join_pieces(jnp.stack([bit_c, 1 - bit_c]).astype(jnp.int32), [got_o, core_o])
    near_1 = [swap(got_1[0], 1), swap(got_1[1], 2)]
    core_1 = [swap(val, 0) for val in got_1]
    sent_2 = gate(*sent_2, *got_1)[:2]
    got_2 = [across(val) for val in sent_2]
    qkv, ctx, wo, wq = [qkv_own, qkv_oth], [ctx_own, ctx_oth], [out_weight, wo_oth], [wq_own, wq_oth]
    high = lax.Precision.HIGH
    attn = jnp.dot(ctx[0], wo[0], precision=high) + jnp.dot(ctx[1], wo[1], precision=high)
    mid = x_in + attn + out_bias
    unit_mid, inverse_mid = norm_stats(mid)
    normed_mid = unit_mid * ln2_gain + ln2_bias
    pre_own, mlp_out = mlp_forward(normed_mid, fc1_bias[None], fc1_weight, fc2_weight, mid + fc2_bias, deps=got_1)
    mlp_out, *moved = gate(mlp_out, *near_1, *core_1, *got_2)
    near_1, core_1, got_2 = moved[:2], moved[2:4], moved[4:]
    near_2 = [swap(got_2[0], 1), swap(got_2[1], 2)]
    core_1 += [swap(val, 0) for val in near_1]
    core_2 = [swap(val, 0) for val in got_2]
    w1_oth = joined(list(got_1) + list(near_1), core_1)
    w1_oth, *near_2 = gate(w1_oth, *near_2)
    core_2 += [swap(val, 0) for val in near_2]
    w2_oth = joined(list(got_2) + list(near_2), core_2)
    pre_oth, enc = mlp_forward(normed_mid, bias_oth[None, 2 * local_dim :], w1_oth, w2_oth, mlp_out)
    w1, w2, pre_act = (fc1_weight, w1_oth), (fc2_weight, w2_oth), (pre_own, pre_oth)
    enc_got = across(enc)

    cls_features = dense(cls_pick, enc)
    act_cot = action_cotangent * mine_image
    pre_one = dense(cls_features, pol_image) + dense(proprio, pol_proprio)
    hidden_one = jax.nn.elu(pre_one)
    pre_two = dense(hidden_one, pol_hidden)
    hidden_two = jax.nn.elu(pre_two)
    pre_three = dense(hidden_two, pol_third)
    hidden_three = jax.nn.elu(pre_three)
    actions_part = dense(hidden_three, pol_action) * mine_image
    grad_p4 = dense(hidden_three.T, act_cot)
    grad_three = elu_back(dense(act_cot, pol_action.T), pre_three)
    grad_p3 = dense(hidden_two.T, grad_three)
    grad_two = elu_back(dense(grad_three, pol_third.T), pre_two)
    grad_p2 = dense(hidden_one.T, grad_two)
    grad_one = elu_back(dense(grad_two, pol_hidden.T), pre_one)
    grad_pimage = dense(cls_features.T, grad_one)
    grad_pprop = dense(proprio.T, grad_one)
    cls_grad = dense(grad_one, pol_image.T)

    def share(val):
        return val[..., : val.shape[-1] // 2], val[..., val.shape[-1] // 2 :]

    class Chain:
        def __init__(self, terms, order, first, size):
            self.terms, self.moving, self.first, self.size = terms, None, first, size
            levels = 0
            while 8 << levels < n_dp:
                levels += 1
            self.plan = list(order) + ["x"] + list(range(3, 3 + levels))
            self.axis = {1: 2, 2: 1} if order[0] == 1 else {2: 1, 1: 1}

        def part(self, val, index, axis):
            at, sizes = [0] * val.ndim, list(val.shape)
            at[axis], sizes[axis] = index, 1
            at[-2], sizes[-2] = self.first, self.size
            return jnp.squeeze(lax.dynamic_slice(val, at, sizes), axis)

        def step(self, tied):
            if self.moving is not None:
                tied, got = gate(tied, self.moving)
                self.terms.append(got)
            what = self.plan.pop(0)
            if what == "x":
                out, kept = (sum(share(val)[i] for val in self.terms) for i in (1, 0))
                tied, out = gate(tied, out)
                self.terms, self.moving = [kept], across(out)
                return tied
            bit = (mine >> what) & 1
            axis = self.axis.get(what, 1)
            if what >= 3:
                self.terms = [val.reshape((val.shape[0] // 2, 2) + val.shape[1:]) for val in self.terms]
            out, kept = (sum(self.part(val, index, axis) for val in self.terms) for index in (1 - bit, bit))
            self.first = 0
            tied, out = gate(tied, out)
            self.terms, self.moving = [kept], swap(out, what)
            return tied

    class Scatter:
        def __init__(self, parts, orders):
            self.parts, self.orders, self.chains = parts, orders, []
            if split_out:
                self.got = swap(parts[1], 0)

        def step(self, tied):
            if not split_out:
                return tied
            if not self.chains:
                tied, self.got = gate(tied, self.got)
                piece = rows // len(self.orders)
                terms = [val.reshape((n_dp // 8, 2, 2) + val.shape[1:]) for val in (self.parts[0], self.got)]
                self.chains = [Chain(list(terms), order, i * piece, piece) for i, order in enumerate(self.orders)]
            for chain in self.chains:
                if chain.plan:
                    tied = chain.step(tied)
            return tied

        def hold(self, tied):
            for chain in self.chains:
                tied, chain.moving = gate(tied, chain.moving)
            return tied

        def result(self):
            if not split_out:
                own, oth = share(self.parts[0])
                return lax.psum_scatter(own + across(oth), "dp", scatter_dimension=0, tiled=True)
            while not self.chains or any(chain.plan for chain in self.chains):
                self.step(core)
            return jnp.concatenate([sum(val[0] for val in chain.terms + [chain.moving]) for chain in self.chains])

    class Total:
        def __init__(self, val, halve):
            self.halve = halve
            levels = 1
            while 2 << levels <= n_dp:
                levels += 1
            self.plan = list(range(1, levels)) + ["x"]
            if halve:
                pair = val.reshape((2, val.shape[0] // 2) + val.shape[1:])
                self.sent = pick(pair, 1 - bit_c, 0)
                self.val, self.moving = pick(pair, bit_c, 0), swap(self.sent, 0)
            else:
                self.val, self.moving = val, swap(val, 0)

        def step(self, tied):
            tied, got = gate(tied, self.moving)
            self.val = self.val + got
            if self.plan:
                what = self.plan.pop(0)
                self.moving = across(self.val) if what == "x" else swap(self.val, what)
            else:
                self.moving = None
            return gate(tied, self.val)[0]

        def result(self):
            while self.moving is not None:
                self.step(core)
            if not self.halve:
                return self.val
            got = swap(self.val, 0)
            first = jnp.where(bit_c == 0, self.val, got)
            return jnp.concatenate([first, jnp.where(bit_c == 0, got, self.val)])

    both_orders = [(1, 2), (2, 1)] if rows % 16 == 0 else [(1, 2)]
    pad = lambda val, h, w: jnp.pad(val, ((0, h - val.shape[0]), (0, w - val.shape[1])))
    hid = pol_hidden.shape[1]
    rest = jnp.concatenate([pad(grad_p3, hid, hid), pad(grad_p4, pol_hidden.shape[0] - hid, hid)], axis=0)
    pol_pack = jnp.concatenate([grad_pimage, pad(grad_pprop, 16, pol_image.shape[1]), jnp.concatenate([grad_p2, rest], axis=1)])
    enc_grad = jnp.where(owned[:, None], window(out_cotangent), 0.0) + lax.dot_general(
        cls_pick, cls_grad, TN, precision=highest
    )
    pol = Total(pol_pack, True)
    enc_grad = pol.step(enc_grad)
    pre_grad, grad_b1, parts_w2 = mlp_back_a(core, enc_grad, pre_act, w2, rows, split_out, deps=[pol.val])
    sum_2 = Scatter(parts_w2, both_orders)
    pre_grad, enc_got = gate(pre_grad, enc_got)
    pre_grad = pol.step(pre_grad)
    parts_w1 = weight_grad(core, normed_mid, pre_grad, rows, split_out, 512, deps=[pol.val], scale=COVER)
    sum_1 = Scatter(parts_w1, both_orders)
    pre_grad, kept = gate(pre_grad, parts_w1[0])
    pre_grad = sum_2.step(pre_grad)
    normed_mid_grad = mlp_input_grad(pre_grad, w1, deps=[kept])
    normed_mid_grad = sum_1.step(normed_mid_grad)
    mid_grad, sums_mid = norm_back_sums(normed_mid_grad, unit_mid, inverse_mid, ln2_gain, enc_grad)
    ctx_grad, parts_a = out_back(core, mid_grad, wo, ctx, rows, split_out)
    ctx_grad = sum_2.step(ctx_grad)
    dqkv_oth = attend_back(qkv[1], ctx_grad, 1, segs)
    dqkv_oth = sum_1.step(dqkv_oth)
    dqkv_own = attend_back(qkv[0], ctx_grad, 0, segs, deps=[dqkv_oth])
    dqkv_own = sum_2.step(dqkv_own)
    dqkv_own = sum_1.step(dqkv_own)
    merge = functools.partial(weight_grad, core, normed_in, rows=rows, split_out=split_out, block=local_dim, cols=8 * local_dim, scale=COVER)
    parts_a = merge(grad=dqkv_oth, into=parts_a, first=5, deps=[dqkv_own])
    dqkv_own, *parts_a = gate(dqkv_own, *parts_a)
    dqkv_own = pol.step(dqkv_own)
    parts_a = merge(grad=dqkv_own, into=parts_a, first=1)
    sum_a = Scatter(parts_a, both_orders)
    dqkv_own, kept = gate(dqkv_own, parts_a[0])
    dqkv_own = sum_2.step(dqkv_own)
    dqkv = [dqkv_own, dqkv_oth]
    normed_in_grad = qkv_input_grad(dqkv, wq, deps=[kept])
    normed_in_grad = sum_a.step(normed_in_grad)
    patches_grad, sums_in = norm_back_sums(normed_in_grad, unit_in, inverse_in, ln1_gain, mid_grad)

    def token_sum(val):
        return jnp.sum(val, axis=0)

    common = jnp.concatenate([sums_in, sums_mid])
    halves = [
        jnp.concatenate([token_sum(dqkv[i][0]), token_sum(dqkv[i][2]), grad_b1[0, i * local_ff : (i + 1) * local_ff]])
        for i in range(2)
    ]
    vec_got = across(jnp.concatenate([common, halves[1], actions_part.reshape(-1)]))
    patches_grad = sum_1.step(patches_grad)
    pg_got = across(patches_grad)
    tied = pol.step(patches_grad)
    tied = sum_2.hold(tied)
    tied = sum_a.step(tied)
    tied, vec_got = gate(tied, vec_got)
    vec = jnp.concatenate([common, halves[0]])
    small = Total(vec + vec_got[: vec.size], False)
    actions = actions_part + vec_got[vec.size :].reshape(actions_part.shape)
    small.plan.remove("x")
    tied = small.step(tied)
    tied = sum_a.step(tied)
    tied = small.step(tied)
    tied, pg_got = gate(tied, pg_got)
    tied = sum_1.hold(tied)
    tied = pol.step(tied)
    tied = sum_a.step(tied)
    patches_grad = small.step(tied)
    vec = small.result()
    summed_w2, summed_w1, summed_attn, pol_sum = sum_2.result(), sum_1.result(), sum_a.result(), pol.result()
    common, halves = vec[: 6 * dim].reshape(6, dim), vec[6 * dim :]

    def assemble(own, got):
        left = jnp.where(side == 0, own, got)
        right = jnp.where(side == 0, got, own)
        overlap = toks - low
        inside = low + jnp.arange(overlap, dtype=jnp.int32)
        return jnp.concatenate(
            [left[:low], jnp.where((inside < cut)[:, None], left[low:], right[:overlap]), right[overlap:]]
        )

    width = pol_image.shape[0]
    tail = pol_sum[width + 16 :]
    return (
        assemble(enc, enc_got),
        actions,
        assemble(patches_grad, pg_got),
        common[0],
        common[1],
        summed_attn[:, local_dim:].reshape(rows, 3, local_dim),
        halves[: 2 * local_dim].reshape(2, local_dim),
        summed_attn[:, :local_dim].T,
        common[2],
        common[3],
        common[4],
        summed_w1,
        halves[2 * local_dim :],
        summed_w2.T,
        common[5],
        pol_sum[:width],
        pol_sum[width : width + proprio.shape[1]],
        tail[:, :hid],
        tail[:hid, hid : hid + pol_third.shape[1]],
        tail[hid : hid + pol_action.shape[0], hid : hid + pol_action.shape[1]],
    )


def solution(mesh):
    return jax.shard_map(
        functools.partial(per_device, mesh.shape["dp"]),
        mesh=mesh,
        in_specs=(
            P("dp", None),
            P("dp", None),
            P("dp", None),
            P(),
            P(),
            P(None, None, "tensor"),
            P(None, "tensor"),
            P("tensor", None),
            P(),
            P(),
            P(),
            P(None, "tensor"),
            P("tensor"),
            P("tensor", None),
            P(),
            P(),
            P(),
            P(),
            P(),
            P(),
            P("dp", None),
            P("dp", None),
        ),
        out_specs=(
            P("dp", None),
            P("dp", None),
            P("dp", None),
            P(),
            P(),
            P("dp", None, "tensor"),
            P(None, "tensor"),
            P("tensor", "dp"),
            P(),
            P(),
            P(),
            P("dp", "tensor"),
            P("tensor"),
            P("tensor", "dp"),
            P(),
            P(),
            P(),
            P(),
            P(),
            P(),
        ),
        check_vma=False,
    )
```

```python
import functools
import math

import jax
import jax.numpy as jnp
from jax import lax
from jax.experimental import pallas as pl
from jax.experimental.pallas import tpu as pltpu
from jax.sharding import PartitionSpec as P

HEAD_DIM = 64
MOST = 50
LANES = 128
TILE = 128
SPAN = 256
SCALE = 0.02
COVER = 20.0

highest = lax.Precision.HIGHEST
norm_eps = 1e-06
f32 = jnp.float32
bf16 = jnp.bfloat16

NN = (((1,), (0,)), ((), ()))
NT = (((1,), (1,)), ((), ()))
TN = (((0,), (0,)), ((), ()))


def split(val):
    high = val.astype(bf16)
    return high, (val - high.astype(f32)).astype(bf16)


def mul(left, right, dims):
    return lax.dot_general(left, right, dims, preferred_element_type=f32)


def mul3(left, right, dims):
    (lh, ll), (rh, rl) = left, right
    return mul(lh, rh, dims) + (mul(lh, rl, dims) + mul(ll, rh, dims))


def dense(left, right):
    return jnp.dot(left, right, precision=highest)


def norm_stats(inputs):
    centred = inputs - jnp.mean(inputs, axis=-1, keepdims=True)
    inverse = lax.rsqrt(jnp.mean(centred * centred, axis=-1, keepdims=True) + norm_eps)
    return centred * inverse, inverse


def norm_back(upstream, unit_val, inverse, gain):
    scaled = upstream * gain
    centred = scaled - jnp.mean(scaled, axis=-1, keepdims=True)
    return inverse * (centred - unit_val * jnp.mean(scaled * unit_val, axis=-1, keepdims=True))


def elu_back(upstream, pre_act):
    return upstream * jnp.where(pre_act > 0, 1.0, jnp.exp(jnp.minimum(pre_act, 0.0)))


def params(limit_mib=56):
    return pltpu.CompilerParams(vmem_limit_bytes=limit_mib << 20)


def cost(flops, nbytes, trans=0, scale=SCALE):
    return pl.CostEstimate(flops=int(flops * scale), bytes_accessed=int(nbytes * scale), transcendentals=int(trans * scale))


def shape(*dims):
    return jax.ShapeDtypeStruct(dims, f32)


def whole(*dims):
    zeros = (0,) * len(dims)
    return pl.BlockSpec(dims, lambda *_: zeros)


def untouched(deps):
    return [pl.BlockSpec(memory_space=pl.ANY)] * len(deps)


def leaving_out(kernel, first, deps):
    return lambda *refs: kernel(*refs[:first], *refs[first + len(deps) :])


def join_kernel(where_ref, *refs):
    out_ref = refs[-1]
    for i, ref in enumerate(refs[:-1]):
        out_ref[pl.ds(where_ref[i], 1)] = ref[...][None]


def join_pieces(where, pieces):
    rows, cols = pieces[0].shape
    count = len(pieces)
    steps = next(n for n in (4, 3, 2, 1) if rows % (8 * n) == 0)
    part = rows // steps
    out = pl.pallas_call(
        join_kernel,
        out_shape=shape(count, rows, cols),
        grid_spec=pltpu.PrefetchScalarGridSpec(
            num_scalar_prefetch=1,
            grid=(steps,),
            in_specs=[pl.BlockSpec((part, cols), lambda i, w: (i, 0))] * count,
            out_specs=pl.BlockSpec((count, part, cols), lambda i, w: (0, i, 0)),
        ),
        compiler_params=params(),
        cost_estimate=cost(0, 8 * count * rows * cols),
        name="join_pieces",
    )(where, *pieces)
    return out.reshape(count * rows, cols)


def store_rows(core_ref, tile, keep_ref, send_ref, lanes, block):
    if send_ref is None:
        keep_ref[:, lanes] = tile
        return
    pairs = tile.shape[0] // (2 * block)

    def put(first, second):
        for i in range(pairs):
            low = 2 * i * block
            first[i, :, lanes] = tile[low : low + block]
            second[i, :, lanes] = tile[low + block : low + 2 * block]

    @pl.when(core_ref[0] == 0)
    def _():
        put(keep_ref, send_ref)

    @pl.when(core_ref[0] != 0)
    def _():
        put(send_ref, keep_ref)


def qkv_kernel(x_ref, w_ref, b_ref, out_ref, xh_ref, xl_ref):
    @pl.when(pl.program_id(0) == 0)
    def _():
        xh_ref[...], xl_ref[...] = split(x_ref[...])

    out_ref[...] = mul3((xh_ref[...], xl_ref[...]), split(w_ref[0]), NN) + b_ref[...]


def qkv_forward(normed, weight, bias, deps=()):
    toks, dim = normed.shape
    width = weight.shape[2]
    return pl.pallas_call(
        leaving_out(qkv_kernel, 3, deps),
        out_shape=shape(toks, 3 * width),
        grid=(3,),
        in_specs=[
            whole(toks, dim),
            pl.BlockSpec((1, dim, width), lambda c: (c, 0, 0)),
            pl.BlockSpec((1, width), lambda c: (0, c)),
        ]
        + untouched(deps),
        out_specs=pl.BlockSpec((toks, width), lambda c: (0, c)),
        scratch_shapes=[pltpu.VMEM((toks, dim), bf16)] * 2,
        compiler_params=params(),
        cost_estimate=cost(18 * toks * dim * width, 4 * (toks * dim + 3 * width * (dim + toks))),
        name="qkv_forward",
    )(normed, weight, bias, *deps)


def starts_of(toks):
    return [min(max(t * TILE - (SPAN - TILE) // 2, 0), toks - SPAN) for t in range(toks // TILE)]


def both_heads(val):
    lane = lax.broadcasted_iota(jnp.int32, val.shape, 1)
    return jnp.concatenate([jnp.where(lane < HEAD_DIM, val, 0.0), jnp.where(lane >= HEAD_DIM, val, 0.0)])


def one_head_each(val):
    rows = val.shape[0] // 2
    lane = lax.broadcasted_iota(jnp.int32, (rows, LANES), 1)
    return jnp.where(lane < HEAD_DIM, val[:rows], val[rows:])


def mul_deep(left, right):
    (lh, ll), (rh, rl) = left, right
    return mul(jnp.concatenate([lh, ll], 1), jnp.concatenate([rh, rh], 1), NT) + mul(lh, rl, NT)


def mul_wide(left, right, dims):
    (lh, ll), (rh, rl) = left, right
    cols = rh.shape[1]
    both = mul(lh, jnp.concatenate([rh, rl], 1), dims)
    return both[:, :cols] + (both[:, cols:] + mul(ll, rh, dims))


def probs_of(scores, same, axis):
    scores = jnp.where(same, scores, -1e30)
    exponent = jnp.exp(scores - jnp.max(scores, axis=axis, keepdims=True))
    return exponent * (1.0 / jnp.sum(exponent, axis=axis, keepdims=True))


def attend_kernel(q_ref, k_ref, v_ref, col_ref, win_ref, out_ref):
    toks = q_ref.shape[0]
    scale = 1.0 / math.sqrt(HEAD_DIM)
    for t, start in enumerate(starts_of(toks)):
        rows, keys = pl.ds(t * TILE, TILE), pl.ds(start, SPAN)
        same = col_ref[rows, :] == win_ref[t]
        scores = mul_deep(split(both_heads(q_ref[rows, :] * scale)), split(k_ref[keys, :]))
        probs = probs_of(scores, jnp.concatenate([same, same]), 1)
        out_ref[rows, :] = one_head_each(mul_wide(split(probs), split(v_ref[keys, :]), NN))


def pair_specs(toks, pairs, parts):
    return [
        pl.BlockSpec((toks, LANES), functools.partial(lambda part, i: (0, part * pairs + i), part))
        for part in range(parts)
    ]


def attend(qkv, segs, deps=()):
    toks, width = qkv.shape[0], qkv.shape[1] // 3
    pairs = width // LANES
    seg_col, seg_win, _ = segs
    return pl.pallas_call(
        leaving_out(attend_kernel, 5, deps),
        out_shape=shape(toks, width),
        grid=(pairs,),
        in_specs=pair_specs(toks, pairs, 3) + [whole(*seg_col.shape), whole(*seg_win.shape)] + untouched(deps),
        out_specs=pl.BlockSpec((toks, LANES), lambda i: (0, i)),
        compiler_params=params(),
        cost_estimate=cost(24 * toks * SPAN * width, 16 * toks * width, toks * SPAN * width // 64),
        name="attend",
    )(qkv, qkv, qkv, seg_col, seg_win, *deps)


def attend_back_kernel(q_ref, k_ref, v_ref, do_ref, col_ref, row_ref, out_ref):
    toks = q_ref.shape[0]
    scale = 1.0 / math.sqrt(HEAD_DIM)
    out_ref[1:] = jnp.zeros_like(out_ref[1:])
    for t, start in enumerate(starts_of(toks)):
        rows, keys = pl.ds(t * TILE, TILE), pl.ds(start, SPAN)
        same = col_ref[keys, :] == row_ref[t]
        q_pair, g_pair = split(both_heads(q_ref[rows, :] * scale)), split(both_heads(do_ref[rows, :]))
        k_pair, v_pair = split(k_ref[keys, :]), split(v_ref[keys, :])
        probs = probs_of(mul_deep(k_pair, q_pair), same, 0)
        dprobs = mul_deep(v_pair, g_pair)
        dscores = split(probs * (dprobs - jnp.sum(probs * dprobs, axis=0, keepdims=True)))
        out_ref[0, rows, :] = one_head_each(mul_wide(dscores, k_pair, TN)) * scale
        out_ref[1, keys, :] += mul_wide(dscores, q_pair, NN)
        out_ref[2, keys, :] += mul_wide(split(probs), g_pair, NN)


def attend_back(qkv, grad, half, segs, deps=()):
    toks, width = qkv.shape[0], qkv.shape[1] // 3
    pairs = width // LANES
    seg_col, _, seg_row = segs
    return pl.pallas_call(
        leaving_out(attend_back_kernel, 6, deps),
        out_shape=shape(3, toks, width),
        grid=(pairs,),
        in_specs=pair_specs(toks, pairs, 3)
        + [
            pl.BlockSpec((toks, LANES), lambda i: (0, half * pairs + i)),
            whole(*seg_col.shape),
            whole(*seg_row.shape),
        ]
        + untouched(deps),
        out_specs=pl.BlockSpec((3, toks, LANES), lambda i: (0, 0, i)),
        compiler_params=params(),
        cost_estimate=cost(60 * toks * SPAN * width, 28 * toks * width, toks * SPAN * width // 64),
        name="attend_back",
    )(qkv, qkv, qkv, grad, seg_col, seg_row, *deps)


def cdf_of(pre):
    return 0.5 * (1.0 + lax.erf(pre * (1.0 / math.sqrt(2.0))))


def mlp_kernel(x_ref, b_ref, w1_ref, w2_ref, acc_ref, pre_ref, y_ref, xh_ref, xl_ref):
    @pl.when(pl.program_id(0) == 0)
    def _():
        xh_ref[...], xl_ref[...] = split(x_ref[...])
        y_ref[...] = acc_ref[...]

    pre = mul3((xh_ref[...], xl_ref[...]), split(w1_ref[...]), NN) + b_ref[...]
    pre_ref[...] = pre
    y_ref[...] += mul3(split(pre * cdf_of(pre)), split(w2_ref[...]), NN)


def mlp_forward(normed, bias, w1, w2, acc, deps=(), block=512):
    toks, dim = normed.shape
    hidden = w1.shape[1]
    return pl.pallas_call(
        leaving_out(mlp_kernel, 5, deps),
        out_shape=(shape(toks, hidden), shape(toks, dim)),
        grid=(hidden // block,),
        in_specs=[
            whole(toks, dim),
            pl.BlockSpec((1, block), lambda j: (0, j)),
            pl.BlockSpec((dim, block), lambda j: (0, j)),
            pl.BlockSpec((block, dim), lambda j: (j, 0)),
            whole(toks, dim),
        ]
        + untouched(deps),
        out_specs=(pl.BlockSpec((toks, block), lambda j: (0, j)), whole(toks, dim)),
        scratch_shapes=[pltpu.VMEM((toks, dim), bf16)] * 2,
        compiler_params=params(),
        cost_estimate=cost(12 * toks * dim * hidden, 8 * dim * hidden + 4 * toks * (hidden + 2 * dim), toks * hidden),
        name="mlp_forward",
    )(normed, bias, w1, w2, acc, *deps)


def own_then_other(half):
    return (lambda j: jnp.minimum(j, half - 1)), (lambda j: jnp.maximum(j - half, 0))


def fill_transposed(src_ref, high_ref, low_ref):
    high_ref[...], low_ref[...] = split(jnp.transpose(src_ref[...]))


def mlp_back_a_kernel(half, block, split_out, core_ref, eg_ref, prea_ref, preb_ref, w2a_ref, w2b_ref, *refs):
    j = pl.program_id(0)
    pg_ref, b1_ref, keep_ref = refs[:3]
    send_ref = refs[3] if split_out else None
    eh_ref, el_ref, th_ref, tl_ref = refs[-4:]

    @pl.when(j == 0)
    def _():
        eh_ref[...], el_ref[...] = split(eg_ref[...])
        fill_transposed(eg_ref, th_ref, tl_ref)

    def step(pre_ref, w2_ref):
        pre = pre_ref[...]
        cdf = cdf_of(pre)
        pdf = jnp.exp(-0.5 * pre * pre) * (1.0 / math.sqrt(2.0 * math.pi))
        pg = mul3((eh_ref[...], el_ref[...]), split(w2_ref[...]), NT) * (cdf + pre * pdf)
        pg_ref[...] = pg
        b1_ref[...] = jnp.sum(pg, axis=0, keepdims=True)
        tile = mul3((th_ref[...], tl_ref[...]), split(pre * cdf), NN)
        store_rows(core_ref, tile, keep_ref, send_ref, slice(None), block)

    @pl.when(j < half)
    def _():
        step(prea_ref, w2a_ref)

    @pl.when(j >= half)
    def _():
        step(preb_ref, w2b_ref)


def grad_shapes(dim, cols, block, split_out):
    if split_out:
        return [shape(dim // (2 * block), block, cols)] * 2
    return [shape(dim, cols)]


def grad_specs(dim, cols, block, split_out):
    if split_out:
        return [pl.BlockSpec((dim // (2 * block), block, cols), lambda j, *_: (0, 0, j))] * 2
    return [pl.BlockSpec((dim, cols), lambda j, *_: (0, j))]


def mlp_back_a(core, enc_grad, pre, w2, rows, split_out, deps=(), block=512):
    toks, dim = enc_grad.shape
    hidden = 2 * pre[0].shape[1]
    half = hidden // 2 // block
    low, high = own_then_other(half)
    out = pl.pallas_call(
        leaving_out(functools.partial(mlp_back_a_kernel, half, rows, split_out), 6, deps),
        out_shape=[shape(toks, hidden), shape(1, hidden)] + grad_shapes(dim, hidden, rows, split_out),
        grid_spec=pltpu.PrefetchScalarGridSpec(
            num_scalar_prefetch=1,
            grid=(2 * half,),
            in_specs=[
                whole(toks, dim),
                pl.BlockSpec((toks, block), lambda j, _: (0, low(j))),
                pl.BlockSpec((toks, block), lambda j, _: (0, high(j))),
                pl.BlockSpec((block, dim), lambda j, _: (low(j), 0)),
                pl.BlockSpec((block, dim), lambda j, _: (high(j), 0)),
            ]
            + untouched(deps),
            out_specs=[
                pl.BlockSpec((toks, block), lambda j, _: (0, j)),
                pl.BlockSpec((1, block), lambda j, _: (0, j)),
            ]
            + grad_specs(dim, block, rows, split_out),
            scratch_shapes=[pltpu.VMEM((toks, dim), bf16)] * 2 + [pltpu.VMEM((dim, toks), bf16)] * 2,
        ),
        compiler_params=params(),
        cost_estimate=cost(12 * toks * dim * hidden, 8 * dim * hidden + 8 * toks * hidden, 2 * toks * hidden),
        name="mlp_back_a",
    )(core, enc_grad, *pre, *w2, *deps)
    return out[0], out[1], out[2:]


def mlp_input_kernel(half, pg_ref, wa_ref, wb_ref, dx_ref):
    j = pl.program_id(0)

    @pl.when(j == 0)
    def _():
        dx_ref[...] = jnp.zeros_like(dx_ref)

    @pl.when(j < half)
    def _():
        dx_ref[...] += mul3(split(pg_ref[...]), split(wa_ref[...]), NT)

    @pl.when(j >= half)
    def _():
        dx_ref[...] += mul3(split(pg_ref[...]), split(wb_ref[...]), NT)


def mlp_input_grad(pre_grad, w1, deps=(), block=768):
    toks, hidden = pre_grad.shape
    dim = w1[0].shape[0]
    half = hidden // 2 // block
    low, high = own_then_other(half)
    return pl.pallas_call(
        leaving_out(functools.partial(mlp_input_kernel, half), 3, deps),
        out_shape=shape(toks, dim),
        grid=(2 * half,),
        in_specs=[
            pl.BlockSpec((toks, block), lambda j: (0, j)),
            pl.BlockSpec((dim, block), lambda j: (0, low(j))),
            pl.BlockSpec((dim, block), lambda j: (0, high(j))),
        ]
        + untouched(deps),
        out_specs=whole(toks, dim),
        compiler_params=params(),
        cost_estimate=cost(6 * toks * dim * hidden, 4 * dim * hidden + 4 * toks * hidden, scale=COVER),
        name="mlp_input_grad",
    )(pre_grad, *w1, *deps)


def weight_grad_kernel(rows, split_out, core_ref, x_ref, g_ref, *refs):
    th_ref, tl_ref = refs[-2:]
    outs = refs[-4:-2] if split_out else (refs[-3], None)

    @pl.when(pl.program_id(0) == 0)
    def _():
        fill_transposed(x_ref, th_ref, tl_ref)

    grad = g_ref[0] if len(g_ref.shape) == 3 else g_ref[...]
    tile = mul3((th_ref[...], tl_ref[...]), split(grad), NN)
    store_rows(core_ref, tile, *outs, slice(None), rows)


def weight_grad(core, inputs, grad, rows, split_out, block, into=(), first=0, cols=None, deps=(), scale=SCALE):
    toks, dim = inputs.shape
    planes = grad.ndim == 3
    steps = grad.shape[0] if planes else grad.shape[1] // block
    width = steps * block
    cols = cols or width
    g_spec = (
        pl.BlockSpec((1, toks, block), lambda j, _: (j, 0, 0)) if planes else pl.BlockSpec((toks, block), lambda j, _: (0, j))
    )
    shapes = grad_shapes(dim, cols, rows, split_out)
    if split_out:
        out_spec = pl.BlockSpec((dim // (2 * rows), rows, block), lambda j, _: (0, 0, j + first))
    else:
        out_spec = pl.BlockSpec((dim, block), lambda j, _: (0, j + first))
    return pl.pallas_call(
        functools.partial(weight_grad_kernel, rows, split_out),
        out_shape=shapes,
        grid_spec=pltpu.PrefetchScalarGridSpec(
            num_scalar_prefetch=1,
            grid=(steps,),
            in_specs=[whole(toks, dim), g_spec] + untouched(into) + untouched(deps),
            out_specs=[out_spec] * len(shapes),
            scratch_shapes=[pltpu.VMEM((dim, toks), bf16)] * 2,
        ),
        input_output_aliases={3 + i: i for i in range(len(into))},
        compiler_params=params(),
        cost_estimate=cost(6 * toks * dim * width, 4 * (toks * dim + dim * width + toks * width), scale=scale),
        name="weight_grad",
    )(core, inputs, grad, *into, *deps)


def out_back_kernel(rows, split_out, core_ref, g_ref, wa_ref, wb_ref, ca_ref, cb_ref, *refs):
    j = pl.program_id(0)
    dc_ref, keep_ref = refs[:2]
    send_ref = refs[2] if split_out else None
    gh_ref, gl_ref, th_ref, tl_ref = refs[-4:]

    @pl.when(j == 0)
    def _():
        gh_ref[...], gl_ref[...] = split(g_ref[...])
        fill_transposed(g_ref, th_ref, tl_ref)

    def step(w_ref, c_ref):
        dc_ref[...] = mul3((gh_ref[...], gl_ref[...]), split(w_ref[...]), NT)
        tile = mul3((th_ref[...], tl_ref[...]), split(c_ref[...]), NN)
        store_rows(core_ref, tile, keep_ref, send_ref, slice(None), rows)

    @pl.when(j == 0)
    def _():
        step(wa_ref, ca_ref)

    @pl.when(j == 1)
    def _():
        step(wb_ref, cb_ref)


def out_back(core, mid_grad, weights, ctx, rows, split_out, deps=()):
    toks, dim = mid_grad.shape
    width = ctx[0].shape[1]
    cols = 8 * width
    shapes = grad_shapes(dim, cols, rows, split_out)
    if split_out:
        spec = pl.BlockSpec((dim // (2 * rows), rows, width), lambda j, _: (0, 0, 4 * j))
    else:
        spec = pl.BlockSpec((dim, width), lambda j, _: (0, 4 * j))
    out = pl.pallas_call(
        leaving_out(functools.partial(out_back_kernel, rows, split_out), 6, deps),
        out_shape=[shape(toks, 2 * width)] + shapes,
        grid_spec=pltpu.PrefetchScalarGridSpec(
            num_scalar_prefetch=1,
            grid=(2,),
            in_specs=[whole(toks, dim)] + [whole(width, dim)] * 2 + [whole(toks, width)] * 2 + untouched(deps),
            out_specs=[pl.BlockSpec((toks, width), lambda j, _: (0, j))] + [spec] * len(shapes),
            scratch_shapes=[pltpu.VMEM((toks, dim), bf16)] * 2 + [pltpu.VMEM((dim, toks), bf16)] * 2,
        ),
        compiler_params=params(),
        cost_estimate=cost(24 * toks * dim * width, 4 * (toks * dim + 4 * dim * width + 4 * toks * width)),
        name="out_back",
    )(core, mid_grad, *weights, *ctx, *deps)
    return out[0], out[1:]


def qkv_input_kernel(ga_ref, gb_ref, wa_ref, wb_ref, dx_ref):
    @pl.when(pl.program_id(0) == 0)
    def _():
        dx_ref[...] = jnp.zeros_like(dx_ref)

    for g_ref, w_ref in ((ga_ref, wa_ref), (gb_ref, wb_ref)):
        dx_ref[...] += mul3(split(g_ref[0]), split(w_ref[0]), NT)


def qkv_input_grad(grads, weights, deps=()):
    toks = grads[0].shape[1]
    _, dim, width = weights[0].shape
    grad_spec = pl.BlockSpec((1, toks, width), lambda c: (c, 0, 0))
    w_spec = pl.BlockSpec((1, dim, width), lambda c: (c, 0, 0))
    return pl.pallas_call(
        leaving_out(qkv_input_kernel, 4, deps),
        out_shape=shape(toks, dim),
        grid=(3,),
        in_specs=[grad_spec, grad_spec, w_spec, w_spec] + untouched(deps),
        out_specs=whole(toks, dim),
        compiler_params=params(),
        cost_estimate=cost(36 * toks * dim * width, 4 * (toks * dim + 6 * dim * width + 6 * toks * width), scale=COVER),
        name="qkv_input_grad",
    )(*grads, *weights, *deps)


def norm_back_kernel(up_ref, unit_ref, inverse_ref, gain_ref, base_ref, out_ref, sums_ref):
    @pl.when(pl.program_id(0) == 0)
    def _():
        sums_ref[...] = jnp.zeros_like(sums_ref)

    upstream, unit_val, base = up_ref[...], unit_ref[...], base_ref[...]
    out_ref[...] = base + norm_back(upstream, unit_val, inverse_ref[...], gain_ref[...])
    for i, val in enumerate((upstream * unit_val, upstream, base)):
        sums_ref[i : i + 1, :] += jnp.sum(val, axis=0, keepdims=True)


def norm_back_sums(upstream, unit_val, inverse, gain, base, steps=4):
    toks, dim = upstream.shape
    block = pl.BlockSpec((toks // steps, dim), lambda i: (i, 0))
    out, sums = pl.pallas_call(
        norm_back_kernel,
        out_shape=(shape(toks, dim), shape(8, dim)),
        grid=(steps,),
        in_specs=[block, block, pl.BlockSpec((toks // steps, 1), lambda i: (i, 0)), whole(1, dim), block],
        out_specs=(block, whole(8, dim)),
        compiler_params=params(),
        cost_estimate=cost(20 * toks * dim, 16 * toks * dim),
        name="norm_back",
    )(upstream, unit_val, inverse, gain[None], base)
    return out, sums[:3].reshape(-1)


def per_device(
    n_dp,
    patches,
    segment_ids,
    proprio,
    ln1_gain,
    ln1_bias,
    qkv_weight,
    qv_bias,
    out_weight,
    out_bias,
    ln2_gain,
    ln2_bias,
    fc1_weight,
    fc1_bias,
    fc2_weight,
    fc2_bias,
    pol_image,
    pol_proprio,
    pol_hidden,
    pol_third,
    pol_action,
    out_cotangent,
    action_cotangent,
):
    row_len, dim = patches.shape
    images = proprio.shape[0]
    local_dim = qkv_weight.shape[2]
    local_ff = fc1_weight.shape[1]
    toks = -(-(row_len // 2 + MOST // 2) // TILE) * TILE
    low = row_len - toks
    rows = dim // n_dp
    split_out = rows % 8 == 0

    mine = lax.axis_index("dp")
    side = lax.axis_index("tensor")
    bit_c, bit_y, bit_z, bits_h = mine & 1, (mine >> 1) & 1, (mine >> 2) & 1, mine >> 3
    core = jnp.reshape(bit_c, (1,)).astype(jnp.int32)

    def across(val):
        return lax.ppermute(val, "tensor", [(0, 1), (1, 0)])

    def swap(val, bit):
        return lax.ppermute(val, "dp", [(i, i ^ (1 << bit)) for i in range(n_dp)])

    def pick(val, index, axis):
        return lax.dynamic_index_in_dim(val, index, axis, keepdims=False)

    def gate(*vals):
        return lax.optimization_barrier(vals)

    def slices(weight):
        piece = weight.shape[0] // 8
        return [
            lax.dynamic_slice_in_dim(weight, index * piece, piece, 0)
            for index in (2 * bit_y + bit_c, 4 + 2 * bit_z + bit_c)
        ]

    def joined(pieces, others):
        place = []
        for c in (bit_c, 1 - bit_c):
            place += [2 * bit_y + c, 4 + 2 * bit_z + c, 2 * (1 - bit_y) + c, 4 + 2 * (1 - bit_z) + c]
        return join_pieces(jnp.stack(place).astype(jnp.int32), pieces + others)

    bias_pack = jnp.concatenate([qv_bias.reshape(-1), fc1_bias])
    wq_own = jnp.transpose(qkv_weight, (1, 0, 2))

    seg = segment_ids[0]
    pos = jnp.arange(row_len, dtype=jnp.int32)
    first_tok = jnp.concatenate([jnp.ones((1,), bool), seg[1:] != seg[:-1]])
    cut = jnp.min(jnp.where(first_tok & (pos >= low), pos, row_len))
    start = side * low

    def window(val):
        return lax.dynamic_slice_in_dim(val, start, toks, 0)

    here = start + jnp.arange(toks, dtype=jnp.int32)
    owned = jnp.where(side == 0, here < cut, here >= cut)
    seg_here, first_here = window(seg), window(first_tok)
    seg_col = seg_here[:, None]
    seg_win = jnp.stack([seg_here[s : s + SPAN] for s in starts_of(toks)])[:, None, :]
    seg_tile = seg_here.reshape(-1, 1, TILE)
    segs = (seg_col, seg_win, jnp.concatenate([seg_tile, seg_tile], axis=2))
    cls_pick = (
        (seg_here[None, :] == jnp.arange(images, dtype=jnp.int32)[:, None]) & (first_here & owned)[None, :]
    ).astype(f32)
    mine_image = jnp.sum(cls_pick, axis=1, keepdims=True)

    bias_oth = across(bias_pack)
    sent_q = slices(wq_own.reshape(3 * dim, local_dim))
    got_q = [across(val) for val in sent_q]
    x_in = window(patches)
    unit_in, inverse_in = norm_stats(x_in)
    normed_in = unit_in * ln1_gain + ln1_bias

    def qkv_bias_of(flat):
        return jnp.concatenate([flat[:local_dim], jnp.zeros((local_dim,), f32), flat[local_dim : 2 * local_dim]])[None]

    qkv_own = qkv_forward(normed_in, wq_own, qkv_bias_of(bias_pack))
    qkv_own, bias_oth, *got_q = gate(qkv_own, bias_oth, *got_q)
    near_q = [swap(got_q[0], 1), swap(got_q[1], 2)]
    core_q = [swap(val, 0) for val in got_q]
    half = out_weight.shape[0] // 2
    wo_part = lax.dynamic_slice_in_dim(out_weight, bit_c * half, half, 0)
    wo_part, *sent_1 = gate(wo_part, *slices(fc1_weight), *got_q)[:3]
    got_o = across(wo_part)
    got_1 = [across(val) for val in sent_1]
    ctx_own = attend(qkv_own, segs, deps=[wo_part, *sent_1])
    ctx_own, *near_q = gate(ctx_own, *near_q)
    core_q += [swap(val, 0) for val in near_q]
    wq_oth = joined(list(got_q) + list(near_q), core_q).reshape(3, dim, local_dim)
    sent_2 = slices(fc2_weight)
    qkv_oth = qkv_forward(normed_in, wq_oth, qkv_bias_of(bias_oth), deps=[ctx_own, *sent_2])
    qkv_oth, got_o = gate(qkv_oth, got_o)
    core_o = swap(got_o, 0)
    ctx_oth = attend(qkv_oth, segs, deps=[got_o])
    ctx_oth, core_o, *got_1 = gate(ctx_oth, core_o, *got_1)
    wo_oth = join_pieces(jnp.stack([bit_c, 1 - bit_c]).astype(jnp.int32), [got_o, core_o])
    near_1 = [swap(got_1[0], 1), swap(got_1[1], 2)]
    core_1 = [swap(val, 0) for val in got_1]
    sent_2 = gate(*sent_2, *got_1)[:2]
    got_2 = [across(val) for val in sent_2]
    qkv, ctx, wo, wq = [qkv_own, qkv_oth], [ctx_own, ctx_oth], [out_weight, wo_oth], [wq_own, wq_oth]
    high = lax.Precision.HIGH
    attn = jnp.dot(ctx[0], wo[0], precision=high) + jnp.dot(ctx[1], wo[1], precision=high)
    mid = x_in + attn + out_bias
    unit_mid, inverse_mid = norm_stats(mid)
    normed_mid = unit_mid * ln2_gain + ln2_bias
    pre_own, mlp_out = mlp_forward(normed_mid, fc1_bias[None], fc1_weight, fc2_weight, mid + fc2_bias, deps=got_1)
    mlp_out, *moved = gate(mlp_out, *near_1, *core_1, *got_2)
    near_1, core_1, got_2 = moved[:2], moved[2:4], moved[4:]
    near_2 = [swap(got_2[0], 1), swap(got_2[1], 2)]
    core_1 += [swap(val, 0) for val in near_1]
    core_2 = [swap(val, 0) for val in got_2]
    w1_oth = joined(list(got_1) + list(near_1), core_1)
    w1_oth, *near_2 = gate(w1_oth, *near_2)
    core_2 += [swap(val, 0) for val in near_2]
    w2_oth = joined(list(got_2) + list(near_2), core_2)
    pre_oth, enc = mlp_forward(normed_mid, bias_oth[None, 2 * local_dim :], w1_oth, w2_oth, mlp_out)
    w1, w2, pre_act = (fc1_weight, w1_oth), (fc2_weight, w2_oth), (pre_own, pre_oth)
    enc_got = across(enc)

    cls_features = dense(cls_pick, enc)
    act_cot = action_cotangent * mine_image
    pre_one = dense(cls_features, pol_image) + dense(proprio, pol_proprio)
    hidden_one = jax.nn.elu(pre_one)
    pre_two = dense(hidden_one, pol_hidden)
    hidden_two = jax.nn.elu(pre_two)
    pre_three = dense(hidden_two, pol_third)
    hidden_three = jax.nn.elu(pre_three)
    actions_part = dense(hidden_three, pol_action) * mine_image
    grad_p4 = dense(hidden_three.T, act_cot)
    grad_three = elu_back(dense(act_cot, pol_action.T), pre_three)
    grad_p3 = dense(hidden_two.T, grad_three)
    grad_two = elu_back(dense(grad_three, pol_third.T), pre_two)
    grad_p2 = dense(hidden_one.T, grad_two)
    grad_one = elu_back(dense(grad_two, pol_hidden.T), pre_one)
    grad_pimage = dense(cls_features.T, grad_one)
    grad_pprop = dense(proprio.T, grad_one)
    cls_grad = dense(grad_one, pol_image.T)

    def share(val):
        return val[..., : val.shape[-1] // 2], val[..., val.shape[-1] // 2 :]

    class Chain:
        def __init__(self, terms, order, first, size):
            self.terms, self.moving, self.first, self.size = terms, None, first, size
            levels = 0
            while 8 << levels < n_dp:
                levels += 1
            self.plan = list(order) + ["x"] + list(range(3, 3 + levels))
            self.axis = {1: 2, 2: 1} if order[0] == 1 else {2: 1, 1: 1}

        def part(self, val, index, axis):
            at, sizes = [0] * val.ndim, list(val.shape)
            at[axis], sizes[axis] = index, 1
            at[-2], sizes[-2] = self.first, self.size
            return jnp.squeeze(lax.dynamic_slice(val, at, sizes), axis)

        def step(self, tied):
            if self.moving is not None:
                tied, got = gate(tied, self.moving)
                self.terms.append(got)
            what = self.plan.pop(0)
            if what == "x":
                out, kept = (sum(share(val)[i] for val in self.terms) for i in (1, 0))
                tied, out = gate(tied, out)
                self.terms, self.moving = [kept], across(out)
                return tied
            bit = (mine >> what) & 1
            axis = self.axis.get(what, 1)
            if what >= 3:
                self.terms = [val.reshape((val.shape[0] // 2, 2) + val.shape[1:]) for val in self.terms]
            out, kept = (sum(self.part(val, index, axis) for val in self.terms) for index in (1 - bit, bit))
            self.first = 0
            tied, out = gate(tied, out)
            self.terms, self.moving = [kept], swap(out, what)
            return tied

    class Scatter:
        def __init__(self, parts, orders):
            self.parts, self.orders, self.chains = parts, orders, []
            if split_out:
                self.got = swap(parts[1], 0)

        def step(self, tied):
            if not split_out:
                return tied
            if not self.chains:
                tied, self.got = gate(tied, self.got)
                piece = rows // len(self.orders)
                terms = [val.reshape((n_dp // 8, 2, 2) + val.shape[1:]) for val in (self.parts[0], self.got)]
                self.chains = [Chain(list(terms), order, i * piece, piece) for i, order in enumerate(self.orders)]
            for chain in self.chains:
                if chain.plan:
                    tied = chain.step(tied)
            return tied

        def hold(self, tied):
            for chain in self.chains:
                tied, chain.moving = gate(tied, chain.moving)
            return tied

        def result(self):
            if not split_out:
                own, oth = share(self.parts[0])
                return lax.psum_scatter(own + across(oth), "dp", scatter_dimension=0, tiled=True)
            while not self.chains or any(chain.plan for chain in self.chains):
                self.step(core)
            return jnp.concatenate([sum(val[0] for val in chain.terms + [chain.moving]) for chain in self.chains])

    class Total:
        def __init__(self, val, halvings):
            self.halvings = halvings
            levels = 1
            while 2 << levels <= n_dp:
                levels += 1
            self.plan = list(range(levels)) + ["x"]
            self.val = val
            self.send()

        def send(self):
            what = self.plan.pop(0) if self.plan else None
            if what is None:
                self.moving = None
            elif what == "x":
                self.moving = across(self.val)
            elif what < self.halvings:
                bit = (mine >> what) & 1
                pair = self.val.reshape((2, self.val.shape[0] // 2) + self.val.shape[1:])
                self.sent = pick(pair, 1 - bit, 0)
                self.val, self.moving = pick(pair, bit, 0), swap(self.sent, what)
            else:
                self.moving = swap(self.val, what)

        def step(self, tied):
            tied, got = gate(tied, self.moving)
            self.val = self.val + got
            self.send()
            return gate(tied, self.val)[0]

        def result(self):
            while self.moving is not None:
                self.step(core)
            for what in reversed(range(self.halvings)):
                bit = (mine >> what) & 1
                got = swap(self.val, what)
                first = jnp.where(bit == 0, self.val, got)
                self.val = jnp.concatenate([first, jnp.where(bit == 0, got, self.val)])
            return self.val

    both_orders = [(1, 2), (2, 1)] if rows % 16 == 0 else [(1, 2)]
    pad = lambda val, h, w: jnp.pad(val, ((0, h - val.shape[0]), (0, w - val.shape[1])))
    hid = pol_hidden.shape[1]
    rest = jnp.concatenate([pad(grad_p3, hid, hid), pad(grad_p4, pol_hidden.shape[0] - hid, hid)], axis=0)
    pol_pack = jnp.concatenate([grad_pimage, pad(grad_pprop, 32, pol_image.shape[1]), jnp.concatenate([grad_p2, rest], axis=1)])
    enc_grad = jnp.where(owned[:, None], window(out_cotangent), 0.0) + lax.dot_general(
        cls_pick, cls_grad, TN, precision=highest
    )
    pol = Total(pol_pack, 2)
    enc_grad = pol.step(enc_grad)
    pre_grad, grad_b1, parts_w2 = mlp_back_a(core, enc_grad, pre_act, w2, rows, split_out, deps=[pol.val])
    sum_2 = Scatter(parts_w2, both_orders)
    pre_grad, enc_got = gate(pre_grad, enc_got)
    pre_grad = pol.step(pre_grad)
    parts_w1 = weight_grad(core, normed_mid, pre_grad, rows, split_out, 512, deps=[pol.val], scale=COVER)
    sum_1 = Scatter(parts_w1, both_orders)
    pre_grad, kept = gate(pre_grad, parts_w1[0])
    pre_grad = sum_2.step(pre_grad)
    normed_mid_grad = mlp_input_grad(pre_grad, w1, deps=[kept])
    normed_mid_grad = sum_1.step(normed_mid_grad)
    mid_grad, sums_mid = norm_back_sums(normed_mid_grad, unit_mid, inverse_mid, ln2_gain, enc_grad)
    ctx_grad, parts_a = out_back(core, mid_grad, wo, ctx, rows, split_out)
    ctx_grad = sum_2.step(ctx_grad)
    dqkv_oth = attend_back(qkv[1], ctx_grad, 1, segs)
    dqkv_oth = sum_1.step(dqkv_oth)
    dqkv_own = attend_back(qkv[0], ctx_grad, 0, segs, deps=[dqkv_oth])
    dqkv_own = sum_2.step(dqkv_own)
    merge = functools.partial(weight_grad, core, normed_in, rows=rows, split_out=split_out, block=local_dim, cols=8 * local_dim)
    parts_a = merge(grad=dqkv_oth, into=parts_a, first=5, deps=[dqkv_own])
    dqkv_own, *parts_a = gate(dqkv_own, *parts_a)
    dqkv_own = pol.step(dqkv_own)
    parts_a = merge(grad=dqkv_own, into=parts_a, first=1)
    sum_a = Scatter(parts_a, both_orders)
    dqkv_own, kept = gate(dqkv_own, parts_a[0])
    dqkv_own = sum_2.step(dqkv_own)
    dqkv = [dqkv_own, dqkv_oth]
    normed_in_grad = qkv_input_grad(dqkv, wq, deps=[kept])
    normed_in_grad = sum_a.step(normed_in_grad)
    patches_grad, sums_in = norm_back_sums(normed_in_grad, unit_in, inverse_in, ln1_gain, mid_grad)

    def token_sum(val):
        return jnp.sum(val, axis=0)

    common = jnp.concatenate([sums_in, sums_mid])
    halves = [
        jnp.concatenate([token_sum(dqkv[i][0]), token_sum(dqkv[i][2]), grad_b1[0, i * local_ff : (i + 1) * local_ff]])
        for i in range(2)
    ]
    vec_got = across(jnp.concatenate([common, halves[1], actions_part.reshape(-1)]))
    patches_grad = sum_1.step(patches_grad)
    patches_grad = pol.step(patches_grad)
    pg_got = across(patches_grad)
    tied = sum_2.hold(patches_grad)
    tied = sum_a.step(tied)
    tied = sum_1.step(tied)
    tied = sum_a.step(tied)
    tied, pg_got, vec_got = gate(tied, pg_got, vec_got)
    vec = jnp.concatenate([common, halves[0]])
    small = Total(vec + vec_got[: vec.size], 0)
    actions = actions_part + vec_got[vec.size :].reshape(actions_part.shape)
    small.plan.remove("x")
    tied = small.step(tied)
    tied = pol.step(tied)
    tied = sum_1.hold(tied)
    tied = sum_a.step(tied)
    patches_grad = small.step(tied)
    vec = small.result()
    summed_w2, summed_w1, summed_attn, pol_sum = sum_2.result(), sum_1.result(), sum_a.result(), pol.result()
    common, halves = vec[: 6 * dim].reshape(6, dim), vec[6 * dim :]

    def assemble(own, got):
        left = jnp.where(side == 0, own, got)
        right = jnp.where(side == 0, got, own)
        overlap = toks - low
        inside = low + jnp.arange(overlap, dtype=jnp.int32)
        return jnp.concatenate(
            [left[:low], jnp.where((inside < cut)[:, None], left[low:], right[:overlap]), right[overlap:]]
        )

    width = pol_image.shape[0]
    tail = pol_sum[width + 32 :]
    return (
        assemble(enc, enc_got),
        actions,
        assemble(patches_grad, pg_got),
        common[0],
        common[1],
        summed_attn[:, local_dim:].reshape(rows, 3, local_dim),
        halves[: 2 * local_dim].reshape(2, local_dim),
        summed_attn[:, :local_dim].T,
        common[2],
        common[3],
        common[4],
        summed_w1,
        halves[2 * local_dim :],
        summed_w2.T,
        common[5],
        pol_sum[:width],
        pol_sum[width : width + proprio.shape[1]],
        tail[:, :hid],
        tail[:hid, hid : hid + pol_third.shape[1]],
        tail[hid : hid + pol_action.shape[0], hid : hid + pol_action.shape[1]],
    )


def solution(mesh):
    return jax.shard_map(
        functools.partial(per_device, mesh.shape["dp"]),
        mesh=mesh,
        in_specs=(
            P("dp", None),
            P("dp", None),
            P("dp", None),
            P(),
            P(),
            P(None, None, "tensor"),
            P(None, "tensor"),
            P("tensor", None),
            P(),
            P(),
            P(),
            P(None, "tensor"),
            P("tensor"),
            P("tensor", None),
            P(),
            P(),
            P(),
            P(),
            P(),
            P(),
            P("dp", None),
            P("dp", None),
        ),
        out_specs=(
            P("dp", None),
            P("dp", None),
            P("dp", None),
            P(),
            P(),
            P("dp", None, "tensor"),
            P(None, "tensor"),
            P("tensor", "dp"),
            P(),
            P(),
            P(),
            P("dp", "tensor"),
            P("tensor"),
            P("tensor", "dp"),
            P(),
            P(),
            P(),
            P(),
            P(),
            P(),
        ),
        check_vma=False,
    )
```

```python
import functools
import math

import jax
import jax.numpy as jnp
from jax import lax
from jax.experimental import pallas as pl
from jax.experimental.pallas import tpu as pltpu
from jax.sharding import PartitionSpec as P

HEAD_DIM = 64
MOST = 50
LANES = 128
TILE = 128
SPAN = 256
SCALE = 0.02
COVER = 20.0

highest = lax.Precision.HIGHEST
norm_eps = 1e-06
f32 = jnp.float32
bf16 = jnp.bfloat16

NN = (((1,), (0,)), ((), ()))
NT = (((1,), (1,)), ((), ()))
TN = (((0,), (0,)), ((), ()))


def split(val):
    high = val.astype(bf16)
    return high, (val - high.astype(f32)).astype(bf16)


def mul(left, right, dims):
    return lax.dot_general(left, right, dims, preferred_element_type=f32)


def mul3(left, right, dims):
    (lh, ll), (rh, rl) = left, right
    return mul(lh, rh, dims) + (mul(lh, rl, dims) + mul(ll, rh, dims))


def dense(left, right):
    return jnp.dot(left, right, precision=highest)


def norm_stats(inputs):
    centred = inputs - jnp.mean(inputs, axis=-1, keepdims=True)
    inverse = lax.rsqrt(jnp.mean(centred * centred, axis=-1, keepdims=True) + norm_eps)
    return centred * inverse, inverse


def norm_back(upstream, unit_val, inverse, gain):
    scaled = upstream * gain
    centred = scaled - jnp.mean(scaled, axis=-1, keepdims=True)
    return inverse * (centred - unit_val * jnp.mean(scaled * unit_val, axis=-1, keepdims=True))


def elu_back(upstream, pre_act):
    return upstream * jnp.where(pre_act > 0, 1.0, jnp.exp(jnp.minimum(pre_act, 0.0)))


def params(limit_mib=56):
    return pltpu.CompilerParams(vmem_limit_bytes=limit_mib << 20)


def cost(flops, nbytes, trans=0, scale=SCALE):
    return pl.CostEstimate(flops=int(flops * scale), bytes_accessed=int(nbytes * scale), transcendentals=int(trans * scale))


def shape(*dims):
    return jax.ShapeDtypeStruct(dims, f32)


def whole(*dims):
    zeros = (0,) * len(dims)
    return pl.BlockSpec(dims, lambda *_: zeros)


def untouched(deps):
    return [pl.BlockSpec(memory_space=pl.ANY)] * len(deps)


def leaving_out(kernel, first, deps):
    return lambda *refs: kernel(*refs[:first], *refs[first + len(deps) :])


def join_kernel(where_ref, *refs):
    out_ref = refs[-1]
    for i, ref in enumerate(refs[:-1]):
        out_ref[pl.ds(where_ref[i], 1)] = ref[...][None]


def join_pieces(where, pieces):
    rows, cols = pieces[0].shape
    count = len(pieces)
    steps = next(n for n in (4, 3, 2, 1) if rows % (8 * n) == 0)
    part = rows // steps
    out = pl.pallas_call(
        join_kernel,
        out_shape=shape(count, rows, cols),
        grid_spec=pltpu.PrefetchScalarGridSpec(
            num_scalar_prefetch=1,
            grid=(steps,),
            in_specs=[pl.BlockSpec((part, cols), lambda i, w: (i, 0))] * count,
            out_specs=pl.BlockSpec((count, part, cols), lambda i, w: (0, i, 0)),
        ),
        compiler_params=params(),
        cost_estimate=cost(0, 8 * count * rows * cols),
        name="join_pieces",
    )(where, *pieces)
    return out.reshape(count * rows, cols)


def store_rows(core_ref, tile, keep_ref, send_ref, lanes, block):
    if send_ref is None:
        keep_ref[:, lanes] = tile
        return
    pairs = tile.shape[0] // (2 * block)

    def put(first, second):
        for i in range(pairs):
            low = 2 * i * block
            first[i, :, lanes] = tile[low : low + block]
            second[i, :, lanes] = tile[low + block : low + 2 * block]

    @pl.when(core_ref[0] == 0)
    def _():
        put(keep_ref, send_ref)

    @pl.when(core_ref[0] != 0)
    def _():
        put(send_ref, keep_ref)


def qkv_kernel(x_ref, w_ref, b_ref, out_ref, xh_ref, xl_ref):
    @pl.when(pl.program_id(0) == 0)
    def _():
        xh_ref[...], xl_ref[...] = split(x_ref[...])

    out_ref[...] = mul3((xh_ref[...], xl_ref[...]), split(w_ref[0]), NN) + b_ref[...]


def qkv_forward(normed, weight, bias, deps=()):
    toks, dim = normed.shape
    width = weight.shape[2]
    return pl.pallas_call(
        leaving_out(qkv_kernel, 3, deps),
        out_shape=shape(toks, 3 * width),
        grid=(3,),
        in_specs=[
            whole(toks, dim),
            pl.BlockSpec((1, dim, width), lambda c: (c, 0, 0)),
            pl.BlockSpec((1, width), lambda c: (0, c)),
        ]
        + untouched(deps),
        out_specs=pl.BlockSpec((toks, width), lambda c: (0, c)),
        scratch_shapes=[pltpu.VMEM((toks, dim), bf16)] * 2,
        compiler_params=params(),
        cost_estimate=cost(18 * toks * dim * width, 4 * (toks * dim + 3 * width * (dim + toks))),
        name="qkv_forward",
    )(normed, weight, bias, *deps)


def starts_of(toks):
    return [min(max(t * TILE - (SPAN - TILE) // 2, 0), toks - SPAN) for t in range(toks // TILE)]


def both_heads(val):
    lane = lax.broadcasted_iota(jnp.int32, val.shape, 1)
    return jnp.concatenate([jnp.where(lane < HEAD_DIM, val, 0.0), jnp.where(lane >= HEAD_DIM, val, 0.0)])


def one_head_each(val):
    rows = val.shape[0] // 2
    lane = lax.broadcasted_iota(jnp.int32, (rows, LANES), 1)
    return jnp.where(lane < HEAD_DIM, val[:rows], val[rows:])


def mul_deep(left, right):
    (lh, ll), (rh, rl) = left, right
    return mul(jnp.concatenate([lh, ll], 1), jnp.concatenate([rh, rh], 1), NT) + mul(lh, rl, NT)


def mul_wide(left, right, dims):
    (lh, ll), (rh, rl) = left, right
    cols = rh.shape[1]
    both = mul(lh, jnp.concatenate([rh, rl], 1), dims)
    return both[:, :cols] + (both[:, cols:] + mul(ll, rh, dims))


def probs_of(scores, same, axis):
    scores = jnp.where(same, scores, -1e30)
    exponent = jnp.exp(scores - jnp.max(scores, axis=axis, keepdims=True))
    return exponent * (1.0 / jnp.sum(exponent, axis=axis, keepdims=True))


def attend_kernel(q_ref, k_ref, v_ref, col_ref, win_ref, out_ref):
    toks = q_ref.shape[0]
    scale = 1.0 / math.sqrt(HEAD_DIM)
    for t, start in enumerate(starts_of(toks)):
        rows, keys = pl.ds(t * TILE, TILE), pl.ds(start, SPAN)
        same = col_ref[rows, :] == win_ref[t]
        scores = mul_deep(split(both_heads(q_ref[rows, :] * scale)), split(k_ref[keys, :]))
        probs = probs_of(scores, jnp.concatenate([same, same]), 1)
        out_ref[rows, :] = one_head_each(mul_wide(split(probs), split(v_ref[keys, :]), NN))


def pair_specs(toks, pairs, parts):
    return [
        pl.BlockSpec((toks, LANES), functools.partial(lambda part, i: (0, part * pairs + i), part))
        for part in range(parts)
    ]


def attend(qkv, segs, deps=()):
    toks, width = qkv.shape[0], qkv.shape[1] // 3
    pairs = width // LANES
    seg_col, seg_win, _ = segs
    return pl.pallas_call(
        leaving_out(attend_kernel, 5, deps),
        out_shape=shape(toks, width),
        grid=(pairs,),
        in_specs=pair_specs(toks, pairs, 3) + [whole(*seg_col.shape), whole(*seg_win.shape)] + untouched(deps),
        out_specs=pl.BlockSpec((toks, LANES), lambda i: (0, i)),
        compiler_params=params(),
        cost_estimate=cost(24 * toks * SPAN * width, 16 * toks * width, toks * SPAN * width // 64),
        name="attend",
    )(qkv, qkv, qkv, seg_col, seg_win, *deps)


def attend_back_kernel(q_ref, k_ref, v_ref, do_ref, col_ref, row_ref, out_ref):
    toks = q_ref.shape[0]
    scale = 1.0 / math.sqrt(HEAD_DIM)
    out_ref[1:] = jnp.zeros_like(out_ref[1:])
    for t, start in enumerate(starts_of(toks)):
        rows, keys = pl.ds(t * TILE, TILE), pl.ds(start, SPAN)
        same = col_ref[keys, :] == row_ref[t]
        q_pair, g_pair = split(both_heads(q_ref[rows, :] * scale)), split(both_heads(do_ref[rows, :]))
        k_pair, v_pair = split(k_ref[keys, :]), split(v_ref[keys, :])
        probs = probs_of(mul_deep(k_pair, q_pair), same, 0)
        dprobs = mul_deep(v_pair, g_pair)
        dscores = split(probs * (dprobs - jnp.sum(probs * dprobs, axis=0, keepdims=True)))
        out_ref[0, rows, :] = one_head_each(mul_wide(dscores, k_pair, TN)) * scale
        out_ref[1, keys, :] += mul_wide(dscores, q_pair, NN)
        out_ref[2, keys, :] += mul_wide(split(probs), g_pair, NN)


def attend_back(qkv, grad, half, segs, deps=()):
    toks, width = qkv.shape[0], qkv.shape[1] // 3
    pairs = width // LANES
    seg_col, _, seg_row = segs
    return pl.pallas_call(
        leaving_out(attend_back_kernel, 6, deps),
        out_shape=shape(3, toks, width),
        grid=(pairs,),
        in_specs=pair_specs(toks, pairs, 3)
        + [
            pl.BlockSpec((toks, LANES), lambda i: (0, half * pairs + i)),
            whole(*seg_col.shape),
            whole(*seg_row.shape),
        ]
        + untouched(deps),
        out_specs=pl.BlockSpec((3, toks, LANES), lambda i: (0, 0, i)),
        compiler_params=params(),
        cost_estimate=cost(60 * toks * SPAN * width, 28 * toks * width, toks * SPAN * width // 64),
        name="attend_back",
    )(qkv, qkv, qkv, grad, seg_col, seg_row, *deps)


def cdf_of(pre):
    return 0.5 * (1.0 + lax.erf(pre * (1.0 / math.sqrt(2.0))))


def mlp_kernel(x_ref, b_ref, w1_ref, w2_ref, acc_ref, pre_ref, y_ref, xh_ref, xl_ref):
    @pl.when(pl.program_id(0) == 0)
    def _():
        xh_ref[...], xl_ref[...] = split(x_ref[...])
        y_ref[...] = acc_ref[...]

    pre = mul3((xh_ref[...], xl_ref[...]), split(w1_ref[...]), NN) + b_ref[...]
    pre_ref[...] = pre
    y_ref[...] += mul3(split(pre * cdf_of(pre)), split(w2_ref[...]), NN)


def mlp_forward(normed, bias, w1, w2, acc, deps=(), block=512):
    toks, dim = normed.shape
    hidden = w1.shape[1]
    return pl.pallas_call(
        leaving_out(mlp_kernel, 5, deps),
        out_shape=(shape(toks, hidden), shape(toks, dim)),
        grid=(hidden // block,),
        in_specs=[
            whole(toks, dim),
            pl.BlockSpec((1, block), lambda j: (0, j)),
            pl.BlockSpec((dim, block), lambda j: (0, j)),
            pl.BlockSpec((block, dim), lambda j: (j, 0)),
            whole(toks, dim),
        ]
        + untouched(deps),
        out_specs=(pl.BlockSpec((toks, block), lambda j: (0, j)), whole(toks, dim)),
        scratch_shapes=[pltpu.VMEM((toks, dim), bf16)] * 2,
        compiler_params=params(),
        cost_estimate=cost(12 * toks * dim * hidden, 8 * dim * hidden + 4 * toks * (hidden + 2 * dim), toks * hidden),
        name="mlp_forward",
    )(normed, bias, w1, w2, acc, *deps)


def own_then_other(half):
    return (lambda j: jnp.minimum(j, half - 1)), (lambda j: jnp.maximum(j - half, 0))


def fill_transposed(src_ref, high_ref, low_ref):
    high_ref[...], low_ref[...] = split(jnp.transpose(src_ref[...]))


def mlp_back_a_kernel(half, block, split_out, core_ref, eg_ref, prea_ref, preb_ref, w2a_ref, w2b_ref, *refs):
    j = pl.program_id(0)
    pg_ref, b1_ref, keep_ref = refs[:3]
    send_ref = refs[3] if split_out else None
    eh_ref, el_ref, th_ref, tl_ref = refs[-4:]

    @pl.when(j == 0)
    def _():
        eh_ref[...], el_ref[...] = split(eg_ref[...])
        fill_transposed(eg_ref, th_ref, tl_ref)

    def step(pre_ref, w2_ref):
        pre = pre_ref[...]
        cdf = cdf_of(pre)
        pdf = jnp.exp(-0.5 * pre * pre) * (1.0 / math.sqrt(2.0 * math.pi))
        pg = mul3((eh_ref[...], el_ref[...]), split(w2_ref[...]), NT) * (cdf + pre * pdf)
        pg_ref[...] = pg
        b1_ref[...] = jnp.sum(pg, axis=0, keepdims=True)
        tile = mul3((th_ref[...], tl_ref[...]), split(pre * cdf), NN)
        store_rows(core_ref, tile, keep_ref, send_ref, slice(None), block)

    @pl.when(j < half)
    def _():
        step(prea_ref, w2a_ref)

    @pl.when(j >= half)
    def _():
        step(preb_ref, w2b_ref)


def grad_shapes(dim, cols, block, split_out):
    if split_out:
        return [shape(dim // (2 * block), block, cols)] * 2
    return [shape(dim, cols)]


def grad_specs(dim, cols, block, split_out):
    if split_out:
        return [pl.BlockSpec((dim // (2 * block), block, cols), lambda j, *_: (0, 0, j))] * 2
    return [pl.BlockSpec((dim, cols), lambda j, *_: (0, j))]


def mlp_back_a(core, enc_grad, pre, w2, rows, split_out, deps=(), block=512):
    toks, dim = enc_grad.shape
    hidden = 2 * pre[0].shape[1]
    half = hidden // 2 // block
    low, high = own_then_other(half)
    out = pl.pallas_call(
        leaving_out(functools.partial(mlp_back_a_kernel, half, rows, split_out), 6, deps),
        out_shape=[shape(toks, hidden), shape(1, hidden)] + grad_shapes(dim, hidden, rows, split_out),
        grid_spec=pltpu.PrefetchScalarGridSpec(
            num_scalar_prefetch=1,
            grid=(2 * half,),
            in_specs=[
                whole(toks, dim),
                pl.BlockSpec((toks, block), lambda j, _: (0, low(j))),
                pl.BlockSpec((toks, block), lambda j, _: (0, high(j))),
                pl.BlockSpec((block, dim), lambda j, _: (low(j), 0)),
                pl.BlockSpec((block, dim), lambda j, _: (high(j), 0)),
            ]
            + untouched(deps),
            out_specs=[
                pl.BlockSpec((toks, block), lambda j, _: (0, j)),
                pl.BlockSpec((1, block), lambda j, _: (0, j)),
            ]
            + grad_specs(dim, block, rows, split_out),
            scratch_shapes=[pltpu.VMEM((toks, dim), bf16)] * 2 + [pltpu.VMEM((dim, toks), bf16)] * 2,
        ),
        compiler_params=params(),
        cost_estimate=cost(12 * toks * dim * hidden, 8 * dim * hidden + 8 * toks * hidden, 2 * toks * hidden),
        name="mlp_back_a",
    )(core, enc_grad, *pre, *w2, *deps)
    return out[0], out[1], out[2:]


def mlp_input_kernel(half, pg_ref, wa_ref, wb_ref, dx_ref):
    j = pl.program_id(0)

    @pl.when(j == 0)
    def _():
        dx_ref[...] = jnp.zeros_like(dx_ref)

    @pl.when(j < half)
    def _():
        dx_ref[...] += mul3(split(pg_ref[...]), split(wa_ref[...]), NT)

    @pl.when(j >= half)
    def _():
        dx_ref[...] += mul3(split(pg_ref[...]), split(wb_ref[...]), NT)


def mlp_input_grad(pre_grad, w1, deps=(), block=768):
    toks, hidden = pre_grad.shape
    dim = w1[0].shape[0]
    half = hidden // 2 // block
    low, high = own_then_other(half)
    return pl.pallas_call(
        leaving_out(functools.partial(mlp_input_kernel, half), 3, deps),
        out_shape=shape(toks, dim),
        grid=(2 * half,),
        in_specs=[
            pl.BlockSpec((toks, block), lambda j: (0, j)),
            pl.BlockSpec((dim, block), lambda j: (0, low(j))),
            pl.BlockSpec((dim, block), lambda j: (0, high(j))),
        ]
        + untouched(deps),
        out_specs=whole(toks, dim),
        compiler_params=params(),
        cost_estimate=cost(6 * toks * dim * hidden, 4 * dim * hidden + 4 * toks * hidden, scale=COVER),
        name="mlp_input_grad",
    )(pre_grad, *w1, *deps)


def weight_grad_kernel(rows, split_out, core_ref, x_ref, g_ref, *refs):
    th_ref, tl_ref = refs[-2:]
    outs = refs[-4:-2] if split_out else (refs[-3], None)

    @pl.when(pl.program_id(0) == 0)
    def _():
        fill_transposed(x_ref, th_ref, tl_ref)

    grad = g_ref[0] if len(g_ref.shape) == 3 else g_ref[...]
    tile = mul3((th_ref[...], tl_ref[...]), split(grad), NN)
    store_rows(core_ref, tile, *outs, slice(None), rows)


def weight_grad(core, inputs, grad, rows, split_out, block, into=(), first=0, cols=None, deps=(), scale=SCALE):
    toks, dim = inputs.shape
    planes = grad.ndim == 3
    steps = grad.shape[0] if planes else grad.shape[1] // block
    width = steps * block
    cols = cols or width
    g_spec = (
        pl.BlockSpec((1, toks, block), lambda j, _: (j, 0, 0)) if planes else pl.BlockSpec((toks, block), lambda j, _: (0, j))
    )
    shapes = grad_shapes(dim, cols, rows, split_out)
    if split_out:
        out_spec = pl.BlockSpec((dim // (2 * rows), rows, block), lambda j, _: (0, 0, j + first))
    else:
        out_spec = pl.BlockSpec((dim, block), lambda j, _: (0, j + first))
    return pl.pallas_call(
        functools.partial(weight_grad_kernel, rows, split_out),
        out_shape=shapes,
        grid_spec=pltpu.PrefetchScalarGridSpec(
            num_scalar_prefetch=1,
            grid=(steps,),
            in_specs=[whole(toks, dim), g_spec] + untouched(into) + untouched(deps),
            out_specs=[out_spec] * len(shapes),
            scratch_shapes=[pltpu.VMEM((dim, toks), bf16)] * 2,
        ),
        input_output_aliases={3 + i: i for i in range(len(into))},
        compiler_params=params(),
        cost_estimate=cost(6 * toks * dim * width, 4 * (toks * dim + dim * width + toks * width), scale=scale),
        name="weight_grad",
    )(core, inputs, grad, *into, *deps)


def out_back_kernel(rows, split_out, core_ref, g_ref, wa_ref, wb_ref, ca_ref, cb_ref, *refs):
    j = pl.program_id(0)
    dc_ref, keep_ref = refs[:2]
    send_ref = refs[2] if split_out else None
    gh_ref, gl_ref, th_ref, tl_ref = refs[-4:]

    @pl.when(j == 0)
    def _():
        gh_ref[...], gl_ref[...] = split(g_ref[...])
        fill_transposed(g_ref, th_ref, tl_ref)

    def step(w_ref, c_ref):
        dc_ref[...] = mul3((gh_ref[...], gl_ref[...]), split(w_ref[...]), NT)
        tile = mul3((th_ref[...], tl_ref[...]), split(c_ref[...]), NN)
        store_rows(core_ref, tile, keep_ref, send_ref, slice(None), rows)

    @pl.when(j == 0)
    def _():
        step(wa_ref, ca_ref)

    @pl.when(j == 1)
    def _():
        step(wb_ref, cb_ref)


def out_back(core, mid_grad, weights, ctx, rows, split_out, deps=()):
    toks, dim = mid_grad.shape
    width = ctx[0].shape[1]
    cols = 8 * width
    shapes = grad_shapes(dim, cols, rows, split_out)
    if split_out:
        spec = pl.BlockSpec((dim // (2 * rows), rows, width), lambda j, _: (0, 0, 4 * j))
    else:
        spec = pl.BlockSpec((dim, width), lambda j, _: (0, 4 * j))
    out = pl.pallas_call(
        leaving_out(functools.partial(out_back_kernel, rows, split_out), 6, deps),
        out_shape=[shape(toks, 2 * width)] + shapes,
        grid_spec=pltpu.PrefetchScalarGridSpec(
            num_scalar_prefetch=1,
            grid=(2,),
            in_specs=[whole(toks, dim)] + [whole(width, dim)] * 2 + [whole(toks, width)] * 2 + untouched(deps),
            out_specs=[pl.BlockSpec((toks, width), lambda j, _: (0, j))] + [spec] * len(shapes),
            scratch_shapes=[pltpu.VMEM((toks, dim), bf16)] * 2 + [pltpu.VMEM((dim, toks), bf16)] * 2,
        ),
        compiler_params=params(),
        cost_estimate=cost(24 * toks * dim * width, 4 * (toks * dim + 4 * dim * width + 4 * toks * width)),
        name="out_back",
    )(core, mid_grad, *weights, *ctx, *deps)
    return out[0], out[1:]


def qkv_input_kernel(ga_ref, gb_ref, wa_ref, wb_ref, dx_ref):
    @pl.when(pl.program_id(0) == 0)
    def _():
        dx_ref[...] = jnp.zeros_like(dx_ref)

    for g_ref, w_ref in ((ga_ref, wa_ref), (gb_ref, wb_ref)):
        dx_ref[...] += mul3(split(g_ref[0]), split(w_ref[0]), NT)


def qkv_input_grad(grads, weights, deps=()):
    toks = grads[0].shape[1]
    _, dim, width = weights[0].shape
    grad_spec = pl.BlockSpec((1, toks, width), lambda c: (c, 0, 0))
    w_spec = pl.BlockSpec((1, dim, width), lambda c: (c, 0, 0))
    return pl.pallas_call(
        leaving_out(qkv_input_kernel, 4, deps),
        out_shape=shape(toks, dim),
        grid=(3,),
        in_specs=[grad_spec, grad_spec, w_spec, w_spec] + untouched(deps),
        out_specs=whole(toks, dim),
        compiler_params=params(),
        cost_estimate=cost(36 * toks * dim * width, 4 * (toks * dim + 6 * dim * width + 6 * toks * width), scale=COVER),
        name="qkv_input_grad",
    )(*grads, *weights, *deps)


def norm_back_kernel(up_ref, unit_ref, inverse_ref, gain_ref, base_ref, out_ref, sums_ref):
    @pl.when(pl.program_id(0) == 0)
    def _():
        sums_ref[...] = jnp.zeros_like(sums_ref)

    upstream, unit_val, base = up_ref[...], unit_ref[...], base_ref[...]
    out_ref[...] = base + norm_back(upstream, unit_val, inverse_ref[...], gain_ref[...])
    for i, val in enumerate((upstream * unit_val, upstream, base)):
        sums_ref[i : i + 1, :] += jnp.sum(val, axis=0, keepdims=True)


def norm_back_sums(upstream, unit_val, inverse, gain, base, steps=4):
    toks, dim = upstream.shape
    block = pl.BlockSpec((toks // steps, dim), lambda i: (i, 0))
    out, sums = pl.pallas_call(
        norm_back_kernel,
        out_shape=(shape(toks, dim), shape(8, dim)),
        grid=(steps,),
        in_specs=[block, block, pl.BlockSpec((toks // steps, 1), lambda i: (i, 0)), whole(1, dim), block],
        out_specs=(block, whole(8, dim)),
        compiler_params=params(),
        cost_estimate=cost(20 * toks * dim, 16 * toks * dim),
        name="norm_back",
    )(upstream, unit_val, inverse, gain[None], base)
    return out, sums[:3].reshape(-1)


def per_device(
    n_dp,
    patches,
    segment_ids,
    proprio,
    ln1_gain,
    ln1_bias,
    qkv_weight,
    qv_bias,
    out_weight,
    out_bias,
    ln2_gain,
    ln2_bias,
    fc1_weight,
    fc1_bias,
    fc2_weight,
    fc2_bias,
    pol_image,
    pol_proprio,
    pol_hidden,
    pol_third,
    pol_action,
    out_cotangent,
    action_cotangent,
):
    row_len, dim = patches.shape
    images = proprio.shape[0]
    local_dim = qkv_weight.shape[2]
    local_ff = fc1_weight.shape[1]
    toks = -(-(row_len // 2 + MOST // 2) // TILE) * TILE
    low = row_len - toks
    rows = dim // n_dp
    split_out = rows % 8 == 0

    mine = lax.axis_index("dp")
    side = lax.axis_index("tensor")
    bit_c, bit_y, bit_z, bits_h = mine & 1, (mine >> 1) & 1, (mine >> 2) & 1, mine >> 3
    core = jnp.reshape(bit_c, (1,)).astype(jnp.int32)

    def across(val):
        return lax.ppermute(val, "tensor", [(0, 1), (1, 0)])

    def swap(val, bit):
        return lax.ppermute(val, "dp", [(i, i ^ (1 << bit)) for i in range(n_dp)])

    def pick(val, index, axis):
        return lax.dynamic_index_in_dim(val, index, axis, keepdims=False)

    def gate(*vals):
        return lax.optimization_barrier(vals)

    def slices(weight):
        piece = weight.shape[0] // 8
        return [
            lax.dynamic_slice_in_dim(weight, index * piece, piece, 0)
            for index in (2 * bit_y + bit_c, 4 + 2 * bit_z + bit_c)
        ]

    def joined(pieces, others):
        place = []
        for c in (bit_c, 1 - bit_c):
            place += [2 * bit_y + c, 4 + 2 * bit_z + c, 2 * (1 - bit_y) + c, 4 + 2 * (1 - bit_z) + c]
        return join_pieces(jnp.stack(place).astype(jnp.int32), pieces + others)

    bias_pack = jnp.concatenate([qv_bias.reshape(-1), fc1_bias])
    wq_own = jnp.transpose(qkv_weight, (1, 0, 2))

    seg = segment_ids[0]
    pos = jnp.arange(row_len, dtype=jnp.int32)
    first_tok = jnp.concatenate([jnp.ones((1,), bool), seg[1:] != seg[:-1]])
    cut = jnp.min(jnp.where(first_tok & (pos >= low), pos, row_len))
    start = side * low

    def window(val):
        return lax.dynamic_slice_in_dim(val, start, toks, 0)

    here = start + jnp.arange(toks, dtype=jnp.int32)
    owned = jnp.where(side == 0, here < cut, here >= cut)
    seg_here, first_here = window(seg), window(first_tok)
    seg_col = seg_here[:, None]
    seg_win = jnp.stack([seg_here[s : s + SPAN] for s in starts_of(toks)])[:, None, :]
    seg_tile = seg_here.reshape(-1, 1, TILE)
    segs = (seg_col, seg_win, jnp.concatenate([seg_tile, seg_tile], axis=2))
    cls_pick = (
        (seg_here[None, :] == jnp.arange(images, dtype=jnp.int32)[:, None]) & (first_here & owned)[None, :]
    ).astype(f32)
    mine_image = jnp.sum(cls_pick, axis=1, keepdims=True)

    bias_oth = across(bias_pack)
    sent_q = slices(wq_own.reshape(3 * dim, local_dim))
    got_q = [across(val) for val in sent_q]
    x_in = window(patches)
    unit_in, inverse_in = norm_stats(x_in)
    normed_in = unit_in * ln1_gain + ln1_bias

    def qkv_bias_of(flat):
        return jnp.concatenate([flat[:local_dim], jnp.zeros((local_dim,), f32), flat[local_dim : 2 * local_dim]])[None]

    qkv_own = qkv_forward(normed_in, wq_own, qkv_bias_of(bias_pack))
    qkv_own, bias_oth, *got_q = gate(qkv_own, bias_oth, *got_q)
    near_q = [swap(got_q[0], 1), swap(got_q[1], 2)]
    core_q = [swap(val, 0) for val in got_q]
    half = out_weight.shape[0] // 2
    wo_part = lax.dynamic_slice_in_dim(out_weight, bit_c * half, half, 0)
    wo_part, *sent_1 = gate(wo_part, *slices(fc1_weight), *got_q)[:3]
    got_o = across(wo_part)
    got_1 = [across(val) for val in sent_1]
    ctx_own = attend(qkv_own, segs, deps=[wo_part, *sent_1])
    ctx_own, *near_q = gate(ctx_own, *near_q)
    core_q += [swap(val, 0) for val in near_q]
    wq_oth = joined(list(got_q) + list(near_q), core_q).reshape(3, dim, local_dim)
    sent_2 = slices(fc2_weight)
    qkv_oth = qkv_forward(normed_in, wq_oth, qkv_bias_of(bias_oth), deps=[ctx_own, *sent_2])
    qkv_oth, got_o = gate(qkv_oth, got_o)
    core_o = swap(got_o, 0)
    ctx_oth = attend(qkv_oth, segs, deps=[got_o])
    ctx_oth, core_o, *got_1 = gate(ctx_oth, core_o, *got_1)
    wo_oth = join_pieces(jnp.stack([bit_c, 1 - bit_c]).astype(jnp.int32), [got_o, core_o])
    near_1 = [swap(got_1[0], 1), swap(got_1[1], 2)]
    core_1 = [swap(val, 0) for val in got_1]
    sent_2 = gate(*sent_2, *got_1)[:2]
    got_2 = [across(val) for val in sent_2]
    qkv, ctx, wo, wq = [qkv_own, qkv_oth], [ctx_own, ctx_oth], [out_weight, wo_oth], [wq_own, wq_oth]
    high = lax.Precision.HIGH
    attn = jnp.dot(ctx[0], wo[0], precision=high) + jnp.dot(ctx[1], wo[1], precision=high)
    mid = x_in + attn + out_bias
    unit_mid, inverse_mid = norm_stats(mid)
    normed_mid = unit_mid * ln2_gain + ln2_bias
    pre_own, mlp_out = mlp_forward(normed_mid, fc1_bias[None], fc1_weight, fc2_weight, mid + fc2_bias, deps=got_1)
    mlp_out, *moved = gate(mlp_out, *near_1, *core_1, *got_2)
    near_1, core_1, got_2 = moved[:2], moved[2:4], moved[4:]
    near_2 = [swap(got_2[0], 1), swap(got_2[1], 2)]
    core_1 += [swap(val, 0) for val in near_1]
    core_2 = [swap(val, 0) for val in got_2]
    w1_oth = joined(list(got_1) + list(near_1), core_1)
    w1_oth, *near_2 = gate(w1_oth, *near_2)
    core_2 += [swap(val, 0) for val in near_2]
    w2_oth = joined(list(got_2) + list(near_2), core_2)
    pre_oth, enc = mlp_forward(normed_mid, bias_oth[None, 2 * local_dim :], w1_oth, w2_oth, mlp_out)
    w1, w2, pre_act = (fc1_weight, w1_oth), (fc2_weight, w2_oth), (pre_own, pre_oth)
    enc_got = across(enc)

    cls_features = dense(cls_pick, enc)
    act_cot = action_cotangent * mine_image
    pre_one = dense(cls_features, pol_image) + dense(proprio, pol_proprio)
    hidden_one = jax.nn.elu(pre_one)
    pre_two = dense(hidden_one, pol_hidden)
    hidden_two = jax.nn.elu(pre_two)
    pre_three = dense(hidden_two, pol_third)
    hidden_three = jax.nn.elu(pre_three)
    actions_part = dense(hidden_three, pol_action) * mine_image
    grad_p4 = dense(hidden_three.T, act_cot)
    grad_three = elu_back(dense(act_cot, pol_action.T), pre_three)
    grad_p3 = dense(hidden_two.T, grad_three)
    grad_two = elu_back(dense(grad_three, pol_third.T), pre_two)
    grad_p2 = dense(hidden_one.T, grad_two)
    grad_one = elu_back(dense(grad_two, pol_hidden.T), pre_one)
    grad_pimage = dense(cls_features.T, grad_one)
    grad_pprop = dense(proprio.T, grad_one)
    cls_grad = dense(grad_one, pol_image.T)

    def share(val):
        return val[..., : val.shape[-1] // 2], val[..., val.shape[-1] // 2 :]

    class Chain:
        def __init__(self, terms, order, first, size):
            self.terms, self.moving, self.first, self.size = terms, None, first, size
            levels = 0
            while 8 << levels < n_dp:
                levels += 1
            self.plan = list(order) + ["x"] + list(range(3, 3 + levels))
            self.axis = {1: 2, 2: 1} if order[0] == 1 else {2: 1, 1: 1}

        def part(self, val, index, axis):
            at, sizes = [0] * val.ndim, list(val.shape)
            at[axis], sizes[axis] = index, 1
            at[-2], sizes[-2] = self.first, self.size
            return jnp.squeeze(lax.dynamic_slice(val, at, sizes), axis)

        def step(self, tied):
            if self.moving is not None:
                tied, got = gate(tied, self.moving)
                self.terms.append(got)
            what = self.plan.pop(0)
            if what == "x":
                out, kept = (sum(share(val)[i] for val in self.terms) for i in (1, 0))
                tied, out = gate(tied, out)
                self.terms, self.moving = [kept], across(out)
                return tied
            bit = (mine >> what) & 1
            axis = self.axis.get(what, 1)
            if what >= 3:
                self.terms = [val.reshape((val.shape[0] // 2, 2) + val.shape[1:]) for val in self.terms]
            out, kept = (sum(self.part(val, index, axis) for val in self.terms) for index in (1 - bit, bit))
            self.first = 0
            tied, out = gate(tied, out)
            self.terms, self.moving = [kept], swap(out, what)
            return tied

    class Scatter:
        def __init__(self, parts, orders):
            self.parts, self.orders, self.chains = parts, orders, []
            if split_out:
                self.got = swap(parts[1], 0)

        def step(self, tied):
            if not split_out:
                return tied
            if not self.chains:
                tied, self.got = gate(tied, self.got)
                piece = rows // len(self.orders)
                terms = [val.reshape((n_dp // 8, 2, 2) + val.shape[1:]) for val in (self.parts[0], self.got)]
                self.chains = [Chain(list(terms), order, i * piece, piece) for i, order in enumerate(self.orders)]
            for chain in self.chains:
                if chain.plan:
                    tied = chain.step(tied)
            return tied

        def hold(self, tied):
            for chain in self.chains:
                tied, chain.moving = gate(tied, chain.moving)
            return tied

        def result(self):
            if not split_out:
                own, oth = share(self.parts[0])
                return lax.psum_scatter(own + across(oth), "dp", scatter_dimension=0, tiled=True)
            while not self.chains or any(chain.plan for chain in self.chains):
                self.step(core)
            return jnp.concatenate([sum(val[0] for val in chain.terms + [chain.moving]) for chain in self.chains])

    class Total:
        def __init__(self, val, halvings):
            self.halvings = halvings
            levels = 1
            while 2 << levels <= n_dp:
                levels += 1
            self.plan = list(range(levels)) + ["x"]
            self.val = val
            self.send()

        def send(self):
            what = self.plan.pop(0) if self.plan else None
            if what is None:
                self.moving = None
            elif what == "x":
                self.moving = across(self.val)
            elif what < self.halvings:
                bit = (mine >> what) & 1
                pair = self.val.reshape((2, self.val.shape[0] // 2) + self.val.shape[1:])
                self.sent = pick(pair, 1 - bit, 0)
                self.val, self.moving = pick(pair, bit, 0), swap(self.sent, what)
            else:
                self.moving = swap(self.val, what)

        def step(self, tied):
            tied, got = gate(tied, self.moving)
            self.val = self.val + got
            self.send()
            return gate(tied, self.val)[0]

        def result(self):
            while self.moving is not None:
                self.step(core)
            for what in reversed(range(self.halvings)):
                bit = (mine >> what) & 1
                got = swap(self.val, what)
                first = jnp.where(bit == 0, self.val, got)
                self.val = jnp.concatenate([first, jnp.where(bit == 0, got, self.val)])
            return self.val

    both_orders = [(1, 2), (2, 1)] if rows % 16 == 0 else [(1, 2)]
    pad = lambda val, h, w: jnp.pad(val, ((0, h - val.shape[0]), (0, w - val.shape[1])))
    hid = pol_hidden.shape[1]
    rest = jnp.concatenate([pad(grad_p3, hid, hid), pad(grad_p4, pol_hidden.shape[0] - hid, hid)], axis=0)
    pol_pack = jnp.concatenate([grad_pimage, pad(grad_pprop, 32, pol_image.shape[1]), jnp.concatenate([grad_p2, rest], axis=1)])
    enc_grad = jnp.where(owned[:, None], window(out_cotangent), 0.0) + lax.dot_general(
        cls_pick, cls_grad, TN, precision=highest
    )
    pol = Total(pol_pack, 2)
    enc_grad = pol.step(enc_grad)
    pre_grad, grad_b1, parts_w2 = mlp_back_a(core, enc_grad, pre_act, w2, rows, split_out, deps=[pol.val])
    sum_2 = Scatter(parts_w2, both_orders)
    pre_grad, enc_got = gate(pre_grad, enc_got)
    pre_grad = pol.step(pre_grad)
    parts_w1 = weight_grad(core, normed_mid, pre_grad, rows, split_out, 512, deps=[pol.val], scale=COVER)
    sum_1 = Scatter(parts_w1, both_orders)
    pre_grad, kept = gate(pre_grad, parts_w1[0])
    pre_grad = sum_2.step(pre_grad)
    normed_mid_grad = mlp_input_grad(pre_grad, w1, deps=[kept])
    normed_mid_grad = sum_1.step(normed_mid_grad)
    mid_grad, sums_mid = norm_back_sums(normed_mid_grad, unit_mid, inverse_mid, ln2_gain, enc_grad)
    ctx_grad, parts_a = out_back(core, mid_grad, wo, ctx, rows, split_out)
    ctx_grad = sum_2.step(ctx_grad)
    dqkv_oth = attend_back(qkv[1], ctx_grad, 1, segs)
    dqkv_oth = sum_1.step(dqkv_oth)
    dqkv_own = attend_back(qkv[0], ctx_grad, 0, segs, deps=[dqkv_oth])
    dqkv_own = sum_2.step(dqkv_own)
    merge = functools.partial(weight_grad, core, normed_in, rows=rows, split_out=split_out, block=local_dim, cols=8 * local_dim)
    parts_a = merge(grad=dqkv_oth, into=parts_a, first=5, deps=[dqkv_own])
    dqkv_own, *parts_a = gate(dqkv_own, *parts_a)
    dqkv_own = pol.step(dqkv_own)
    parts_a = merge(grad=dqkv_own, into=parts_a, first=1)
    sum_a = Scatter(parts_a, both_orders)
    dqkv_own, kept = gate(dqkv_own, parts_a[0])
    dqkv_own = sum_2.step(dqkv_own)
    dqkv = [dqkv_own, dqkv_oth]
    normed_in_grad = qkv_input_grad(dqkv, wq, deps=[kept])
    normed_in_grad = sum_a.step(normed_in_grad)
    patches_grad, sums_in = norm_back_sums(normed_in_grad, unit_in, inverse_in, ln1_gain, mid_grad)

    def token_sum(val):
        return jnp.sum(val, axis=0)

    common = jnp.concatenate([sums_in, sums_mid])
    halves = [
        jnp.concatenate([token_sum(dqkv[i][0]), token_sum(dqkv[i][2]), grad_b1[0, i * local_ff : (i + 1) * local_ff]])
        for i in range(2)
    ]
    vec_got = across(jnp.concatenate([common, halves[1], actions_part.reshape(-1)]))
    patches_grad = sum_1.step(patches_grad)
    patches_grad = pol.step(patches_grad)
    pg_got = across(patches_grad)
    tied = sum_2.hold(patches_grad)
    tied = sum_a.step(tied)
    tied = sum_a.step(tied)
    tied = sum_1.step(tied)
    tied, pg_got, vec_got = gate(tied, pg_got, vec_got)
    vec = jnp.concatenate([common, halves[0]])
    small = Total(vec + vec_got[: vec.size], 0)
    actions = actions_part + vec_got[vec.size :].reshape(actions_part.shape)
    small.plan.remove("x")
    tied = small.step(tied)
    tied = pol.step(tied)
    tied = sum_1.hold(tied)
    tied = sum_a.step(tied)
    patches_grad = small.step(tied)
    vec = small.result()
    summed_w2, summed_w1, summed_attn, pol_sum = sum_2.result(), sum_1.result(), sum_a.result(), pol.result()
    common, halves = vec[: 6 * dim].reshape(6, dim), vec[6 * dim :]

    def assemble(own, got):
        left = jnp.where(side == 0, own, got)
        right = jnp.where(side == 0, got, own)
        overlap = toks - low
        inside = low + jnp.arange(overlap, dtype=jnp.int32)
        return jnp.concatenate(
            [left[:low], jnp.where((inside < cut)[:, None], left[low:], right[:overlap]), right[overlap:]]
        )

    width = pol_image.shape[0]
    tail = pol_sum[width + 32 :]
    return (
        assemble(enc, enc_got),
        actions,
        assemble(patches_grad, pg_got),
        common[0],
        common[1],
        summed_attn[:, local_dim:].reshape(rows, 3, local_dim),
        halves[: 2 * local_dim].reshape(2, local_dim),
        summed_attn[:, :local_dim].T,
        common[2],
        common[3],
        common[4],
        summed_w1,
        halves[2 * local_dim :],
        summed_w2.T,
        common[5],
        pol_sum[:width],
        pol_sum[width : width + proprio.shape[1]],
        tail[:, :hid],
        tail[:hid, hid : hid + pol_third.shape[1]],
        tail[hid : hid + pol_action.shape[0], hid : hid + pol_action.shape[1]],
    )


def solution(mesh):
    return jax.shard_map(
        functools.partial(per_device, mesh.shape["dp"]),
        mesh=mesh,
        in_specs=(
            P("dp", None),
            P("dp", None),
            P("dp", None),
            P(),
            P(),
            P(None, None, "tensor"),
            P(None, "tensor"),
            P("tensor", None),
            P(),
            P(),
            P(),
            P(None, "tensor"),
            P("tensor"),
            P("tensor", None),
            P(),
            P(),
            P(),
            P(),
            P(),
            P(),
            P("dp", None),
            P("dp", None),
        ),
        out_specs=(
            P("dp", None),
            P("dp", None),
            P("dp", None),
            P(),
            P(),
            P("dp", None, "tensor"),
            P(None, "tensor"),
            P("tensor", "dp"),
            P(),
            P(),
            P(),
            P("dp", "tensor"),
            P("tensor"),
            P("tensor", "dp"),
            P(),
            P(),
            P(),
            P(),
            P(),
            P(),
        ),
        check_vma=False,
    )
```
